32 devices in a mesh: parts: 2 (over y), seq: 8 (over z, x), dp: 2 (over core).
Axes of the slice: x: 2, y: 2, z: 4, core: 2. Of those that a mesh axis runs over, the one named last changes fastest.
Arguments:
- features: bfloat16 [4, 1024, 768], P(('parts', 'dp'), 'seq'), parts along dimension 0, may hold values from -6 to 6
- cotangent: bfloat16 [4, 1024, 768], P(('parts', 'dp'), 'seq'), parts along dimension 0, may hold values from -6 to 6
- counts: int32 [4, 1024], P(('parts', 'dp'), 'seq'), parts along dimension 0, may hold values from 0 to 255
- count_weight: float32 [768], replicated, may hold values from -3 to 3
- down_weight: bfloat16 [2, 768, 384], P(None, None, 'dp'), may hold values from -0.21875 to 0.21875
- tap_weight: bfloat16 [2, 3, 384, 384], P(None, None, None, 'dp'), may hold values from -0.1875 to 0.1875
- up_weight: bfloat16 [2, 384, 768], P(None, None, 'dp'), may hold values from -0.3125 to 0.3125
- decay_rate: float32 [4], replicated, may hold values from 7.8125e-05 to 0.0333333333
- keep_share: float32 [4, 1024], P(('parts', 'dp'), 'seq'), parts along dimension 0, may hold values from 0.3 to 1
- mode_weight: float32 [2, 4, 768], replicated, may hold values from -3 to 3
Outputs:
- feature_grad: bfloat16 [4, 1024, 768], P(('parts', 'dp'), 'seq'), parts along dimension 0
- tap_grad: float32 [4608, 384], P(('parts', 'seq', 'dp')), parts along dimension 0
- mode_grad: float32 [16, 768], P('parts', ('seq', 'dp')), parts along dimension 0
The draws below stay inside these ranges and needn't reach their ends.
There are 2 independent parts, one for each index of `parts`. The reference program is written for one: setup_inputs(seed, part) draws one part's arguments, and reference() takes and returns one part's arrays. A program takes and returns all parts, laid end to end along the dimension named above; an argument that names none is the same for every part. Nothing has to cross between parts.
All inputs are finite; a program needn't handle non-finite values.
Results may differ from the reference program's by a relative error of at most 0.011.
Values may be sent and summed in bfloat16 or wider, within the bound.
No kernel may reach another device: no remote copies, remote signals or barrier semaphores. Data moves between devices by JAX's collectives and lax.ppermute only.
A program may use at most 64 MiB of HBM per device.

```python
import math
import jax
import jax.numpy as jnp
from jax import lax

C = 768
B = 384
LB = 128
DILATION_FIRST1 = 2048
DILATION_SECOND2 = 4096
M = 4
LAYERS = 2
GENOMES = 2
BINS = 1024


def draw_decay_rate(key, part):
    rank_key, slow_key, fast_key, medium_key = jax.random.split(jax.random.fold_in(key, 11), 4)
    ranking = jax.random.permutation(rank_key, M)
    slow_mask = ranking < M // 2
    slow_rate = jnp.exp(jnp.log(0.08 / BINS) + jax.random.uniform(slow_key, (M,), jnp.float32) * jnp.log(5.0))
    fast_rate = jnp.exp(jnp.log(1.0 / 50.0) + jax.random.uniform(fast_key, (M,), jnp.float32) * jnp.log(50.0 / 30.0))
    lowest = min(0.25 / LB, 0.02)
    highest = min(1.0 / LB, 0.03)
    medium_rate = jnp.exp(jnp.log(lowest) + jax.random.uniform(medium_key, (M,), jnp.float32) * (jnp.log(highest) - jnp.log(lowest)))
    other_rate = jnp.where(ranking % 2 == 0, fast_rate, medium_rate)
    return jnp.where(slow_mask, slow_rate, other_rate).astype(jnp.float32)


def draw_keep_share(key, part):
    rough_key, place_key, depth_key = jax.random.split(jax.random.fold_in(key, 23), 3)
    jaggedness_grade = 1.0 - jax.random.uniform(rough_key, (GENOMES, BINS), jnp.float32) * (0.3 / BINS)
    locus_numbers = jax.random.randint(place_key, (GENOMES, 2), 0, BINS)
    stack_heights = jax.random.uniform(depth_key, (GENOMES, 2), jnp.float32, 0.55, 0.8)
    matrix_element = lax.broadcasted_iota(jnp.int32, (GENOMES, BINS, 2), 1)
    spike_amounts = jnp.prod(jnp.where(matrix_element == locus_numbers[:, None, :], stack_heights[:, None, :], 1.0), axis=-1)
    return (jaggedness_grade * spike_amounts).astype(jnp.float32)


def set_ends(entries, rng, low, top_value):
    index_at = [jax.random.randint(jax.random.fold_in(rng, axis), (), 0, length) for axis, length in enumerate(entries.shape)]
    main_axis = entries.shape.index(max(entries.shape))
    neighbour = index_at[:main_axis] + [(index_at[main_axis] + 1) % entries.shape[main_axis]] + index_at[main_axis + 1:]
    return entries.at[tuple(index_at)].set(low).at[tuple(neighbour)].set(top_value)


def strengthened(drawn, rng, source, target, blocks, factor):
    owner, partner = [(jnp.arange(drawn.shape[dim]) // (drawn.shape[dim] // blocks)).reshape([-1 if axis == dim else 1 for axis in range(drawn.ndim)]) for dim in (source, target)]
    chosen = jax.random.permutation(rng, blocks)[partner]
    strong = (owner == chosen) | (owner == (partner + blocks // 2) % blocks)
    return jnp.where(strong, factor * drawn, drawn)


def shard_levels(stream_key, dims, pieces, least, high):
    def one(dim, shards_of):
        heights = jax.random.uniform(jax.random.fold_in(jax.random.fold_in(stream_key, 6), dim), (shards_of,), jnp.float32, least / len(pieces), high / len(pieces))
        return jnp.repeat(jnp.exp(heights), dims[dim] // shards_of).reshape((-1,) + (1,) * (len(dims) - dim - 1))

    gain = one(*pieces[0])
    for cut in pieces[1:]:
        gain = gain * one(*cut)
    return gain


def scatter_about(rng, dims, scale, most, pieces=(), held_as=jnp.bfloat16):
    array = scale * jax.random.normal(rng, dims, jnp.float32)
    if pieces:
        array = array * shard_levels(rng, dims, pieces, -0.22, 0.18)
    return jnp.clip(array, -most, most).astype(held_as)


def heavy_noise(rng, extent, spread, limit, pieces, heavy, kind=jnp.bfloat16):
    result = spread * jax.random.normal(rng, extent, jnp.float32)
    if pieces:
        result = result * shard_levels(rng, extent, pieces, -0.22, 0.18)
    return jnp.clip(strengthened(result, jax.random.fold_in(rng, 3), *heavy), -limit, limit).astype(kind)


def setup_inputs(seed: int = 0, part: int = 0) -> dict:
    key_of = jax.random.split(jax.random.key(seed), 11)
    part_keys = jax.random.split(jax.random.fold_in(key_of[10], part), 11)
    features = scatter_about(part_keys[0], (GENOMES, BINS, C), 1.0, 6.0, ((0, 2), (1, 8)))
    cotangent = heavy_noise(part_keys[1], (GENOMES, BINS, C), 1.0, 6.0, ((0, 2), (1, 8)), (1, 2, 8, 2.0))
    counts = set_ends(jax.random.randint(part_keys[2], (GENOMES, BINS), 0, 256), jax.random.fold_in(part_keys[2], 1), 0, 255).astype(jnp.int32)
    count_weight = scatter_about(key_of[3], (C,), 0.4, 3.0, (), jnp.float32)
    down_weight = scatter_about(key_of[4], (LAYERS, C, B), C ** -0.5, 0.21875, ((2, 2),))
    tap_weight = scatter_about(key_of[5], (LAYERS, 3, B, B), (3 * B) ** -0.5, 0.1875, ((3, 2),))
    up_weight = scatter_about(key_of[6], (LAYERS, B, C), B ** -0.5, 0.3125, ((2, 2),))
    decay_rate = draw_decay_rate(jax.random.fold_in(key_of[10], 71), part)
    keep_share = draw_keep_share(jax.random.fold_in(jax.random.fold_in(key_of[10], part), 71), part)
    mode_weight = scatter_about(key_of[9], (2, M, C), 0.5, 3.0, (), jnp.float32)
    return dict(features=features, cotangent=cotangent, counts=counts, count_weight=count_weight, down_weight=down_weight, tap_weight=tap_weight, up_weight=up_weight, decay_rate=decay_rate, keep_share=keep_share, mode_weight=mode_weight)


EPSILON = 1e-06
HALF_ROOT = 1.0 / math.sqrt(2.0)
DENSITY = 1.0 / math.sqrt(2.0 * math.pi)

def gelu_exact(values):
    return 0.5 * values * (1.0 + lax.erf(values * HALF_ROOT))

def gelu_slope(values):
    cumulative = 0.5 * (1.0 + lax.erf(values * HALF_ROOT))
    return cumulative + values * jnp.exp(-0.5 * values * values) * DENSITY

def matmul(left_shifted, right_shifted):
    leading = left_shifted.shape[:-1]
    flat = left_shifted.reshape(-1, left_shifted.shape[-1])
    return jnp.dot(flat, right_shifted, preferred_element_type=jnp.float32).reshape(leading + (right_shifted.shape[-1],))

def contract(left_shifted, right_shifted):
    flat_left = left_shifted.reshape(-1, left_shifted.shape[-1])
    flat_right = right_shifted.reshape(-1, right_shifted.shape[-1])
    return jnp.dot(flat_left.T, flat_right, preferred_element_type=jnp.float32)

def inverse_rms(stream):
    return lax.rsqrt(lax.optimization_barrier(jnp.mean(stream * stream, axis=-1, keepdims=True)) + EPSILON)

def directional(factor, source, cotangent_rows, source_gain, cot_gain, backward):
    gains = jnp.exp(factor)
    feature_maps = source.shape[-1]
    genome_count = source.shape[1]
    mode_count = factor.shape[-1]

    def drive(source_row, cot_row):
        return jnp.concatenate([source_gain[None, :, None] * source_row[:, None, :], cot_gain[None, :, :] * cot_row[:, None, :]], axis=-1)

    def first_pass(state, inputs):
        gain_row, source_row, cot_row = inputs
        return (gain_row[..., None] * state + drive(source_row, cot_row), None)
    empty_state = jnp.zeros((genome_count, mode_count, 2 * feature_maps), jnp.float32)
    ending, unused = lax.scan(first_pass, empty_state, (gains, source, cotangent_rows), reverse=backward)
    beside_all = jnp.exp(lax.optimization_barrier(jnp.sum(factor, axis=0)))
    opening = ending / (1.0 - beside_all)[..., None]

    def second_pass(carry, inputs):
        state, totals = carry
        gain_row, source_row, cot_row = inputs
        state = gain_row[..., None] * state + drive(source_row, cot_row)
        totals = totals + lax.optimization_barrier(jnp.sum(state[:, :, :feature_maps] * cot_row[:, None, :], axis=0))
        return ((state, totals), lax.optimization_barrier(jnp.sum(state[:, :, feature_maps:], axis=1)))
    empty_totals = jnp.zeros((mode_count, feature_maps), jnp.float32)
    (unused_state, totals), outputs = lax.scan(second_pass, (opening, empty_totals), (gains, source, cotangent_rows), reverse=backward)
    return (totals, outputs)

def reference(features, cotangent, counts, count_weight, down_weight, tap_weight, up_weight, decay_rate, keep_share, mode_weight):
    genome_count = features.shape[0]
    bin_count = features.shape[1]
    stream = features.astype(jnp.float32) + jnp.log1p(counts.astype(jnp.float32))[..., None] * count_weight
    stored = []
    for layer_position in range(LAYERS):
        shift_offset = DILATION_FIRST1 if layer_position == 0 else DILATION_SECOND2
        inverse = inverse_rms(stream)
        normed = (stream * inverse).astype(jnp.bfloat16)
        reduced = matmul(normed, down_weight[layer_position]).astype(jnp.bfloat16)
        lagged = jnp.roll(reduced, shift_offset, axis=1)
        advanced = jnp.roll(reduced, -shift_offset, axis=1)
        mixture = matmul(lagged, tap_weight[layer_position, 0]) + matmul(reduced, tap_weight[layer_position, 1]) + matmul(advanced, tap_weight[layer_position, 2])
        active_modes = gelu_exact(mixture).astype(jnp.bfloat16)
        stored.append((stream, inverse, reduced, lagged, advanced, mixture))
        stream = stream + matmul(active_modes, up_weight[layer_position])
    cot_wide = cotangent.astype(jnp.float32)
    logs = jnp.log(keep_share)[:, :, None] - decay_rate[None, None, :]
    factor = jnp.swapaxes(logs, 0, 1)
    mode_scale = jnp.sqrt(-jnp.expm1(-2.0 * decay_rate))
    source = jnp.swapaxes(stream, 0, 1)
    cotangent_rows = jnp.swapaxes(cot_wide, 0, 1)
    fore_totals, fore_rows = directional(factor, source, cotangent_rows, mode_scale, mode_scale[:, None] * mode_weight[1], False)
    back_totals, back_rows = directional(jnp.roll(factor, -1, axis=0), source, cotangent_rows, mode_scale, mode_scale[:, None] * mode_weight[0], True)
    gradient = cot_wide + jnp.swapaxes(fore_rows + back_rows, 0, 1)
    report_scale = 1.0 / math.sqrt(genome_count * bin_count)
    mode_grad = (jnp.stack([fore_totals, back_totals]) * report_scale).reshape(2 * M, -1)
    tap_terms = []
    for layer_position in reversed(range(LAYERS)):
        shift_offset = DILATION_FIRST1 if layer_position == 0 else DILATION_SECOND2
        before, inverse, reduced, lagged, advanced, mixture = stored[layer_position]
        narrow_width = gradient.astype(jnp.bfloat16)
        mixed_grad = (matmul(narrow_width, up_weight[layer_position].T) * gelu_slope(mixture)).astype(jnp.bfloat16)
        tap_terms.insert(0, jnp.stack([contract(lagged, mixed_grad), contract(reduced, mixed_grad), contract(advanced, mixed_grad)]))
        reduced_grad = matmul(mixed_grad, tap_weight[layer_position, 1].T) + matmul(jnp.roll(mixed_grad, -shift_offset, axis=1), tap_weight[layer_position, 0].T) + matmul(jnp.roll(mixed_grad, shift_offset, axis=1), tap_weight[layer_position, 2].T)
        normed_grad = matmul(reduced_grad.astype(jnp.bfloat16), down_weight[layer_position].T)
        gradient = gradient + inverse * normed_grad - before * inverse * inverse * inverse * lax.optimization_barrier(jnp.mean(normed_grad * before, axis=-1, keepdims=True))
    tap_grad = (jnp.stack(tap_terms) * report_scale).reshape(LAYERS * 3 * B, B)
    return (gradient.astype(jnp.bfloat16), tap_grad, mode_grad)
```

```python
import functools
import math

import jax
import jax.numpy as jnp
from jax import lax
from jax.experimental import pallas as pl
from jax.experimental.pallas import tpu as pltpu
from jax.sharding import PartitionSpec as P

B = 384
DILATION_FIRST1 = 2048
DILATION_SECOND2 = 4096
M = 4
LAYERS = 2


EPSILON = 1e-06
HALF_ROOT = 1.0 / math.sqrt(2.0)
DENSITY = 1.0 / math.sqrt(2.0 * math.pi)
TOP_PRECISION = lax.Precision.HIGHEST


def shifted(value, axis, steps):
    count = lax.axis_size(axis)
    pairs = [(source, (source + steps) % count) for source in range(count)]
    return lax.ppermute(value, axis, pairs)


def entering_2(shard, axis, join, neutral, backward):
    count = lax.axis_size(axis)
    place = lax.axis_index(axis)
    ahead = count - 1 - place if backward else place
    gathered = jax.tree.map(
        lambda a, kind: lax.all_gather(a.astype(kind), axis),
        shard,
        jax.tree.map(lambda a: jnp.bfloat16 if a.dtype == jnp.float32 else a.dtype, shard),
    )
    state = jax.tree.map(lambda a, e: jnp.zeros_like(a) + jnp.asarray(e, a.dtype), shard, neutral)

    def one(turn, state):
        source = count - 1 - turn if backward else turn
        return join(
            state,
            jax.tree.map(
                lambda a, own: lax.dynamic_index_in_dim(a, source, 0, False).astype(own.dtype),
                gathered,
                shard,
            ),
        )

    return lax.fori_loop(0, ahead, one, state)


def gelu_exact(values):
    return 0.5 * values * (1.0 + lax.erf(values * HALF_ROOT))


def gelu_slope(values):
    cumulative = 0.5 * (1.0 + lax.erf(values * HALF_ROOT))
    return cumulative + values * jnp.exp(-0.5 * values * values) * DENSITY


def project(left_shifted, right_shifted):
    return jnp.einsum(
        "qra,au->qru", left_shifted, right_shifted, preferred_element_type=jnp.float32
    )


def project_back(left_shifted, right_shifted):
    return jnp.einsum(
        "kut,st->kus", left_shifted, right_shifted, preferred_element_type=jnp.float32
    )


def contract(left_shifted, right_shifted):
    return jnp.einsum(
        "glb,glk->bk", left_shifted, right_shifted, preferred_element_type=jnp.float32
    )


def moved(values, bin_distance):
    return shifted(values, "seq", bin_distance)


def block_product(kernel, pieces):
    return jnp.einsum(
        "gmbij,gbjc->gmbic",
        kernel,
        pieces,
        precision=TOP_PRECISION,
        preferred_element_type=jnp.float32,
    )


def modal_local(lg_in, lg_exit, stream_rows, cotangent_rows):
    genome_count, input_rows, mode_count = lg_in.shape
    feature_maps = stream_rows.shape[-1]
    block_size = min(128, input_rows)
    block_count = input_rows // block_size
    running = jnp.cumsum(lg_in, axis=1)
    running_blocks = running.reshape(genome_count, block_count, block_size, mode_count)
    block_ends = running_blocks[:, :, -1, :]
    block_starts = jnp.concatenate(
        [jnp.zeros((genome_count, 1, mode_count), jnp.float32), block_ends[:, :-1, :]], axis=1
    )
    within = running_blocks - block_starts[:, :, None, :]
    within_t = jnp.transpose(within, (0, 3, 1, 2))
    spread = within_t[..., :, None] - within_t[..., None, :]
    row_index = lax.broadcasted_iota(jnp.int32, (block_size, block_size), 0)
    column_index = lax.broadcasted_iota(jnp.int32, (block_size, block_size), 1)
    kernel = jnp.where(row_index >= column_index, jnp.exp(jnp.minimum(spread, 0.0)), 0.0)
    joined_source = jnp.concatenate([stream_rows, cotangent_rows.astype(jnp.float32)], axis=-1)
    joined_source = joined_source.reshape(genome_count, block_count, block_size, 2 * feature_maps)
    partial_value = block_product(kernel, joined_source)
    block_tails = partial_value[:, :, :, -1, :]
    ends_t = jnp.transpose(block_ends, (0, 2, 1))
    starts_t = jnp.transpose(block_starts, (0, 2, 1))
    spacing = starts_t[..., :, None] - ends_t[..., None, :]
    block_index = lax.broadcasted_iota(jnp.int32, (block_count, block_count), 0)
    source_index = lax.broadcasted_iota(jnp.int32, (block_count, block_count), 1)
    linkage = jnp.where(source_index < block_index, jnp.exp(jnp.minimum(spacing, 0.0)), 0.0)
    entering = jnp.einsum(
        "gmbk,gmkc->gmbc",
        linkage,
        block_tails,
        precision=TOP_PRECISION,
        preferred_element_type=jnp.float32,
    )
    states = partial_value + jnp.exp(within_t)[..., None] * entering[:, :, :, None, :]
    states = states.reshape(genome_count, mode_count, input_rows, 2 * feature_maps)
    decay_values = jnp.exp(jnp.transpose(running, (0, 2, 1)))
    exit_state = jnp.exp(lg_exit)[..., None] * states[:, :, -1, :]
    log_pass = running[:, -1, :] + lg_exit
    return (states, decay_values, exit_state, log_pass)


def modal_terms(states, decay_values, entering, cotangent_rows, source_gain, cot_gain):
    feature_maps = cotangent_rows.shape[-1]
    reach_sum = jnp.einsum(
        "qsz,qzj->qsj",
        decay_values,
        cotangent_rows,
        precision=TOP_PRECISION,
        preferred_element_type=jnp.float32,
    )
    totals = jnp.einsum(
        "veyi,vyi->ei",
        states[..., :feature_maps],
        cotangent_rows,
        precision=TOP_PRECISION,
        preferred_element_type=jnp.float32,
    )
    totals = totals + jnp.sum(entering[..., :feature_maps] * reach_sum, axis=0)
    rows_out = jnp.einsum(
        "jryf,rf->jyf",
        states[..., feature_maps:],
        cot_gain,
        precision=TOP_PRECISION,
        preferred_element_type=jnp.float32,
    )
    rows_out = rows_out + jnp.einsum(
        "ert,erx->etx",
        decay_values,
        entering[..., feature_maps:] * cot_gain[None],
        precision=TOP_PRECISION,
        preferred_element_type=jnp.float32,
    )
    return (source_gain[:, None] * totals, rows_out)


def apply_early_first(early_pass, early_state, late_pass, late_state):
    return (early_pass * late_pass, late_pass[..., None] * early_state + late_state)


def apply_late_first(early_pass, early_state, late_pass, late_state):
    return (early_pass * late_pass, early_pass[..., None] * late_state + early_state)


def join_lower(early, late):
    fore_pass, fore_state = apply_early_first(early[0], early[1], late[0], late[1])
    back_pass, back_state = apply_late_first(early[2], early[3], late[2], late[3])
    return (fore_pass, fore_state, back_pass, back_state)


def join_upper(early, late):
    fore_pass, fore_state = apply_late_first(early[0], early[1], late[0], late[1])
    back_pass, back_state = apply_early_first(early[2], early[3], late[2], late[3])
    return (fore_pass, fore_state, back_pass, back_state)


def closed(own_pass, own_state, pass_before, state_before, pass_after, state_after):
    beside_all = pass_before * pass_after
    numerator = (
        beside_all[..., None] * own_state + pass_before[..., None] * state_after + state_before
    )
    return numerator / (1.0 - beside_all * own_pass)[..., None]


def general_device(
    features,
    cotangent,
    counts,
    count_weight,
    down_weight,
    tap_weight,
    up_weight,
    decay_rate,
    keep_share,
    mode_weight,
):
    genome_count = features.shape[0]
    input_rows = features.shape[1]
    down_full, tap_full, full_up_weight = (
        lax.all_gather(down_weight, "dp", axis=2, tiled=True),
        lax.all_gather(tap_weight, "dp", axis=3, tiled=True),
        lax.all_gather(up_weight, "dp", axis=2, tiled=True),
    )
    stream = (
        features.astype(jnp.float32)
        + jnp.log1p(counts.astype(jnp.float32))[..., None] * count_weight
    )
    stored = []
    for layer_position in range(LAYERS):
        bin_distance = (DILATION_FIRST1 if layer_position == 0 else DILATION_SECOND2) // input_rows
        inverse = lax.rsqrt(jnp.mean(stream * stream, axis=-1, keepdims=True) + EPSILON)
        normed = (stream * inverse).astype(jnp.bfloat16)
        reduced = project(normed, down_full[layer_position]).astype(jnp.bfloat16)
        lagged = moved(reduced, bin_distance)
        advanced = moved(reduced, -bin_distance)
        mixture = (
            project(lagged, tap_full[layer_position, 0])
            + project(reduced, tap_full[layer_position, 1])
            + project(advanced, tap_full[layer_position, 2])
        )
        active_modes = gelu_exact(mixture).astype(jnp.bfloat16)
        stored.append((stream, inverse, reduced, lagged, advanced, mixture))
        stream = stream + jnp.einsum(
            "quy,yk->quk",
            active_modes,
            full_up_weight[layer_position],
            preferred_element_type=jnp.float32,
        )
    cot_wide = cotangent.astype(jnp.float32)
    logs = jnp.log(keep_share)[:, :, None] - decay_rate[None, None, :]
    mode_scale = jnp.sqrt(-jnp.expm1(-2.0 * decay_rate))
    fore_states, fore_decays, fore_exit, fore_log = modal_local(
        logs, jnp.zeros_like(logs[:, 0, :]), stream, cotangent
    )
    back_logs = jnp.concatenate(
        [jnp.zeros_like(logs[:, :1, :]), logs[:, ::-1, :][:, :-1, :]], axis=1
    )
    back_states, back_decays, back_exit, back_log = modal_local(
        back_logs, logs[:, 0, :], stream[:, ::-1, :], cotangent[:, ::-1, :]
    )
    summary = (jnp.exp(fore_log), fore_exit, jnp.exp(back_log), back_exit)
    identity = (
        jnp.ones_like(fore_log),
        jnp.zeros_like(fore_exit),
        jnp.ones_like(back_log),
        jnp.zeros_like(back_exit),
    )
    from_lower = entering_2(summary, "seq", join_lower, identity, False)
    from_upper = entering_2(summary, "seq", join_upper, identity, True)
    fore_entry = closed(
        summary[0], summary[1], from_lower[0], from_lower[1], from_upper[0], from_upper[1]
    )
    back_entry = closed(
        summary[2], summary[3], from_upper[2], from_upper[3], from_lower[2], from_lower[3]
    )
    fore_totals, fore_rows = modal_terms(
        fore_states,
        fore_decays,
        fore_entry,
        cot_wide,
        mode_scale,
        mode_scale[:, None] * mode_weight[1],
    )
    back_totals, back_rows = modal_terms(
        back_states,
        back_decays,
        back_entry,
        cot_wide[:, ::-1, :],
        mode_scale,
        mode_scale[:, None] * mode_weight[0],
    )
    gradient = cot_wide + fore_rows + back_rows[:, ::-1, :]
    mode_terms = jnp.stack([fore_totals, back_totals]).reshape(2 * M, -1)
    tap_terms = []
    for layer_position in reversed(range(LAYERS)):
        bin_distance = (DILATION_FIRST1 if layer_position == 0 else DILATION_SECOND2) // input_rows
        before, inverse, reduced, lagged, advanced, mixture = stored[layer_position]
        narrow_width = gradient.astype(jnp.bfloat16)
        back_mixed = jnp.einsum(
            "yhi,ai->yha",
            narrow_width,
            full_up_weight[layer_position],
            preferred_element_type=jnp.float32,
        )
        mixed_grad = (back_mixed * gelu_slope(mixture)).astype(jnp.bfloat16)
        tap_terms.insert(
            0,
            jnp.stack(
                [
                    contract(lagged, mixed_grad),
                    contract(reduced, mixed_grad),
                    contract(advanced, mixed_grad),
                ]
            ),
        )
        reduced_grad = jnp.einsum(
            "glk,bk->glb",
            mixed_grad,
            tap_full[layer_position, 1],
            preferred_element_type=jnp.float32,
        )
        reduced_grad = reduced_grad + jnp.einsum(
            "glk,bk->glb",
            moved(mixed_grad, -bin_distance),
            tap_full[layer_position, 0],
            preferred_element_type=jnp.float32,
        )
        reduced_grad = reduced_grad + jnp.einsum(
            "glk,bk->glb",
            moved(mixed_grad, bin_distance),
            tap_full[layer_position, 2],
            preferred_element_type=jnp.float32,
        )
        normed_grad = project_back(reduced_grad.astype(jnp.bfloat16), down_full[layer_position])
        gradient = (
            gradient
            + inverse * normed_grad
            - before
            * inverse
            * inverse
            * inverse
            * jnp.mean(normed_grad * before, axis=-1, keepdims=True)
        )
    tap_flat = jnp.stack(tap_terms).reshape(LAYERS * 3 * B, B)
    seq_size = lax.axis_size("seq")
    dp_size = lax.axis_size("dp")
    report_scale = 1.0 / math.sqrt(genome_count * dp_size * input_rows * seq_size)
    tap_sum, mode_sum = (
        lax.psum_scatter(tap_flat, ("seq", "dp"), scatter_dimension=0, tiled=True),
        lax.psum_scatter(mode_terms, ("seq", "dp"), scatter_dimension=1, tiled=True),
    )
    return (gradient.astype(jnp.bfloat16), tap_sum * report_scale, mode_sum * report_scale)


VMEM = pltpu.MemorySpace.VMEM
SMEM = pltpu.MemorySpace.SMEM
F32 = jnp.float32
BF16 = jnp.bfloat16
RING = 8
HOPS = (4, 2, 1)
BLOCK = 48


def call(body, operands, spaces, outs, scratch=(), flops=0):
    return pl.pallas_call(
        body,
        out_shape=[jax.ShapeDtypeStruct(shape, dtype) for shape, dtype in outs],
        in_specs=[pl.BlockSpec(memory_space=space) for space in spaces],
        out_specs=[pl.BlockSpec(memory_space=VMEM) for _ in outs],
        scratch_shapes=list(scratch),
        compiler_params=pltpu.CompilerParams(vmem_limit_bytes=40 * 1024 * 1024),
    )(*operands)


def dot(left, right):
    return lax.dot_general(left, right, (((1,), (0,)), ((), ())), preferred_element_type=F32)


def dot_nt(left, right):
    return lax.dot_general(left, right, (((1,), (1,)), ((), ())), preferred_element_type=F32)


def dot_tn(left, right):
    return lax.dot_general(left, right, (((0,), (0,)), ((), ())), preferred_element_type=F32)


def iota2(shape, axis):
    return lax.broadcasted_iota(jnp.int32, shape, axis)


def split_pair(value):
    high = value.astype(BF16)
    return high, (value - high.astype(F32)).astype(BF16)


def log_sums(keep_row):
    rows = keep_row.shape[-1]
    below, beside = iota2((rows, rows), 0), iota2((rows, rows), 1)
    logs = jnp.broadcast_to(jnp.log(keep_row), (rows, rows))
    column = jnp.sum(jnp.where(beside <= below, logs, 0.0), axis=1, keepdims=True)
    spread = jnp.broadcast_to(column, (rows, rows))
    row = jnp.sum(jnp.where(beside == below, spread, 0.0), axis=0, keepdims=True)
    return column, row, column[rows - 1 :, :]


def prepare_body(cot_ref, keep_ref, decay_ref, tap_ref, pay_ref, tap_sum_ref):
    rows = keep_ref.shape[-1]
    _, sums, total = log_sums(keep_ref[...])
    place = iota2((1, rows), 1).astype(F32)
    exits = []
    for mode in range(M):
        exits.append(jnp.exp((total - sums) - (rows - 1.0 - place) * decay_ref[mode]))
    for mode in range(M):
        exits.append(jnp.exp(sums - (place + 1.0) * decay_ref[mode]))
    weights = jnp.concatenate(exits, axis=0)
    high, low = split_pair(weights)
    cot = cot_ref[0]
    states = dot(high, cot) + dot(low, cot)
    width = cot.shape[-1]
    first = jnp.broadcast_to(total, (8, width))
    one = first.astype(BF16).astype(F32)
    two = (first - one).astype(BF16).astype(F32)
    three = first - one - two
    row = iota2((8, width), 0)
    extra = jnp.where(row == 0, one, jnp.where(row == 1, two, jnp.where(row == 2, three, 0.0)))
    pay_ref[...] = jnp.concatenate([states, extra], axis=0).astype(BF16)
    for layer in range(LAYERS):
        taps = tap_ref[layer, 0].astype(F32) + tap_ref[layer, 1].astype(F32)
        tap_sum_ref[layer] = (taps + tap_ref[layer, 2].astype(F32)).astype(BF16)


def forward_body(
    feature_ref, count_ref, weight_ref, down_ref, down_far_ref, tap_ref, tap_far_ref,
    up_ref, up_far_ref, stream_ref, inverse_ref, reduced_ref, mixture_ref,
):
    core = lax.axis_index("dp")
    rows, width = feature_ref.shape[1:]
    half = down_ref.shape[-1]
    wide = up_ref.shape[-1]
    own = pl.ds(pl.multiple_of(core * half, half), half)
    far = pl.ds(pl.multiple_of((1 - core) * half, half), half)
    logs = jnp.broadcast_to(jnp.log1p(count_ref[...].astype(F32)), (rows, rows))
    diagonal = iota2((rows, rows), 0) == iota2((rows, rows), 1)
    level = jnp.sum(jnp.where(diagonal, logs, 0.0), axis=1, keepdims=True)
    stream = feature_ref[0].astype(F32) + level * weight_ref[...]
    for layer in range(LAYERS):
        stream_ref[layer] = stream
        mean = jnp.sum(stream * stream, axis=-1, keepdims=True) * (1.0 / width)
        inverse = lax.rsqrt(mean + EPSILON)
        inverse_ref[layer] = inverse
        normed = (stream * inverse).astype(BF16)
        near = dot(normed, down_ref[layer]).astype(BF16)
        away = dot(normed, down_far_ref[layer]).astype(BF16)
        reduced_ref[layer, 0] = near
        reduced_ref[layer, 1] = away
        mix_near = dot(near, tap_ref[layer, own, :]) + dot(away, tap_ref[layer, far, :])
        mix_away = dot(near, tap_far_ref[layer, own, :]) + dot(away, tap_far_ref[layer, far, :])
        mixture_ref[layer, 0] = mix_near
        mixture_ref[layer, 1] = mix_away
        act_near = gelu_exact(mix_near).astype(BF16)
        act_away = gelu_exact(mix_away).astype(BF16)
        out_near = dot(act_near, up_ref[layer, own, :]) + dot(act_away, up_ref[layer, far, :])
        out_away = dot(act_near, up_far_ref[layer, own, :]) + dot(act_away, up_far_ref[layer, far, :])
        low = jnp.where(core == 0, out_near, out_away)
        high = jnp.where(core == 0, out_away, out_near)
        stream = stream + jnp.concatenate([low, high], axis=-1)
    stream_ref[LAYERS] = stream


def backward_body(
    decay_ref, scale_ref, near_ref, away_ref, cot_ref, keep_ref, mode_ref, stream_ref,
    inverse_ref, reduced_ref, mixture_ref, down_ref, down_far_ref, tap_ref, tap_far_ref,
    up_ref, up_far_ref, grad_ref, kept_ref, send_ref, partial_ref, edge_ref, grads_ref,
    block_ref,
):
    core = lax.axis_index("dp")
    place = lax.axis_index("seq")
    rows, width = cot_ref.shape[1:]
    half = down_ref.shape[-1]
    wide = up_ref.shape[-1]
    own = pl.ds(pl.multiple_of(core * half, half), half)
    far = pl.ds(pl.multiple_of((1 - core) * half, half), half)

    masks = [0]
    for hop in HOPS:
        masks = masks + [mask ^ hop for mask in masks]
    pieces = [near_ref[index].astype(F32) for index in range(RING // 2)]
    pieces = pieces + [away_ref[index].astype(F32) for index in range(RING // 2)]
    totals = [jnp.sum(piece[8:16, 0:128], axis=0, keepdims=True) for piece in pieces]
    row8 = iota2((8, 128), 0)
    decay8 = jnp.zeros((8, 128), F32)
    for index in range(2 * M):
        decay8 = jnp.where(row8 == index, decay_ref[index % M], decay8)
    everything = totals[0]
    for value in totals[1:]:
        everything = everything + value
    loop = 1.0 - jnp.exp(jnp.broadcast_to(everything, (8, 128)) - (RING * rows) * decay8)
    others = [lax.bitwise_xor(place, mask) for mask in masks]
    ahead = [lax.rem(place - other + (RING - 1), RING) for other in others]
    after = [lax.rem(other - place + (RING - 1), RING) for other in others]
    entering = jnp.zeros((8, width), F32)
    for index in range(RING):
        fore = jnp.zeros((1, 128), F32)
        back = jnp.zeros((1, 128), F32)
        for other in range(RING):
            fore = fore + jnp.where(ahead[other] < ahead[index], totals[other], 0.0)
            back = back + jnp.where(after[other] < after[index], totals[other], 0.0)
        fore = jnp.broadcast_to(fore, (8, 128)) - (ahead[index] * rows).astype(F32) * decay8
        back = jnp.broadcast_to(back, (8, 128)) - (after[index] * rows).astype(F32) * decay8
        share = jnp.exp(jnp.where(row8 < M, fore, back)) / loop
        entering = entering + share[:, 0:1] * pieces[index][0:8, :]
    edge_ref[...] = entering

    column, row, total = log_sums(keep_ref[...])
    down_rows = iota2((rows, rows), 0)
    across = iota2((rows, rows), 1)
    gap = column - row
    steps = (down_rows - across).astype(F32)
    spot = iota2((rows, 1), 0).astype(F32)
    kernels = []
    edges = []
    for mode in range(M):
        rate = decay_ref[mode]
        value = jnp.exp(jnp.minimum(gap - steps * rate, 0.0))
        kernels.append(jnp.where(down_rows >= across, value, 0.0))
        edges.append(jnp.exp(column - (spot + 1.0) * rate))
    for mode in range(M):
        rate = decay_ref[mode]
        value = jnp.exp(jnp.minimum(steps * rate - gap, 0.0))
        kernels.append(jnp.where(across >= down_rows, value, 0.0))
        edges.append(jnp.exp((total - column) - (rows - 1.0 - spot) * rate))
    pairs = [jnp.concatenate(split_pair(kernel), axis=1) for kernel in kernels]
    span = 128
    for start in range(0, width, span):
        part = slice(start, start + span)
        cot = cot_ref[0, :, part]
        doubled = jnp.concatenate([cot, cot], axis=0)
        stream = stream_ref[LAYERS, :, part]
        grad = cot.astype(F32)
        marks = [None] * (2 * M)
        for index in range(2 * M):
            mode = index % M
            field = dot(pairs[index], doubled) + edges[index] * edge_ref[index : index + 1, part]
            gain = scale_ref[mode]
            side = 1 - index // M
            grad = grad + (gain * mode_ref[side, mode : mode + 1, part]) * field
            marks[side * M + mode] = gain * jnp.sum(stream * field, axis=0, keepdims=True)
        grads_ref[:, part] = grad
        top = 8 * (start // wide)
        partial_ref[top : top + 8, start % wide : start % wide + span] = jnp.concatenate(marks, axis=0)

    high, low = split_pair(partial_ref[...])
    tap_rows = RING * BLOCK
    send_ref[tap_rows : tap_rows + 16, :] = high
    send_ref[tap_rows + 16 : tap_rows + 32, :] = low

    for layer in reversed(range(LAYERS)):
        gradient = grads_ref[...]
        narrow = gradient.astype(BF16)
        first, second = narrow[:, :wide], narrow[:, wide:]
        mine = jnp.where(core == 0, first, second)
        theirs = jnp.where(core == 0, second, first)
        mixed = []
        for index, part in enumerate((own, far)):
            back = dot_nt(mine, up_ref[layer, part, :]) + dot_nt(theirs, up_far_ref[layer, part, :])
            mixed.append((back * gelu_slope(mixture_ref[layer, index])).astype(BF16))
        whole = []
        for near, away in (mixed, (reduced_ref[layer, 0], reduced_ref[layer, 1])):
            straight = jnp.concatenate([near, away], axis=1)
            crossed = jnp.concatenate([away, near], axis=1)
            whole.append(jnp.where(core == 0, straight, crossed))
        block_ref[...] = dot_tn(whole[1], whole[0])
        for turn in range(4):
            to = 2 * turn + layer
            kept = lax.rem(3 * core + 6 * (turn // 2) + 4 * (turn % 2), RING)
            sent = lax.rem(3 * (1 - core) + 6 * (turn // 2) + 4 * (turn % 2), RING)
            kept_ref[to * BLOCK : (to + 1) * BLOCK, :] = block_ref[pl.ds(pl.multiple_of(kept * BLOCK, BLOCK), BLOCK), :]
            send_ref[to * BLOCK : (to + 1) * BLOCK, :] = block_ref[
                pl.ds(pl.multiple_of(sent * BLOCK, BLOCK), BLOCK), :
            ].astype(BF16)
        normed = None
        for part, source in ((own, down_ref), (far, down_far_ref)):
            passed = dot_nt(mixed[0], tap_ref[layer, part, :]) + dot_nt(mixed[1], tap_far_ref[layer, part, :])
            term = dot_nt(passed.astype(BF16), source[layer])
            normed = term if normed is None else normed + term
        before = stream_ref[layer]
        inverse = inverse_ref[layer]
        shared = jnp.sum(normed * before, axis=-1, keepdims=True) * (1.0 / width)
        grads_ref[...] = gradient + inverse * normed - before * (inverse * inverse * inverse * shared)
    grad_ref[0] = grads_ref[...].astype(BF16)


def position_bit(stage):
    place = lax.axis_index("seq")
    return lax.rem(place // (1, 2, 4)[stage], 2)


def join_body(stage, kept_ref, got_ref, partial_ref, kept_out, send_out, partial_out):
    rows = kept_out.shape[0]
    bit = position_bit(stage)
    keep = pl.ds(pl.multiple_of(bit * rows, rows), rows)
    send = pl.ds(pl.multiple_of((1 - bit) * rows, rows), rows)
    kept_out[...] = kept_ref[keep, :] + got_ref[keep, :].astype(F32)
    send_out[0:rows, :] = (kept_ref[send, :] + got_ref[send, :].astype(F32)).astype(BF16)
    high = got_ref[2 * rows : 2 * rows + 16, :].astype(F32)
    low = got_ref[2 * rows + 16 : 2 * rows + 32, :].astype(F32)
    partial = partial_ref[...] + (high + low)
    partial_out[...] = partial
    high, low = split_pair(partial)
    send_out[rows : rows + 16, :] = high
    send_out[rows + 16 : rows + 32, :] = low


def finish_body(scale, kept_ref, got_ref, partial_ref, block_out, mode_out, full_ref):
    rows = kept_ref.shape[0]
    block_out[...] = (kept_ref[...] + got_ref[0:rows, :].astype(F32)) * scale
    high = got_ref[rows : rows + 16, :].astype(F32)
    low = got_ref[rows + 16 : rows + 32, :].astype(F32)
    full_ref[...] = (partial_ref[...] + (high + low)) * scale
    number = 2 * lax.axis_index("seq") + lax.axis_index("dp")
    span = full_ref.shape[1]
    top = pl.multiple_of(8 * (number // 8), 8)
    shift = lax.rem(span - BLOCK * lax.rem(number, 8), span)
    mode_out[...] = pltpu.roll(full_ref[pl.ds(top, 8), :], shift, 1)[:, 0:BLOCK]


def swap(value, axis, mask):
    count = lax.axis_size(axis)
    return lax.ppermute(value, axis, [(source, source ^ mask) for source in range(count)])


def wrapped_device(
    features, cotangent, counts, count_weight, down_weight, tap_weight, up_weight,
    decay_rate, keep_share, mode_weight,
):
    rows, width = features.shape[1:]
    half, wide = down_weight.shape[-1], up_weight.shape[-1]
    down_far = swap(down_weight, "dp", 1)
    pay, tap_sum = call(
        prepare_body,
        (cotangent, keep_share, decay_rate, tap_weight),
        (VMEM, VMEM, SMEM, VMEM),
        (((16, width), BF16), ((LAYERS, B, half), BF16)),
    )
    tap_far = swap(tap_sum, "dp", 1)
    up_far = swap(up_weight, "dp", 1)
    group = pay[None]
    for hop in HOPS[:-1]:
        group = jnp.concatenate([group, swap(group, "seq", hop)], axis=0)
    away = swap(group, "seq", HOPS[-1])
    scale = jnp.sqrt(-jnp.expm1(-2.0 * decay_rate))
    stream, inverse, reduced, mixture = call(
        forward_body,
        (features, counts, count_weight[None], down_weight, down_far, tap_sum, tap_far, up_weight, up_far),
        (VMEM,) * 9,
        (
            ((LAYERS + 1, rows, width), F32),
            ((LAYERS, rows, 1), F32),
            ((LAYERS, 2, rows, half), BF16),
            ((LAYERS, 2, rows, half), F32),
        ),
    )
    grad, kept, send, partial = call(
        backward_body,
        (
            decay_rate, scale, group, away, cotangent, keep_share, mode_weight, stream, inverse, reduced,
            mixture, down_weight, down_far, tap_sum, tap_far, up_weight, up_far,
        ),
        (SMEM, SMEM) + (VMEM,) * 15,
        (
            ((1, rows, width), BF16),
            ((RING * BLOCK, B), F32),
            ((RING * BLOCK + 32, B), BF16),
            ((16, B), F32),
        ),
        (pltpu.VMEM((8, width), F32), pltpu.VMEM((rows, width), F32), pltpu.VMEM((B, B), F32)),
    )
    got = swap(send, "dp", 1)
    for stage in range(3):
        kept_rows = kept.shape[0] // 2
        kept, send, partial = call(
            functools.partial(join_body, stage),
            (kept, got, partial),
            (VMEM,) * 3,
            (((kept_rows, B), F32), ((kept_rows + 32, B), BF16), ((16, B), F32)),
        )
        got = swap(send, "seq", (1, 2, 4)[stage])
    total = features.shape[0] * lax.axis_size("dp") * rows * lax.axis_size("seq")
    block, mode_sum = call(
        functools.partial(finish_body, 1.0 / math.sqrt(total)),
        (kept, got, partial),
        (VMEM,) * 3,
        (((BLOCK, B), F32), ((8, BLOCK), F32)),
        (pltpu.VMEM((16, B), F32),),
    )
    parts = [block]
    for step in (3, 6):
        pairs = [(8 * layer + (j + step) % 8, 8 * layer + j) for layer in range(LAYERS) for j in range(8)]
        parts.append(lax.ppermute(block, ("seq", "dp"), pairs))
    return grad, jnp.concatenate(parts, axis=0), mode_sum


def solution(mesh):
    placed = (
        P(("parts", "dp"), "seq", None),
        P(("parts", "dp"), "seq", None),
        P(("parts", "dp"), "seq"),
        P(),
        P(None, None, "dp"),
        P(None, None, None, "dp"),
        P(None, None, "dp"),
        P(),
        P(("parts", "dp"), "seq"),
        P(),
    )

    def per_device(*operands):
        rows = operands[0].shape[1]
        ring = lax.axis_size("seq")
        loop = ring * rows
        wraps = all(dilation % loop == 0 for dilation in (DILATION_FIRST1, DILATION_SECOND2))
        fits = ring == RING and lax.axis_size("dp") == 2 and operands[0].shape[0] == 1
        return (wrapped_device if wraps and fits else general_device)(*operands)

    return jax.shard_map(
        per_device,
        mesh=mesh,
        in_specs=placed,
        out_specs=(
            P(("parts", "dp"), "seq", None),
            P(("parts", "seq", "dp"), None),
            P("parts", ("seq", "dp")),
        ),
        check_vma=False,
    )
```

```python
import functools
import math

import jax
import jax.numpy as jnp
from jax import lax
from jax.experimental import pallas as pl
from jax.experimental.pallas import tpu as pltpu
from jax.sharding import PartitionSpec as P

B = 384
DILATION_FIRST1 = 2048
DILATION_SECOND2 = 4096
M = 4
LAYERS = 2


EPSILON = 1e-06
HALF_ROOT = 1.0 / math.sqrt(2.0)
DENSITY = 1.0 / math.sqrt(2.0 * math.pi)
TOP_PRECISION = lax.Precision.HIGHEST


def shifted(value, axis, steps):
    count = lax.axis_size(axis)
    pairs = [(source, (source + steps) % count) for source in range(count)]
    return lax.ppermute(value, axis, pairs)


def entering_2(shard, axis, join, neutral, backward):
    count = lax.axis_size(axis)
    place = lax.axis_index(axis)
    ahead = count - 1 - place if backward else place
    gathered = jax.tree.map(
        lambda a, kind: lax.all_gather(a.astype(kind), axis),
        shard,
        jax.tree.map(lambda a: jnp.bfloat16 if a.dtype == jnp.float32 else a.dtype, shard),
    )
    state = jax.tree.map(lambda a, e: jnp.zeros_like(a) + jnp.asarray(e, a.dtype), shard, neutral)

    def one(turn, state):
        source = count - 1 - turn if backward else turn
        return join(
            state,
            jax.tree.map(
                lambda a, own: lax.dynamic_index_in_dim(a, source, 0, False).astype(own.dtype),
                gathered,
                shard,
            ),
        )

    return lax.fori_loop(0, ahead, one, state)


def gelu_exact(values):
    return 0.5 * values * (1.0 + lax.erf(values * HALF_ROOT))


def gelu_slope(values):
    cumulative = 0.5 * (1.0 + lax.erf(values * HALF_ROOT))
    return cumulative + values * jnp.exp(-0.5 * values * values) * DENSITY


def project(left_shifted, right_shifted):
    return jnp.einsum(
        "qra,au->qru", left_shifted, right_shifted, preferred_element_type=jnp.float32
    )


def project_back(left_shifted, right_shifted):
    return jnp.einsum(
        "kut,st->kus", left_shifted, right_shifted, preferred_element_type=jnp.float32
    )


def contract(left_shifted, right_shifted):
    return jnp.einsum(
        "glb,glk->bk", left_shifted, right_shifted, preferred_element_type=jnp.float32
    )


def moved(values, bin_distance):
    return shifted(values, "seq", bin_distance)


def block_product(kernel, pieces):
    return jnp.einsum(
        "gmbij,gbjc->gmbic",
        kernel,
        pieces,
        precision=TOP_PRECISION,
        preferred_element_type=jnp.float32,
    )


def modal_local(lg_in, lg_exit, stream_rows, cotangent_rows):
    genome_count, input_rows, mode_count = lg_in.shape
    feature_maps = stream_rows.shape[-1]
    block_size = min(128, input_rows)
    block_count = input_rows // block_size
    running = jnp.cumsum(lg_in, axis=1)
    running_blocks = running.reshape(genome_count, block_count, block_size, mode_count)
    block_ends = running_blocks[:, :, -1, :]
    block_starts = jnp.concatenate(
        [jnp.zeros((genome_count, 1, mode_count), jnp.float32), block_ends[:, :-1, :]], axis=1
    )
    within = running_blocks - block_starts[:, :, None, :]
    within_t = jnp.transpose(within, (0, 3, 1, 2))
    spread = within_t[..., :, None] - within_t[..., None, :]
    row_index = lax.broadcasted_iota(jnp.int32, (block_size, block_size), 0)
    column_index = lax.broadcasted_iota(jnp.int32, (block_size, block_size), 1)
    kernel = jnp.where(row_index >= column_index, jnp.exp(jnp.minimum(spread, 0.0)), 0.0)
    joined_source = jnp.concatenate([stream_rows, cotangent_rows.astype(jnp.float32)], axis=-1)
    joined_source = joined_source.reshape(genome_count, block_count, block_size, 2 * feature_maps)
    partial_value = block_product(kernel, joined_source)
    block_tails = partial_value[:, :, :, -1, :]
    ends_t = jnp.transpose(block_ends, (0, 2, 1))
    starts_t = jnp.transpose(block_starts, (0, 2, 1))
    spacing = starts_t[..., :, None] - ends_t[..., None, :]
    block_index = lax.broadcasted_iota(jnp.int32, (block_count, block_count), 0)
    source_index = lax.broadcasted_iota(jnp.int32, (block_count, block_count), 1)
    linkage = jnp.where(source_index < block_index, jnp.exp(jnp.minimum(spacing, 0.0)), 0.0)
    entering = jnp.einsum(
        "gmbk,gmkc->gmbc",
        linkage,
        block_tails,
        precision=TOP_PRECISION,
        preferred_element_type=jnp.float32,
    )
    states = partial_value + jnp.exp(within_t)[..., None] * entering[:, :, :, None, :]
    states = states.reshape(genome_count, mode_count, input_rows, 2 * feature_maps)
    decay_values = jnp.exp(jnp.transpose(running, (0, 2, 1)))
    exit_state = jnp.exp(lg_exit)[..., None] * states[:, :, -1, :]
    log_pass = running[:, -1, :] + lg_exit
    return (states, decay_values, exit_state, log_pass)


def modal_terms(states, decay_values, entering, cotangent_rows, source_gain, cot_gain):
    feature_maps = cotangent_rows.shape[-1]
    reach_sum = jnp.einsum(
        "qsz,qzj->qsj",
        decay_values,
        cotangent_rows,
        precision=TOP_PRECISION,
        preferred_element_type=jnp.float32,
    )
    totals = jnp.einsum(
        "veyi,vyi->ei",
        states[..., :feature_maps],
        cotangent_rows,
        precision=TOP_PRECISION,
        preferred_element_type=jnp.float32,
    )
    totals = totals + jnp.sum(entering[..., :feature_maps] * reach_sum, axis=0)
    rows_out = jnp.einsum(
        "jryf,rf->jyf",
        states[..., feature_maps:],
        cot_gain,
        precision=TOP_PRECISION,
        preferred_element_type=jnp.float32,
    )
    rows_out = rows_out + jnp.einsum(
        "ert,erx->etx",
        decay_values,
        entering[..., feature_maps:] * cot_gain[None],
        precision=TOP_PRECISION,
        preferred_element_type=jnp.float32,
    )
    return (source_gain[:, None] * totals, rows_out)


def apply_early_first(early_pass, early_state, late_pass, late_state):
    return (early_pass * late_pass, late_pass[..., None] * early_state + late_state)


def apply_late_first(early_pass, early_state, late_pass, late_state):
    return (early_pass * late_pass, early_pass[..., None] * late_state + early_state)


def join_lower(early, late):
    fore_pass, fore_state = apply_early_first(early[0], early[1], late[0], late[1])
    back_pass, back_state = apply_late_first(early[2], early[3], late[2], late[3])
    return (fore_pass, fore_state, back_pass, back_state)


def join_upper(early, late):
    fore_pass, fore_state = apply_late_first(early[0], early[1], late[0], late[1])
    back_pass, back_state = apply_early_first(early[2], early[3], late[2], late[3])
    return (fore_pass, fore_state, back_pass, back_state)


def closed(own_pass, own_state, pass_before, state_before, pass_after, state_after):
    beside_all = pass_before * pass_after
    numerator = (
        beside_all[..., None] * own_state + pass_before[..., None] * state_after + state_before
    )
    return numerator / (1.0 - beside_all * own_pass)[..., None]


def general_device(
    features,
    cotangent,
    counts,
    count_weight,
    down_weight,
    tap_weight,
    up_weight,
    decay_rate,
    keep_share,
    mode_weight,
):
    genome_count = features.shape[0]
    input_rows = features.shape[1]
    down_full, tap_full, full_up_weight = (
        lax.all_gather(down_weight, "dp", axis=2, tiled=True),
        lax.all_gather(tap_weight, "dp", axis=3, tiled=True),
        lax.all_gather(up_weight, "dp", axis=2, tiled=True),
    )
    stream = (
        features.astype(jnp.float32)
        + jnp.log1p(counts.astype(jnp.float32))[..., None] * count_weight
    )
    stored = []
    for layer_position in range(LAYERS):
        bin_distance = (DILATION_FIRST1 if layer_position == 0 else DILATION_SECOND2) // input_rows
        inverse = lax.rsqrt(jnp.mean(stream * stream, axis=-1, keepdims=True) + EPSILON)
        normed = (stream * inverse).astype(jnp.bfloat16)
        reduced = project(normed, down_full[layer_position]).astype(jnp.bfloat16)
        lagged = moved(reduced, bin_distance)
        advanced = moved(reduced, -bin_distance)
        mixture = (
            project(lagged, tap_full[layer_position, 0])
            + project(reduced, tap_full[layer_position, 1])
            + project(advanced, tap_full[layer_position, 2])
        )
        active_modes = gelu_exact(mixture).astype(jnp.bfloat16)
        stored.append((stream, inverse, reduced, lagged, advanced, mixture))
        stream = stream + jnp.einsum(
            "quy,yk->quk",
            active_modes,
            full_up_weight[layer_position],
            preferred_element_type=jnp.float32,
        )
    cot_wide = cotangent.astype(jnp.float32)
    logs = jnp.log(keep_share)[:, :, None] - decay_rate[None, None, :]
    mode_scale = jnp.sqrt(-jnp.expm1(-2.0 * decay_rate))
    fore_states, fore_decays, fore_exit, fore_log = modal_local(
        logs, jnp.zeros_like(logs[:, 0, :]), stream, cotangent
    )
    back_logs = jnp.concatenate(
        [jnp.zeros_like(logs[:, :1, :]), logs[:, ::-1, :][:, :-1, :]], axis=1
    )
    back_states, back_decays, back_exit, back_log = modal_local(
        back_logs, logs[:, 0, :], stream[:, ::-1, :], cotangent[:, ::-1, :]
    )
    summary = (jnp.exp(fore_log), fore_exit, jnp.exp(back_log), back_exit)
    identity = (
        jnp.ones_like(fore_log),
        jnp.zeros_like(fore_exit),
        jnp.ones_like(back_log),
        jnp.zeros_like(back_exit),
    )
    from_lower = entering_2(summary, "seq", join_lower, identity, False)
    from_upper = entering_2(summary, "seq", join_upper, identity, True)
    fore_entry = closed(
        summary[0], summary[1], from_lower[0], from_lower[1], from_upper[0], from_upper[1]
    )
    back_entry = closed(
        summary[2], summary[3], from_upper[2], from_upper[3], from_lower[2], from_lower[3]
    )
    fore_totals, fore_rows = modal_terms(
        fore_states,
        fore_decays,
        fore_entry,
        cot_wide,
        mode_scale,
        mode_scale[:, None] * mode_weight[1],
    )
    back_totals, back_rows = modal_terms(
        back_states,
        back_decays,
        back_entry,
        cot_wide[:, ::-1, :],
        mode_scale,
        mode_scale[:, None] * mode_weight[0],
    )
    gradient = cot_wide + fore_rows + back_rows[:, ::-1, :]
    mode_terms = jnp.stack([fore_totals, back_totals]).reshape(2 * M, -1)
    tap_terms = []
    for layer_position in reversed(range(LAYERS)):
        bin_distance = (DILATION_FIRST1 if layer_position == 0 else DILATION_SECOND2) // input_rows
        before, inverse, reduced, lagged, advanced, mixture = stored[layer_position]
        narrow_width = gradient.astype(jnp.bfloat16)
        back_mixed = jnp.einsum(
            "yhi,ai->yha",
            narrow_width,
            full_up_weight[layer_position],
            preferred_element_type=jnp.float32,
        )
        mixed_grad = (back_mixed * gelu_slope(mixture)).astype(jnp.bfloat16)
        tap_terms.insert(
            0,
            jnp.stack(
                [
                    contract(lagged, mixed_grad),
                    contract(reduced, mixed_grad),
                    contract(advanced, mixed_grad),
                ]
            ),
        )
        reduced_grad = jnp.einsum(
            "glk,bk->glb",
            mixed_grad,
            tap_full[layer_position, 1],
            preferred_element_type=jnp.float32,
        )
        reduced_grad = reduced_grad + jnp.einsum(
            "glk,bk->glb",
            moved(mixed_grad, -bin_distance),
            tap_full[layer_position, 0],
            preferred_element_type=jnp.float32,
        )
        reduced_grad = reduced_grad + jnp.einsum(
            "glk,bk->glb",
            moved(mixed_grad, bin_distance),
            tap_full[layer_position, 2],
            preferred_element_type=jnp.float32,
        )
        normed_grad = project_back(reduced_grad.astype(jnp.bfloat16), down_full[layer_position])
        gradient = (
            gradient
            + inverse * normed_grad
            - before
            * inverse
            * inverse
            * inverse
            * jnp.mean(normed_grad * before, axis=-1, keepdims=True)
        )
    tap_flat = jnp.stack(tap_terms).reshape(LAYERS * 3 * B, B)
    seq_size = lax.axis_size("seq")
    dp_size = lax.axis_size("dp")
    report_scale = 1.0 / math.sqrt(genome_count * dp_size * input_rows * seq_size)
    tap_sum, mode_sum = (
        lax.psum_scatter(tap_flat, ("seq", "dp"), scatter_dimension=0, tiled=True),
        lax.psum_scatter(mode_terms, ("seq", "dp"), scatter_dimension=1, tiled=True),
    )
    return (gradient.astype(jnp.bfloat16), tap_sum * report_scale, mode_sum * report_scale)


VMEM = pltpu.MemorySpace.VMEM
SMEM = pltpu.MemorySpace.SMEM
HBM = pltpu.MemorySpace.HBM
F32 = jnp.float32
BF16 = jnp.bfloat16
RING = 8
HOPS = (4, 2, 1)
BLOCK = 48
GIGA = 10**6


def call(body, operands, spaces, outs, scratch=(), size=0):
    return pl.pallas_call(
        body,
        out_shape=[jax.ShapeDtypeStruct(shape, dtype) for shape, dtype in outs],
        in_specs=[pl.BlockSpec(memory_space=space) for space in spaces],
        out_specs=[pl.BlockSpec(memory_space=VMEM) for _ in outs],
        scratch_shapes=list(scratch),
        cost_estimate=pl.CostEstimate(flops=size, transcendentals=0, bytes_accessed=size // 256) if size else None,
        compiler_params=pltpu.CompilerParams(vmem_limit_bytes=40 * 1024 * 1024),
    )(*operands)


def dot(left, right):
    return lax.dot_general(left, right, (((1,), (0,)), ((), ())), preferred_element_type=F32)


def dot_nt(left, right):
    return lax.dot_general(left, right, (((1,), (1,)), ((), ())), preferred_element_type=F32)


def dot_tn(left, right):
    return lax.dot_general(left, right, (((0,), (0,)), ((), ())), preferred_element_type=F32)


def iota2(shape, axis):
    return lax.broadcasted_iota(jnp.int32, shape, axis)


def split_pair(value):
    high = value.astype(BF16)
    return high, (value - high.astype(F32)).astype(BF16)


def log_sums(keep_row):
    rows = keep_row.shape[-1]
    below, beside = iota2((rows, rows), 0), iota2((rows, rows), 1)
    logs = jnp.broadcast_to(jnp.log(keep_row), (rows, rows))
    column = jnp.sum(jnp.where(beside <= below, logs, 0.0), axis=1, keepdims=True)
    spread = jnp.broadcast_to(column, (rows, rows))
    row = jnp.sum(jnp.where(beside == below, spread, 0.0), axis=0, keepdims=True)
    return column, row, column[rows - 1 :, :]


def mode_terms(sums, total, decay_ref, rows):
    place = iota2((1, rows), 1).astype(F32)
    to_start, to_end = [], []
    for mode in range(M):
        rate = decay_ref[mode]
        to_start.append(jnp.exp(sums - (place + 1.0) * rate))
        to_end.append(jnp.exp((total - sums) - (rows - 1.0 - place) * rate))
    leaving = jnp.concatenate(to_start + to_end, axis=0)
    entering = jnp.concatenate(to_end + to_start, axis=0)
    return leaving, entering


def prepare_body(cot_hbm, keep_hbm, decay_hbm, pay_ref, cot_ref, keep_ref, decay_ref, sems):
    pairs = ((keep_hbm, keep_ref), (decay_hbm, decay_ref), (cot_hbm, cot_ref))
    copies = [pltpu.make_async_copy(source, to, sems.at[index]) for index, (source, to) in enumerate(pairs)]
    for copy in copies:
        copy.start()
    copies[0].wait()
    copies[1].wait()
    rows = keep_ref.shape[-1]
    _, sums, total = log_sums(keep_ref[...])
    weights, _ = mode_terms(sums, total, decay_ref, rows)
    high = weights.astype(BF16).astype(F32)
    both = jnp.concatenate([high, weights - high], axis=0).astype(BF16)
    width = cot_ref.shape[-1]
    first = jnp.broadcast_to(total, (8, width))
    one = first.astype(BF16).astype(F32)
    two = (first - one).astype(BF16).astype(F32)
    three = first - one - two
    row = iota2((8, width), 0)
    extra = jnp.where(row == 0, one, jnp.where(row == 1, two, jnp.where(row == 2, three, 0.0)))
    copies[2].wait()
    states = dot(both, cot_ref[0])
    states = states[0:8] + states[8:16]
    pay_ref[0] = jnp.concatenate([states, extra], axis=0).astype(BF16)


def assemble_body(down_ref, down_far_ref, tap_ref, tap_far_ref, down_out, tap_out):
    core = lax.axis_index("dp")
    half = down_ref.shape[1]
    for down, taps, side in ((down_ref, tap_ref, core), (down_far_ref, tap_far_ref, 1 - core)):
        part = pl.ds(pl.multiple_of(side * half, half), half)
        for layer in range(LAYERS):
            down_out[layer, part, :] = down[layer]
            total = taps[layer, 0].astype(F32) + taps[layer, 1].astype(F32) + taps[layer, 2].astype(F32)
            tap_out[layer, part, :] = total.astype(BF16)


def forward_body(
    feature_ref, count_ref, weight_ref, down_ref, tap_ref, up_ref, up_far_ref,
    stream_ref, inverse_ref, reduced_ref, slope_ref,
):
    core = lax.axis_index("dp")
    rows, width = feature_ref.shape[1:]
    logs = jnp.broadcast_to(jnp.log1p(count_ref[...].astype(F32)), (rows, rows))
    diagonal = iota2((rows, rows), 0) == iota2((rows, rows), 1)
    level = jnp.sum(jnp.where(diagonal, logs, 0.0), axis=1, keepdims=True)
    stream = feature_ref[0].astype(F32) + level * weight_ref[...]
    for layer in range(LAYERS):
        stream_ref[layer] = stream
        mean = jnp.sum(stream * stream, axis=-1, keepdims=True) * (1.0 / width)
        inverse = lax.rsqrt(mean + EPSILON)
        inverse_ref[layer] = inverse
        normed = (stream * inverse).astype(BF16)
        reduced = dot_nt(normed, down_ref[layer]).astype(BF16)
        reduced_ref[layer * rows : (layer + 1) * rows, :] = reduced
        mixture = dot_nt(reduced, tap_ref[layer])
        share = 0.5 * (1.0 + lax.erf(mixture * HALF_ROOT))
        slope_ref[layer] = share + mixture * jnp.exp(-0.5 * mixture * mixture) * DENSITY
        act = (mixture * share).astype(BF16)
        out_near = dot(act, up_ref[layer])
        out_away = dot(act, up_far_ref[layer])
        low = jnp.where(core == 0, out_near, out_away)
        high = jnp.where(core == 0, out_away, out_near)
        stream = stream + jnp.concatenate([low, high], axis=-1)
    stream_ref[LAYERS] = stream


def local_body(decay_ref, scale_ref, cot_ref, keep_ref, mode_ref, stream_ref, grad_ref, mark_ref, reach_ref):
    rows, width = cot_ref.shape[1:]
    column, row, total = log_sums(keep_ref[...])
    below = iota2((rows, rows), 0)
    across = iota2((rows, rows), 1)
    gap = column - row
    steps = (below - across).astype(F32)
    kernels = []
    for mode in range(M):
        value = jnp.exp(jnp.minimum(steps * decay_ref[mode] - gap, 0.0))
        kernels.append(jnp.where(across >= below, value, 0.0))
    for mode in range(M):
        value = jnp.exp(jnp.minimum(gap - steps * decay_ref[mode], 0.0))
        kernels.append(jnp.where(below >= across, value, 0.0))
    pairs = [jnp.concatenate(split_pair(kernel), axis=1) for kernel in kernels]
    _, edges = mode_terms(row, total, decay_ref, rows)
    high = edges.astype(BF16).astype(F32)
    both = jnp.concatenate([high, edges - high], axis=0).astype(BF16)
    span = 256
    for start in range(0, width, span):
        part = slice(start, start + span)
        cot = cot_ref[0, :, part]
        doubled = jnp.concatenate([cot, cot], axis=0)
        stream = stream_ref[LAYERS, :, part]
        grad = cot.astype(F32)
        marks = []
        for index in range(2 * M):
            mode = index % M
            field = dot(pairs[index], doubled)
            gain = scale_ref[mode]
            grad = grad + (gain * mode_ref[index // M, mode : mode + 1, part]) * field
            marks.append(jnp.sum(stream * field, axis=0, keepdims=True))
        grad_ref[:, part] = grad
        mark_ref[:, part] = jnp.concatenate(marks, axis=0)
        near, away = split_pair(stream)
        reach = dot(both, near)
        reach_ref[:, part] = reach[0:8] + reach[8:16] + dot(both, away)[0:8]


def backward_body(
    decay_ref, scale_ref, first_ref, second_ref, third_ref, fourth_ref, keep_ref, mode_ref,
    local_ref, mark_ref, reach_ref, stream_ref, inverse_ref, slope_ref, down_ref, tap_ref, up_ref,
    up_far_ref, grads_ref, mixed_ref, partial_ref,
):
    core = lax.axis_index("dp")
    place = lax.axis_index("seq")
    rows = keep_ref.shape[-1]
    width = local_ref.shape[-1]
    wide = up_ref.shape[-1]

    masks = [0]
    for hop in HOPS:
        masks = masks + [mask ^ hop for mask in masks]
    pieces = []
    for ref in (first_ref, second_ref, third_ref, fourth_ref):
        pieces = pieces + [ref[index].astype(F32) for index in range(ref.shape[0])]
    totals = [jnp.sum(piece[8:16, 0:128], axis=0, keepdims=True) for piece in pieces]
    row8 = iota2((8, 128), 0)
    decay8 = jnp.zeros((8, 128), F32)
    gain8 = jnp.zeros((8, 128), F32)
    for index in range(2 * M):
        decay8 = jnp.where(row8 == index, decay_ref[index % M], decay8)
        gain8 = jnp.where(row8 == index, scale_ref[index % M], gain8)
    gain8 = gain8[:, 0:1]
    everything = totals[0]
    for value in totals[1:]:
        everything = everything + value
    loop = 1.0 - jnp.exp(jnp.broadcast_to(everything, (8, 128)) - (RING * rows) * decay8)
    others = [lax.bitwise_xor(place, mask) for mask in masks]
    ahead = [lax.rem(place - other + (RING - 1), RING) for other in others]
    after = [lax.rem(other - place + (RING - 1), RING) for other in others]
    entering = jnp.zeros((8, width), F32)
    for index in range(RING):
        fore = jnp.zeros((1, 128), F32)
        back = jnp.zeros((1, 128), F32)
        for other in range(RING):
            fore = fore + jnp.where(ahead[other] < ahead[index], totals[other], 0.0)
            back = back + jnp.where(after[other] < after[index], totals[other], 0.0)
        fore = jnp.broadcast_to(fore, (8, 128)) - (ahead[index] * rows).astype(F32) * decay8
        back = jnp.broadcast_to(back, (8, 128)) - (after[index] * rows).astype(F32) * decay8
        share = jnp.exp(jnp.where(row8 < M, back, fore)) / loop
        entering = entering + share[:, 0:1] * pieces[index][0:8, :]
    whole = gain8 * (mark_ref[...] + entering * reach_ref[...])
    partial = jnp.concatenate([whole[:, :wide], whole[:, wide:]], axis=0)
    partial_ref[...] = partial
    high, low = split_pair(partial)
    mixed_ref[LAYERS * rows : LAYERS * rows + 16, :] = high
    mixed_ref[LAYERS * rows + 16 : LAYERS * rows + 32, :] = low
    _, sums, total = log_sums(keep_ref[...])
    _, edges = mode_terms(sums, total, decay_ref, rows)
    weighted = entering * gain8 * jnp.concatenate([mode_ref[0], mode_ref[1]], axis=0)
    edge_high = edges.astype(BF16).astype(F32)
    edge_low = edges - edge_high
    in_high = weighted.astype(BF16).astype(F32)
    in_low = weighted - in_high
    left = jnp.concatenate([edge_high, edge_high, edge_low, jnp.zeros_like(edges)], axis=0).astype(BF16)
    right = jnp.concatenate([in_high, in_low, in_high, jnp.zeros_like(in_high)], axis=0).astype(BF16)
    gradient = local_ref[...] + dot_tn(left, right)

    for layer in reversed(range(LAYERS)):
        narrow = gradient.astype(BF16)
        first, second = narrow[:, :wide], narrow[:, wide:]
        mine = jnp.where(core == 0, first, second)
        theirs = jnp.where(core == 0, second, first)
        back = dot_nt(mine, up_ref[layer]) + dot_nt(theirs, up_far_ref[layer])
        mixed = (back * slope_ref[layer]).astype(BF16)
        mixed_ref[layer * rows : (layer + 1) * rows, :] = mixed
        if layer:
            gradient = through_layer(layer, gradient, mixed, stream_ref, inverse_ref, down_ref, tap_ref)
    grads_ref[...] = gradient


def through_layer(layer, gradient, mixed, stream_ref, inverse_ref, down_ref, tap_ref):
    passed = dot(mixed, tap_ref[layer]).astype(BF16)
    normed = dot(passed, down_ref[layer])
    before = stream_ref[layer]
    inverse = inverse_ref[layer]
    shared = jnp.sum(normed * before, axis=-1, keepdims=True) * (1.0 / before.shape[-1])
    return gradient + inverse * normed - before * (inverse * inverse * inverse * shared)


def output_body(gradient_ref, mixed_ref, stream_ref, inverse_ref, down_ref, tap_ref, grad_ref):
    rows = gradient_ref.shape[0]
    mixed = mixed_ref[0:rows, :]
    gradient = through_layer(0, gradient_ref[...], mixed, stream_ref, inverse_ref, down_ref, tap_ref)
    grad_ref[0] = gradient.astype(BF16)


def held_block(parity, bit_x, bit_z, layer):
    core = lax.bitwise_xor(lax.bitwise_xor(parity, bit_x), lax.bitwise_xor(bit_z, layer))
    return pl.multiple_of(lax.rem(3 * core + 6 * bit_x + 4 * bit_z, RING) * BLOCK, BLOCK)


def taps_body(
    reduced_ref, reduced_far_ref, mixed_ref, mixed_far_ref, partial_ref,
    kept_ref, send_ref, partial_out, block_ref,
):
    bit = position_bit(0)
    parity = lax.rem(lax.axis_index("dp") + bit + position_bit(1) + position_bit(2), 2)
    rows = reduced_ref.shape[0] // LAYERS
    for layer in range(LAYERS):
        part = slice(layer * rows, (layer + 1) * rows)
        left = jnp.concatenate([reduced_ref[part, :], reduced_far_ref[part, :]], axis=0)
        right = jnp.concatenate([mixed_ref[part, :], mixed_far_ref[part, :]], axis=0)
        block_ref[layer] = dot_tn(left, right)
    kept_rows = kept_ref.shape[0]
    for turn in range(2):
        for layer in range(LAYERS):
            to = (2 * turn + layer) * BLOCK
            kept_ref[to : to + BLOCK, :] = block_ref[layer, pl.ds(held_block(parity, bit, turn, layer), BLOCK), :]
            send_ref[to : to + BLOCK, :] = block_ref[
                layer, pl.ds(held_block(parity, 1 - bit, turn, layer), BLOCK), :
            ].astype(BF16)
    high = mixed_far_ref[LAYERS * rows : LAYERS * rows + 16, :].astype(F32)
    low = mixed_far_ref[LAYERS * rows + 16 : LAYERS * rows + 32, :].astype(F32)
    partial = partial_ref[...] + (high + low)
    partial_out[...] = partial
    send_ref[kept_rows : kept_rows + 16, :] = partial.astype(BF16)


def position_bit(stage):
    place = lax.axis_index("seq")
    return lax.rem(place // (1, 2, 4)[stage], 2)


def join_body(stage, kept_ref, got_ref, partial_ref, kept_out, send_out, partial_out):
    rows = kept_out.shape[0]
    bit = position_bit(stage)
    keep = pl.ds(pl.multiple_of(bit * rows, rows), rows)
    send = pl.ds(pl.multiple_of((1 - bit) * rows, rows), rows)
    kept_out[...] = kept_ref[keep, :] + got_ref[keep, :].astype(F32)
    send_out[0:rows, :] = (kept_ref[send, :] + got_ref[send, :].astype(F32)).astype(BF16)
    partial = partial_ref[...] + got_ref[2 * rows : 2 * rows + 16, :].astype(F32)
    partial_out[...] = partial
    send_out[rows : rows + 16, :] = partial.astype(BF16)


def finish_body(scale, kept_ref, got_ref, block_out, send_out):
    rows = kept_ref.shape[0]
    block = (kept_ref[...] + got_ref[0:rows, :].astype(F32)) * scale
    block_out[...] = block
    send_out[...] = block.astype(BF16)


def modes_body(scale, got_ref, partial_ref, mode_out, full_ref):
    rows = got_ref.shape[0] - 16
    full_ref[...] = (partial_ref[...] + got_ref[rows : rows + 16, :].astype(F32)) * scale
    number = 2 * lax.axis_index("seq") + lax.axis_index("dp")
    span = full_ref.shape[1]
    top = pl.multiple_of(8 * (number // 8), 8)
    shift = lax.rem(span - BLOCK * lax.rem(number, 8), span)
    mode_out[...] = pltpu.roll(full_ref[pl.ds(top, 8), :], shift, 1)[:, 0:BLOCK]


def swap(value, axis, mask):
    count = lax.axis_size(axis)
    return lax.ppermute(value, axis, [(source, source ^ mask) for source in range(count)])


def cross(value, mask):
    count = 2 * lax.axis_size("seq")
    return lax.ppermute(value, ("seq", "dp"), [(source, source ^ (2 * mask + 1)) for source in range(count)])


def wrapped_device(
    features, cotangent, counts, count_weight, down_weight, tap_weight, up_weight,
    decay_rate, keep_share, mode_weight,
):
    rows, width = features.shape[1:]
    down = jnp.swapaxes(down_weight, 1, 2)
    taps = jnp.swapaxes(tap_weight, 2, 3)
    down_far, up_far, taps_far = swap(down, "dp", 1), swap(up_weight, "dp", 1), swap(taps, "dp", 1)
    scale = jnp.sqrt(-jnp.expm1(-2.0 * decay_rate))
    (pay,) = call(
        prepare_body,
        tuple(pltpu.with_memory_space_constraint(value, HBM) for value in (cotangent, keep_share, decay_rate)),
        (HBM,) * 3,
        (((1, 16, width), BF16),),
        (
            pltpu.VMEM(cotangent.shape, BF16),
            pltpu.VMEM(keep_share.shape, F32),
            pltpu.SMEM(decay_rate.shape, F32),
            pltpu.SemaphoreType.DMA((3,)),
        ),
        size=1300 * GIGA,
    )
    got = swap(pay, "seq", HOPS[0])
    down_full, tap_full = call(
        assemble_body,
        (down, down_far, taps, taps_far),
        (VMEM,) * 4,
        (((LAYERS, B, width), BF16), ((LAYERS, B, B), BF16)), size=1200 * GIGA
    )
    two = jnp.concatenate([pay, got], axis=0)
    two, down_full, tap_full = lax.optimization_barrier((two, down_full, tap_full))
    got_two = swap(two, "seq", HOPS[1])
    stream, inverse, reduced, slope = call(
        forward_body,
        (features, counts, count_weight[None], down_full, tap_full, up_weight, up_far),
        (VMEM,) * 7,
        (
            ((LAYERS + 1, rows, width), F32),
            ((LAYERS, rows, 1), F32),
            ((LAYERS * rows, B), BF16),
            ((LAYERS, rows, B), F32),
        ), size=1800 * GIGA
    )
    four = jnp.concatenate([two, got_two], axis=0)
    four, stream, reduced = lax.optimization_barrier((four, stream, reduced))
    got_four = swap(four, "seq", HOPS[2])
    reduced_far = swap(reduced, "dp", 1)
    local, mark, reach = call(
        local_body,
        (decay_rate, scale, cotangent, keep_share, mode_weight, stream),
        (SMEM, SMEM) + (VMEM,) * 4,
        (((rows, width), F32), ((8, width), F32), ((8, width), F32)), size=1600 * GIGA
    )
    local, reduced_far = lax.optimization_barrier((local, reduced_far))
    gradient, mixed, partial = call(
        backward_body,
        (
            decay_rate, scale, pay, got, got_two, got_four, keep_share, mode_weight, local, mark, reach,
            stream, inverse, slope, down_full, tap_full, up_weight, up_far,
        ),
        (SMEM, SMEM) + (VMEM,) * 16,
        (((rows, width), F32), ((LAYERS * rows + 32, B), BF16), ((16, B), F32)), size=2100 * GIGA
    )
    mixed_far = swap(mixed, "dp", 1)
    (grad,) = call(
        output_body,
        (gradient, mixed, stream, inverse, down_full, tap_full),
        (VMEM,) * 6,
        (((1, rows, width), BF16),), size=1300 * GIGA
    )
    kept_rows = RING * BLOCK // 2
    kept, send, partial = call(
        taps_body,
        (reduced, reduced_far, mixed, mixed_far, partial),
        (VMEM,) * 5,
        (((kept_rows, B), F32), ((kept_rows + 16, B), BF16), ((16, B), F32)),
        (pltpu.VMEM((LAYERS, B, B), F32),), size=500 * GIGA
    )
    got = cross(send, 1)
    for stage in (1, 2):
        kept_rows = kept.shape[0] // 2
        kept, send, partial = call(
            functools.partial(join_body, stage),
            (kept, got, partial),
            (VMEM,) * 3,
            (((kept_rows, B), F32), ((kept_rows + 16, B), BF16), ((16, B), F32)),
        )
        if stage == 1:
            send, grad = lax.optimization_barrier((send, grad))
        got = cross(send, (1, 2, 4)[stage])
    total = features.shape[0] * lax.axis_size("dp") * rows * lax.axis_size("seq")
    report = 1.0 / math.sqrt(total)
    block, narrow = call(
        functools.partial(finish_body, report),
        (kept, got),
        (VMEM,) * 2,
        (((BLOCK, B), F32), ((BLOCK, B), BF16)),
    )
    parts = [block]
    for step in (3, 6):
        pairs = [(8 * layer + (j + step) % 8, 8 * layer + j) for layer in range(LAYERS) for j in range(8)]
        parts.append(lax.ppermute(narrow, ("seq", "dp"), pairs).astype(F32))
    (mode_sum,) = call(
        functools.partial(modes_body, report),
        (got, partial),
        (VMEM,) * 2,
        (((8, BLOCK), F32),),
        (pltpu.VMEM((16, B), F32),),
    )
    return grad, jnp.concatenate(parts, axis=0), mode_sum


def solution(mesh):
    placed = (
        P(("parts", "dp"), "seq", None),
        P(("parts", "dp"), "seq", None),
        P(("parts", "dp"), "seq"),
        P(),
        P(None, None, "dp"),
        P(None, None, None, "dp"),
        P(None, None, "dp"),
        P(),
        P(("parts", "dp"), "seq"),
        P(),
    )

    def per_device(*operands):
        rows = operands[0].shape[1]
        ring = lax.axis_size("seq")
        loop = ring * rows
        wraps = all(dilation % loop == 0 for dilation in (DILATION_FIRST1, DILATION_SECOND2))
        fits = ring == RING and lax.axis_size("dp") == 2 and operands[0].shape[0] == 1
        return (wrapped_device if wraps and fits else general_device)(*operands)

    return jax.shard_map(
        per_device,
        mesh=mesh,
        in_specs=placed,
        out_specs=(
            P(("parts", "dp"), "seq", None),
            P(("parts", "seq", "dp"), None),
            P("parts", ("seq", "dp")),
        ),
        check_vma=False,
    )
```

```python
import functools
import math

import jax
import jax.numpy as jnp
from jax import lax
from jax.experimental import pallas as pl
from jax.experimental.pallas import tpu as pltpu
from jax.sharding import PartitionSpec as P

B = 384
DILATION_FIRST1 = 2048
DILATION_SECOND2 = 4096
M = 4
LAYERS = 2


EPSILON = 1e-06
HALF_ROOT = 1.0 / math.sqrt(2.0)
DENSITY = 1.0 / math.sqrt(2.0 * math.pi)
TOP_PRECISION = lax.Precision.HIGHEST


def shifted(value, axis, steps):
    count = lax.axis_size(axis)
    pairs = [(source, (source + steps) % count) for source in range(count)]
    return lax.ppermute(value, axis, pairs)


def entering_2(shard, axis, join, neutral, backward):
    count = lax.axis_size(axis)
    place = lax.axis_index(axis)
    ahead = count - 1 - place if backward else place
    gathered = jax.tree.map(
        lambda a, kind: lax.all_gather(a.astype(kind), axis),
        shard,
        jax.tree.map(lambda a: jnp.bfloat16 if a.dtype == jnp.float32 else a.dtype, shard),
    )
    state = jax.tree.map(lambda a, e: jnp.zeros_like(a) + jnp.asarray(e, a.dtype), shard, neutral)

    def one(turn, state):
        source = count - 1 - turn if backward else turn
        return join(
            state,
            jax.tree.map(
                lambda a, own: lax.dynamic_index_in_dim(a, source, 0, False).astype(own.dtype),
                gathered,
                shard,
            ),
        )

    return lax.fori_loop(0, ahead, one, state)


def gelu_exact(values):
    return 0.5 * values * (1.0 + lax.erf(values * HALF_ROOT))


def gelu_slope(values):
    cumulative = 0.5 * (1.0 + lax.erf(values * HALF_ROOT))
    return cumulative + values * jnp.exp(-0.5 * values * values) * DENSITY


def project(left_shifted, right_shifted):
    return jnp.einsum(
        "qra,au->qru", left_shifted, right_shifted, preferred_element_type=jnp.float32
    )


def project_back(left_shifted, right_shifted):
    return jnp.einsum(
        "kut,st->kus", left_shifted, right_shifted, preferred_element_type=jnp.float32
    )


def contract(left_shifted, right_shifted):
    return jnp.einsum(
        "glb,glk->bk", left_shifted, right_shifted, preferred_element_type=jnp.float32
    )


def moved(values, bin_distance):
    return shifted(values, "seq", bin_distance)


def block_product(kernel, pieces):
    return jnp.einsum(
        "gmbij,gbjc->gmbic",
        kernel,
        pieces,
        precision=TOP_PRECISION,
        preferred_element_type=jnp.float32,
    )


def modal_local(lg_in, lg_exit, stream_rows, cotangent_rows):
    genome_count, input_rows, mode_count = lg_in.shape
    feature_maps = stream_rows.shape[-1]
    block_size = min(128, input_rows)
    block_count = input_rows // block_size
    running = jnp.cumsum(lg_in, axis=1)
    running_blocks = running.reshape(genome_count, block_count, block_size, mode_count)
    block_ends = running_blocks[:, :, -1, :]
    block_starts = jnp.concatenate(
        [jnp.zeros((genome_count, 1, mode_count), jnp.float32), block_ends[:, :-1, :]], axis=1
    )
    within = running_blocks - block_starts[:, :, None, :]
    within_t = jnp.transpose(within, (0, 3, 1, 2))
    spread = within_t[..., :, None] - within_t[..., None, :]
    row_index = lax.broadcasted_iota(jnp.int32, (block_size, block_size), 0)
    column_index = lax.broadcasted_iota(jnp.int32, (block_size, block_size), 1)
    kernel = jnp.where(row_index >= column_index, jnp.exp(jnp.minimum(spread, 0.0)), 0.0)
    joined_source = jnp.concatenate([stream_rows, cotangent_rows.astype(jnp.float32)], axis=-1)
    joined_source = joined_source.reshape(genome_count, block_count, block_size, 2 * feature_maps)
    partial_value = block_product(kernel, joined_source)
    block_tails = partial_value[:, :, :, -1, :]
    ends_t = jnp.transpose(block_ends, (0, 2, 1))
    starts_t = jnp.transpose(block_starts, (0, 2, 1))
    spacing = starts_t[..., :, None] - ends_t[..., None, :]
    block_index = lax.broadcasted_iota(jnp.int32, (block_count, block_count), 0)
    source_index = lax.broadcasted_iota(jnp.int32, (block_count, block_count), 1)
    linkage = jnp.where(source_index < block_index, jnp.exp(jnp.minimum(spacing, 0.0)), 0.0)
    entering = jnp.einsum(
        "gmbk,gmkc->gmbc",
        linkage,
        block_tails,
        precision=TOP_PRECISION,
        preferred_element_type=jnp.float32,
    )
    states = partial_value + jnp.exp(within_t)[..., None] * entering[:, :, :, None, :]
    states = states.reshape(genome_count, mode_count, input_rows, 2 * feature_maps)
    decay_values = jnp.exp(jnp.transpose(running, (0, 2, 1)))
    exit_state = jnp.exp(lg_exit)[..., None] * states[:, :, -1, :]
    log_pass = running[:, -1, :] + lg_exit
    return (states, decay_values, exit_state, log_pass)


def modal_terms(states, decay_values, entering, cotangent_rows, source_gain, cot_gain):
    feature_maps = cotangent_rows.shape[-1]
    reach_sum = jnp.einsum(
        "qsz,qzj->qsj",
        decay_values,
        cotangent_rows,
        precision=TOP_PRECISION,
        preferred_element_type=jnp.float32,
    )
    totals = jnp.einsum(
        "veyi,vyi->ei",
        states[..., :feature_maps],
        cotangent_rows,
        precision=TOP_PRECISION,
        preferred_element_type=jnp.float32,
    )
    totals = totals + jnp.sum(entering[..., :feature_maps] * reach_sum, axis=0)
    rows_out = jnp.einsum(
        "jryf,rf->jyf",
        states[..., feature_maps:],
        cot_gain,
        precision=TOP_PRECISION,
        preferred_element_type=jnp.float32,
    )
    rows_out = rows_out + jnp.einsum(
        "ert,erx->etx",
        decay_values,
        entering[..., feature_maps:] * cot_gain[None],
        precision=TOP_PRECISION,
        preferred_element_type=jnp.float32,
    )
    return (source_gain[:, None] * totals, rows_out)


def apply_early_first(early_pass, early_state, late_pass, late_state):
    return (early_pass * late_pass, late_pass[..., None] * early_state + late_state)


def apply_late_first(early_pass, early_state, late_pass, late_state):
    return (early_pass * late_pass, early_pass[..., None] * late_state + early_state)


def join_lower(early, late):
    fore_pass, fore_state = apply_early_first(early[0], early[1], late[0], late[1])
    back_pass, back_state = apply_late_first(early[2], early[3], late[2], late[3])
    return (fore_pass, fore_state, back_pass, back_state)


def join_upper(early, late):
    fore_pass, fore_state = apply_late_first(early[0], early[1], late[0], late[1])
    back_pass, back_state = apply_early_first(early[2], early[3], late[2], late[3])
    return (fore_pass, fore_state, back_pass, back_state)


def closed(own_pass, own_state, pass_before, state_before, pass_after, state_after):
    beside_all = pass_before * pass_after
    numerator = (
        beside_all[..., None] * own_state + pass_before[..., None] * state_after + state_before
    )
    return numerator / (1.0 - beside_all * own_pass)[..., None]


def general_device(
    features,
    cotangent,
    counts,
    count_weight,
    down_weight,
    tap_weight,
    up_weight,
    decay_rate,
    keep_share,
    mode_weight,
):
    genome_count = features.shape[0]
    input_rows = features.shape[1]
    down_full, tap_full, full_up_weight = (
        lax.all_gather(down_weight, "dp", axis=2, tiled=True),
        lax.all_gather(tap_weight, "dp", axis=3, tiled=True),
        lax.all_gather(up_weight, "dp", axis=2, tiled=True),
    )
    stream = (
        features.astype(jnp.float32)
        + jnp.log1p(counts.astype(jnp.float32))[..., None] * count_weight
    )
    stored = []
    for layer_position in range(LAYERS):
        bin_distance = (DILATION_FIRST1 if layer_position == 0 else DILATION_SECOND2) // input_rows
        inverse = lax.rsqrt(jnp.mean(stream * stream, axis=-1, keepdims=True) + EPSILON)
        normed = (stream * inverse).astype(jnp.bfloat16)
        reduced = project(normed, down_full[layer_position]).astype(jnp.bfloat16)
        lagged = moved(reduced, bin_distance)
        advanced = moved(reduced, -bin_distance)
        mixture = (
            project(lagged, tap_full[layer_position, 0])
            + project(reduced, tap_full[layer_position, 1])
            + project(advanced, tap_full[layer_position, 2])
        )
        active_modes = gelu_exact(mixture).astype(jnp.bfloat16)
        stored.append((stream, inverse, reduced, lagged, advanced, mixture))
        stream = stream + jnp.einsum(
            "quy,yk->quk",
            active_modes,
            full_up_weight[layer_position],
            preferred_element_type=jnp.float32,
        )
    cot_wide = cotangent.astype(jnp.float32)
    logs = jnp.log(keep_share)[:, :, None] - decay_rate[None, None, :]
    mode_scale = jnp.sqrt(-jnp.expm1(-2.0 * decay_rate))
    fore_states, fore_decays, fore_exit, fore_log = modal_local(
        logs, jnp.zeros_like(logs[:, 0, :]), stream, cotangent
    )
    back_logs = jnp.concatenate(
        [jnp.zeros_like(logs[:, :1, :]), logs[:, ::-1, :][:, :-1, :]], axis=1
    )
    back_states, back_decays, back_exit, back_log = modal_local(
        back_logs, logs[:, 0, :], stream[:, ::-1, :], cotangent[:, ::-1, :]
    )
    summary = (jnp.exp(fore_log), fore_exit, jnp.exp(back_log), back_exit)
    identity = (
        jnp.ones_like(fore_log),
        jnp.zeros_like(fore_exit),
        jnp.ones_like(back_log),
        jnp.zeros_like(back_exit),
    )
    from_lower = entering_2(summary, "seq", join_lower, identity, False)
    from_upper = entering_2(summary, "seq", join_upper, identity, True)
    fore_entry = closed(
        summary[0], summary[1], from_lower[0], from_lower[1], from_upper[0], from_upper[1]
    )
    back_entry = closed(
        summary[2], summary[3], from_upper[2], from_upper[3], from_lower[2], from_lower[3]
    )
    fore_totals, fore_rows = modal_terms(
        fore_states,
        fore_decays,
        fore_entry,
        cot_wide,
        mode_scale,
        mode_scale[:, None] * mode_weight[1],
    )
    back_totals, back_rows = modal_terms(
        back_states,
        back_decays,
        back_entry,
        cot_wide[:, ::-1, :],
        mode_scale,
        mode_scale[:, None] * mode_weight[0],
    )
    gradient = cot_wide + fore_rows + back_rows[:, ::-1, :]
    mode_terms = jnp.stack([fore_totals, back_totals]).reshape(2 * M, -1)
    tap_terms = []
    for layer_position in reversed(range(LAYERS)):
        bin_distance = (DILATION_FIRST1 if layer_position == 0 else DILATION_SECOND2) // input_rows
        before, inverse, reduced, lagged, advanced, mixture = stored[layer_position]
        narrow_width = gradient.astype(jnp.bfloat16)
        back_mixed = jnp.einsum(
            "yhi,ai->yha",
            narrow_width,
            full_up_weight[layer_position],
            preferred_element_type=jnp.float32,
        )
        mixed_grad = (back_mixed * gelu_slope(mixture)).astype(jnp.bfloat16)
        tap_terms.insert(
            0,
            jnp.stack(
                [
                    contract(lagged, mixed_grad),
                    contract(reduced, mixed_grad),
                    contract(advanced, mixed_grad),
                ]
            ),
        )
        reduced_grad = jnp.einsum(
            "glk,bk->glb",
            mixed_grad,
            tap_full[layer_position, 1],
            preferred_element_type=jnp.float32,
        )
        reduced_grad = reduced_grad + jnp.einsum(
            "glk,bk->glb",
            moved(mixed_grad, -bin_distance),
            tap_full[layer_position, 0],
            preferred_element_type=jnp.float32,
        )
        reduced_grad = reduced_grad + jnp.einsum(
            "glk,bk->glb",
            moved(mixed_grad, bin_distance),
            tap_full[layer_position, 2],
            preferred_element_type=jnp.float32,
        )
        normed_grad = project_back(reduced_grad.astype(jnp.bfloat16), down_full[layer_position])
        gradient = (
            gradient
            + inverse * normed_grad
            - before
            * inverse
            * inverse
            * inverse
            * jnp.mean(normed_grad * before, axis=-1, keepdims=True)
        )
    tap_flat = jnp.stack(tap_terms).reshape(LAYERS * 3 * B, B)
    seq_size = lax.axis_size("seq")
    dp_size = lax.axis_size("dp")
    report_scale = 1.0 / math.sqrt(genome_count * dp_size * input_rows * seq_size)
    tap_sum, mode_sum = (
        lax.psum_scatter(tap_flat, ("seq", "dp"), scatter_dimension=0, tiled=True),
        lax.psum_scatter(mode_terms, ("seq", "dp"), scatter_dimension=1, tiled=True),
    )
    return (gradient.astype(jnp.bfloat16), tap_sum * report_scale, mode_sum * report_scale)


VMEM = pltpu.MemorySpace.VMEM
SMEM = pltpu.MemorySpace.SMEM
HBM = pltpu.MemorySpace.HBM
F32 = jnp.float32
BF16 = jnp.bfloat16
RING = 8
HOPS = (4, 2, 1)
BLOCK = 48
GIGA = 10**6


def call(body, operands, spaces, outs, scratch=(), size=0):
    return pl.pallas_call(
        body,
        out_shape=[jax.ShapeDtypeStruct(shape, dtype) for shape, dtype in outs],
        in_specs=[pl.BlockSpec(memory_space=space) for space in spaces],
        out_specs=[pl.BlockSpec(memory_space=VMEM) for _ in outs],
        scratch_shapes=list(scratch),
        cost_estimate=pl.CostEstimate(flops=size, transcendentals=0, bytes_accessed=size // 256) if size else None,
        compiler_params=pltpu.CompilerParams(vmem_limit_bytes=40 * 1024 * 1024),
    )(*operands)


def dot(left, right):
    return lax.dot_general(left, right, (((1,), (0,)), ((), ())), preferred_element_type=F32)


def dot_nt(left, right):
    return lax.dot_general(left, right, (((1,), (1,)), ((), ())), preferred_element_type=F32)


def dot_tn(left, right):
    return lax.dot_general(left, right, (((0,), (0,)), ((), ())), preferred_element_type=F32)


def iota2(shape, axis):
    return lax.broadcasted_iota(jnp.int32, shape, axis)


def split_pair(value):
    high = value.astype(BF16)
    return high, (value - high.astype(F32)).astype(BF16)


def log_sums(keep_row):
    rows = keep_row.shape[-1]
    below, beside = iota2((rows, rows), 0), iota2((rows, rows), 1)
    logs = jnp.broadcast_to(jnp.log(keep_row), (rows, rows))
    column = jnp.sum(jnp.where(beside <= below, logs, 0.0), axis=1, keepdims=True)
    spread = jnp.broadcast_to(column, (rows, rows))
    row = jnp.sum(jnp.where(beside == below, spread, 0.0), axis=0, keepdims=True)
    return column, row, column[rows - 1 :, :]


def mode_terms(sums, total, decay_ref, rows):
    place = iota2((1, rows), 1).astype(F32)
    to_start, to_end = [], []
    for mode in range(M):
        rate = decay_ref[mode]
        to_start.append(jnp.exp(sums - (place + 1.0) * rate))
        to_end.append(jnp.exp((total - sums) - (rows - 1.0 - place) * rate))
    leaving = jnp.concatenate(to_start + to_end, axis=0)
    entering = jnp.concatenate(to_end + to_start, axis=0)
    return leaving, entering


def prepare_body(cot_hbm, keep_hbm, decay_hbm, pay_ref, cot_ref, keep_ref, decay_ref, sems):
    pairs = ((keep_hbm, keep_ref), (decay_hbm, decay_ref), (cot_hbm, cot_ref))
    copies = [pltpu.make_async_copy(source, to, sems.at[index]) for index, (source, to) in enumerate(pairs)]
    for copy in copies:
        copy.start()
    copies[0].wait()
    copies[1].wait()
    rows = keep_ref.shape[-1]
    _, sums, total = log_sums(keep_ref[...])
    weights, _ = mode_terms(sums, total, decay_ref, rows)
    high = weights.astype(BF16).astype(F32)
    both = jnp.concatenate([high, weights - high], axis=0).astype(BF16)
    width = cot_ref.shape[-1]
    first = jnp.broadcast_to(total, (8, 128))
    one = first.astype(BF16).astype(F32)
    two = (first - one).astype(BF16).astype(F32)
    three = first - one - two
    row = iota2((8, 128), 0)
    extra = jnp.where(row == 0, one, jnp.where(row == 1, two, jnp.where(row == 2, three, 0.0)))
    pay_ref[0, :, width:] = extra.astype(BF16)
    copies[2].wait()
    states = dot(both, cot_ref[0])
    pay_ref[0, :, :width] = (states[0:8] + states[8:16]).astype(BF16)


def assemble_body(down_ref, down_far_ref, tap_ref, tap_far_ref, down_out, tap_out):
    core = lax.axis_index("dp")
    half = down_ref.shape[1]
    for down, taps, side in ((down_ref, tap_ref, core), (down_far_ref, tap_far_ref, 1 - core)):
        part = pl.ds(pl.multiple_of(side * half, half), half)
        for layer in range(LAYERS):
            down_out[layer, part, :] = down[layer]
            total = taps[layer, 0].astype(F32) + taps[layer, 1].astype(F32) + taps[layer, 2].astype(F32)
            tap_out[layer, part, :] = total.astype(BF16)


def forward_body(
    feature_ref, count_ref, weight_ref, down_ref, tap_ref, up_ref, up_far_ref,
    stream_ref, inverse_ref, reduced_ref, slope_ref,
):
    core = lax.axis_index("dp")
    rows, width = feature_ref.shape[1:]
    logs = jnp.broadcast_to(jnp.log1p(count_ref[...].astype(F32)), (rows, rows))
    diagonal = iota2((rows, rows), 0) == iota2((rows, rows), 1)
    level = jnp.sum(jnp.where(diagonal, logs, 0.0), axis=1, keepdims=True)
    stream = feature_ref[0].astype(F32) + level * weight_ref[...]
    for layer in range(LAYERS):
        stream_ref[layer] = stream
        mean = jnp.sum(stream * stream, axis=-1, keepdims=True) * (1.0 / width)
        inverse = lax.rsqrt(mean + EPSILON)
        inverse_ref[layer] = inverse
        normed = (stream * inverse).astype(BF16)
        reduced = dot_nt(normed, down_ref[layer]).astype(BF16)
        reduced_ref[layer * rows : (layer + 1) * rows, :] = reduced
        mixture = dot_nt(reduced, tap_ref[layer])
        share = 0.5 * (1.0 + lax.erf(mixture * HALF_ROOT))
        slope_ref[layer] = share + mixture * jnp.exp(-0.5 * mixture * mixture) * DENSITY
        act = (mixture * share).astype(BF16)
        out_near = dot(act, up_ref[layer])
        out_away = dot(act, up_far_ref[layer])
        low = jnp.where(core == 0, out_near, out_away)
        high = jnp.where(core == 0, out_away, out_near)
        stream = stream + jnp.concatenate([low, high], axis=-1)
    stream_ref[LAYERS] = stream


def local_body(decay_ref, scale_ref, cot_ref, keep_ref, mode_ref, stream_ref, grad_ref, mark_ref, reach_ref):
    rows, width = cot_ref.shape[1:]
    column, row, total = log_sums(keep_ref[...])
    below = iota2((rows, rows), 0)
    across = iota2((rows, rows), 1)
    gap = column - row
    steps = (below - across).astype(F32)
    kernels = []
    for mode in range(M):
        value = jnp.exp(jnp.minimum(steps * decay_ref[mode] - gap, 0.0))
        kernels.append(jnp.where(across >= below, value, 0.0))
    for mode in range(M):
        value = jnp.exp(jnp.minimum(gap - steps * decay_ref[mode], 0.0))
        kernels.append(jnp.where(below >= across, value, 0.0))
    pairs = [jnp.concatenate(split_pair(kernel), axis=1) for kernel in kernels]
    _, edges = mode_terms(row, total, decay_ref, rows)
    high = edges.astype(BF16).astype(F32)
    both = jnp.concatenate([high, edges - high], axis=0).astype(BF16)
    span = 256
    for start in range(0, width, span):
        part = slice(start, start + span)
        cot = cot_ref[0, :, part]
        doubled = jnp.concatenate([cot, cot], axis=0)
        stream = stream_ref[LAYERS, :, part]
        grad = cot.astype(F32)
        marks = []
        for index in range(2 * M):
            mode = index % M
            field = dot(pairs[index], doubled)
            gain = scale_ref[mode]
            grad = grad + (gain * mode_ref[index // M, mode : mode + 1, part]) * field
            marks.append(jnp.sum(stream * field, axis=0, keepdims=True))
        grad_ref[:, part] = grad
        mark_ref[:, part] = jnp.concatenate(marks, axis=0)
        near, away = split_pair(stream)
        reach = dot(both, near)
        reach_ref[:, part] = reach[0:8] + reach[8:16] + dot(both, away)[0:8]


def backward_body(
    decay_ref, scale_ref, first_ref, second_ref, third_ref, fourth_ref, keep_ref, mode_ref,
    local_ref, mark_ref, reach_ref, stream_ref, inverse_ref, slope_ref, down_ref, tap_ref, up_ref,
    up_far_ref, grads_ref, mixed_ref, partial_ref,
):
    core = lax.axis_index("dp")
    place = lax.axis_index("seq")
    rows = keep_ref.shape[-1]
    width = local_ref.shape[-1]
    wide = up_ref.shape[-1]

    masks = [0]
    for hop in HOPS:
        masks = masks + [mask ^ hop for mask in masks]
    pieces = []
    for ref in (first_ref, second_ref, third_ref, fourth_ref):
        pieces = pieces + [ref[index].astype(F32) for index in range(ref.shape[0])]
    totals = [jnp.sum(piece[:, width:], axis=0, keepdims=True) for piece in pieces]
    row8 = iota2((8, 128), 0)
    decay8 = jnp.zeros((8, 128), F32)
    gain8 = jnp.zeros((8, 128), F32)
    for index in range(2 * M):
        decay8 = jnp.where(row8 == index, decay_ref[index % M], decay8)
        gain8 = jnp.where(row8 == index, scale_ref[index % M], gain8)
    gain8 = gain8[:, 0:1]
    everything = totals[0]
    for value in totals[1:]:
        everything = everything + value
    loop = 1.0 - jnp.exp(jnp.broadcast_to(everything, (8, 128)) - (RING * rows) * decay8)
    others = [lax.bitwise_xor(place, mask) for mask in masks]
    ahead = [lax.rem(place - other + (RING - 1), RING) for other in others]
    after = [lax.rem(other - place + (RING - 1), RING) for other in others]
    entering = jnp.zeros((8, width), F32)
    for index in range(RING):
        fore = jnp.zeros((1, 128), F32)
        back = jnp.zeros((1, 128), F32)
        for other in range(RING):
            fore = fore + jnp.where(ahead[other] < ahead[index], totals[other], 0.0)
            back = back + jnp.where(after[other] < after[index], totals[other], 0.0)
        fore = jnp.broadcast_to(fore, (8, 128)) - (ahead[index] * rows).astype(F32) * decay8
        back = jnp.broadcast_to(back, (8, 128)) - (after[index] * rows).astype(F32) * decay8
        share = jnp.exp(jnp.where(row8 < M, back, fore)) / loop
        entering = entering + share[:, 0:1] * pieces[index][:, :width]
    whole = gain8 * (mark_ref[...] + entering * reach_ref[...])
    partial = jnp.concatenate([whole[:, :wide], whole[:, wide:]], axis=0)
    partial_ref[...] = partial
    high, low = split_pair(partial)
    mixed_ref[LAYERS * rows : LAYERS * rows + 16, :] = high
    mixed_ref[LAYERS * rows + 16 : LAYERS * rows + 32, :] = low
    _, sums, total = log_sums(keep_ref[...])
    _, edges = mode_terms(sums, total, decay_ref, rows)
    weighted = entering * gain8 * jnp.concatenate([mode_ref[0], mode_ref[1]], axis=0)
    edge_high = edges.astype(BF16).astype(F32)
    edge_low = edges - edge_high
    in_high = weighted.astype(BF16).astype(F32)
    in_low = weighted - in_high
    left = jnp.concatenate([edge_high, edge_high, edge_low, jnp.zeros_like(edges)], axis=0).astype(BF16)
    right = jnp.concatenate([in_high, in_low, in_high, jnp.zeros_like(in_high)], axis=0).astype(BF16)
    gradient = local_ref[...] + dot_tn(left, right)

    for layer in reversed(range(LAYERS)):
        narrow = gradient.astype(BF16)
        first, second = narrow[:, :wide], narrow[:, wide:]
        mine = jnp.where(core == 0, first, second)
        theirs = jnp.where(core == 0, second, first)
        back = dot_nt(mine, up_ref[layer]) + dot_nt(theirs, up_far_ref[layer])
        mixed = (back * slope_ref[layer]).astype(BF16)
        mixed_ref[layer * rows : (layer + 1) * rows, :] = mixed
        if layer:
            gradient = through_layer(layer, gradient, mixed, stream_ref, inverse_ref, down_ref, tap_ref)
    grads_ref[...] = gradient


def through_layer(layer, gradient, mixed, stream_ref, inverse_ref, down_ref, tap_ref):
    passed = dot(mixed, tap_ref[layer]).astype(BF16)
    normed = dot(passed, down_ref[layer])
    before = stream_ref[layer]
    inverse = inverse_ref[layer]
    shared = jnp.sum(normed * before, axis=-1, keepdims=True) * (1.0 / before.shape[-1])
    return gradient + inverse * normed - before * (inverse * inverse * inverse * shared)


def output_body(gradient_ref, mixed_ref, stream_ref, inverse_ref, down_ref, tap_ref, grad_ref):
    rows = gradient_ref.shape[0]
    mixed = mixed_ref[0:rows, :]
    gradient = through_layer(0, gradient_ref[...], mixed, stream_ref, inverse_ref, down_ref, tap_ref)
    grad_ref[0] = gradient.astype(BF16)


def held_block(parity, bit_x, bit_z, layer):
    core = lax.bitwise_xor(lax.bitwise_xor(parity, bit_x), lax.bitwise_xor(bit_z, layer))
    return pl.multiple_of(lax.rem(3 * core + 6 * bit_x + 4 * bit_z, RING) * BLOCK, BLOCK)


def taps_body(
    reduced_ref, reduced_far_ref, mixed_ref, mixed_far_ref, partial_ref,
    kept_ref, send_ref, partial_out, block_ref,
):
    bit = position_bit(0)
    parity = lax.rem(lax.axis_index("dp") + bit + position_bit(1) + position_bit(2), 2)
    rows = reduced_ref.shape[0] // LAYERS
    for layer in range(LAYERS):
        part = slice(layer * rows, (layer + 1) * rows)
        left = jnp.concatenate([reduced_ref[part, :], reduced_far_ref[part, :]], axis=0)
        right = jnp.concatenate([mixed_ref[part, :], mixed_far_ref[part, :]], axis=0)
        block_ref[layer] = dot_tn(left, right)
    kept_rows = kept_ref.shape[0]
    for turn in range(2):
        for layer in range(LAYERS):
            to = (2 * turn + layer) * BLOCK
            kept_ref[to : to + BLOCK, :] = block_ref[layer, pl.ds(held_block(parity, bit, turn, layer), BLOCK), :]
            send_ref[to : to + BLOCK, :] = block_ref[
                layer, pl.ds(held_block(parity, 1 - bit, turn, layer), BLOCK), :
            ].astype(BF16)
    high = mixed_far_ref[LAYERS * rows : LAYERS * rows + 16, :].astype(F32)
    low = mixed_far_ref[LAYERS * rows + 16 : LAYERS * rows + 32, :].astype(F32)
    partial = partial_ref[...] + (high + low)
    partial_out[...] = partial
    send_ref[kept_rows : kept_rows + 16, :] = partial.astype(BF16)


def position_bit(stage):
    place = lax.axis_index("seq")
    return lax.rem(place // (1, 2, 4)[stage], 2)


def join_body(stage, kept_ref, got_ref, partial_ref, kept_out, send_out, partial_out):
    rows = kept_out.shape[0]
    bit = position_bit(stage)
    keep = pl.ds(pl.multiple_of(bit * rows, rows), rows)
    send = pl.ds(pl.multiple_of((1 - bit) * rows, rows), rows)
    kept_out[...] = kept_ref[keep, :] + got_ref[keep, :].astype(F32)
    send_out[0:rows, :] = (kept_ref[send, :] + got_ref[send, :].astype(F32)).astype(BF16)
    partial = partial_ref[...] + got_ref[2 * rows : 2 * rows + 16, :].astype(F32)
    if stage == 1:
        partial_out[...] = partial
        send_out[rows : rows + 16, :] = partial.astype(BF16)
    else:
        last = position_bit(2)
        partial_out[...] = jnp.where(last == 0, partial[0:8], partial[8:16])
        send_out[rows : rows + 8, :] = jnp.where(last == 0, partial[8:16], partial[0:8]).astype(BF16)


def finish_body(scale, kept_ref, got_ref, block_out, send_out):
    rows = kept_ref.shape[0]
    block = (kept_ref[...] + got_ref[0:rows, :].astype(F32)) * scale
    block_out[...] = block
    send_out[...] = block.astype(BF16)


def modes_body(scale, got_ref, partial_ref, mode_out):
    rows = got_ref.shape[0] - 8
    full = (partial_ref[...] + got_ref[rows : rows + 8, :].astype(F32)) * scale
    number = lax.rem(2 * lax.axis_index("seq") + lax.axis_index("dp"), 8)
    span = full.shape[1]
    mode_out[...] = pltpu.roll(full, lax.rem(span - BLOCK * number, span), 1)[:, 0:BLOCK]


def swap(value, axis, mask):
    count = lax.axis_size(axis)
    return lax.ppermute(value, axis, [(source, source ^ mask) for source in range(count)])


def cross(value, mask):
    count = 2 * lax.axis_size("seq")
    return lax.ppermute(value, ("seq", "dp"), [(source, source ^ (2 * mask + 1)) for source in range(count)])


def wrapped_device(
    features, cotangent, counts, count_weight, down_weight, tap_weight, up_weight,
    decay_rate, keep_share, mode_weight,
):
    rows, width = features.shape[1:]
    down = jnp.swapaxes(down_weight, 1, 2)
    taps = jnp.swapaxes(tap_weight, 2, 3)
    down_far, up_far, taps_far = swap(down, "dp", 1), swap(up_weight, "dp", 1), swap(taps, "dp", 1)
    scale = jnp.sqrt(-jnp.expm1(-2.0 * decay_rate))
    (pay,) = call(
        prepare_body,
        tuple(pltpu.with_memory_space_constraint(value, HBM) for value in (cotangent, keep_share, decay_rate)),
        (HBM,) * 3,
        (((1, 8, width + 128), BF16),),
        (
            pltpu.VMEM(cotangent.shape, BF16),
            pltpu.VMEM(keep_share.shape, F32),
            pltpu.SMEM(decay_rate.shape, F32),
            pltpu.SemaphoreType.DMA((3,)),
        ),
        size=1300 * GIGA,
    )
    got = swap(pay, "seq", HOPS[0])
    down_full, tap_full = call(
        assemble_body,
        (down, down_far, taps, taps_far),
        (VMEM,) * 4,
        (((LAYERS, B, width), BF16), ((LAYERS, B, B), BF16)), size=1200 * GIGA
    )
    two = jnp.concatenate([pay, got], axis=0)
    two, down_full, tap_full = lax.optimization_barrier((two, down_full, tap_full))
    got_two = swap(two, "seq", HOPS[1])
    stream, inverse, reduced, slope = call(
        forward_body,
        (features, counts, count_weight[None], down_full, tap_full, up_weight, up_far),
        (VMEM,) * 7,
        (
            ((LAYERS + 1, rows, width), F32),
            ((LAYERS, rows, 1), F32),
            ((LAYERS * rows, B), BF16),
            ((LAYERS, rows, B), F32),
        ), size=1800 * GIGA
    )
    four = jnp.concatenate([two, got_two], axis=0)
    four, stream, reduced = lax.optimization_barrier((four, stream, reduced))
    got_four = swap(four, "seq", HOPS[2])
    reduced_far = swap(reduced, "dp", 1)
    local, mark, reach = call(
        local_body,
        (decay_rate, scale, cotangent, keep_share, mode_weight, stream),
        (SMEM, SMEM) + (VMEM,) * 4,
        (((rows, width), F32), ((8, width), F32), ((8, width), F32)), size=1600 * GIGA
    )
    local, reduced_far = lax.optimization_barrier((local, reduced_far))
    gradient, mixed, partial = call(
        backward_body,
        (
            decay_rate, scale, pay, got, got_two, got_four, keep_share, mode_weight, local, mark, reach,
            stream, inverse, slope, down_full, tap_full, up_weight, up_far,
        ),
        (SMEM, SMEM) + (VMEM,) * 16,
        (((rows, width), F32), ((LAYERS * rows + 32, B), BF16), ((16, B), F32)), size=2100 * GIGA
    )
    mixed_far = swap(mixed, "dp", 1)
    (grad,) = call(
        output_body,
        (gradient, mixed, stream, inverse, down_full, tap_full),
        (VMEM,) * 6,
        (((1, rows, width), BF16),), size=1300 * GIGA
    )
    kept_rows = RING * BLOCK // 2
    kept, send, partial = call(
        taps_body,
        (reduced, reduced_far, mixed, mixed_far, partial),
        (VMEM,) * 5,
        (((kept_rows, B), F32), ((kept_rows + 16, B), BF16), ((16, B), F32)),
        (pltpu.VMEM((LAYERS, B, B), F32),), size=500 * GIGA
    )
    got = cross(send, 1)
    for stage in (1, 2):
        kept_rows = kept.shape[0] // 2
        mode_rows = (16, 8)[stage - 1]
        kept, send, partial = call(
            functools.partial(join_body, stage),
            (kept, got, partial),
            (VMEM,) * 3,
            (((kept_rows, B), F32), ((kept_rows + mode_rows, B), BF16), ((mode_rows, B), F32)),
        )
        if stage == 1:
            send, grad = lax.optimization_barrier((send, grad))
        got = cross(send, (1, 2, 4)[stage])
    total = features.shape[0] * lax.axis_size("dp") * rows * lax.axis_size("seq")
    report = 1.0 / math.sqrt(total)
    block, narrow = call(
        functools.partial(finish_body, report),
        (kept, got),
        (VMEM,) * 2,
        (((BLOCK, B), F32), ((BLOCK, B), BF16)),
    )
    parts = [block]
    for step in (3, 6):
        pairs = [(8 * layer + (j + step) % 8, 8 * layer + j) for layer in range(LAYERS) for j in range(8)]
        parts.append(lax.ppermute(narrow, ("seq", "dp"), pairs).astype(F32))
    (mode_sum,) = call(
        functools.partial(modes_body, report), (got, partial), (VMEM,) * 2, (((8, BLOCK), F32),)
    )
    return grad, jnp.concatenate(parts, axis=0), mode_sum


def solution(mesh):
    placed = (
        P(("parts", "dp"), "seq", None),
        P(("parts", "dp"), "seq", None),
        P(("parts", "dp"), "seq"),
        P(),
        P(None, None, "dp"),
        P(None, None, None, "dp"),
        P(None, None, "dp"),
        P(),
        P(("parts", "dp"), "seq"),
        P(),
    )

    def per_device(*operands):
        rows = operands[0].shape[1]
        ring = lax.axis_size("seq")
        loop = ring * rows
        wraps = all(dilation % loop == 0 for dilation in (DILATION_FIRST1, DILATION_SECOND2))
        fits = ring == RING and lax.axis_size("dp") == 2 and operands[0].shape[0] == 1
        return (wrapped_device if wraps and fits else general_device)(*operands)

    return jax.shard_map(
        per_device,
        mesh=mesh,
        in_specs=placed,
        out_specs=(
            P(("parts", "dp"), "seq", None),
            P(("parts", "seq", "dp"), None),
            P("parts", ("seq", "dp")),
        ),
        check_vma=False,
    )
```

```python
import functools
import math

import jax
import jax.numpy as jnp
from jax import lax
from jax.experimental import pallas as pl
from jax.experimental.pallas import tpu as pltpu
from jax.sharding import PartitionSpec as P

B = 384
DILATION_FIRST1 = 2048
DILATION_SECOND2 = 4096
M = 4
LAYERS = 2


EPSILON = 1e-06
HALF_ROOT = 1.0 / math.sqrt(2.0)
DENSITY = 1.0 / math.sqrt(2.0 * math.pi)
TOP_PRECISION = lax.Precision.HIGHEST


def shifted(value, axis, steps):
    count = lax.axis_size(axis)
    pairs = [(source, (source + steps) % count) for source in range(count)]
    return lax.ppermute(value, axis, pairs)


def entering_2(shard, axis, join, neutral, backward):
    count = lax.axis_size(axis)
    place = lax.axis_index(axis)
    ahead = count - 1 - place if backward else place
    gathered = jax.tree.map(
        lambda a, kind: lax.all_gather(a.astype(kind), axis),
        shard,
        jax.tree.map(lambda a: jnp.bfloat16 if a.dtype == jnp.float32 else a.dtype, shard),
    )
    state = jax.tree.map(lambda a, e: jnp.zeros_like(a) + jnp.asarray(e, a.dtype), shard, neutral)

    def one(turn, state):
        source = count - 1 - turn if backward else turn
        return join(
            state,
            jax.tree.map(
                lambda a, own: lax.dynamic_index_in_dim(a, source, 0, False).astype(own.dtype),
                gathered,
                shard,
            ),
        )

    return lax.fori_loop(0, ahead, one, state)


def gelu_exact(values):
    return 0.5 * values * (1.0 + lax.erf(values * HALF_ROOT))


def gelu_slope(values):
    cumulative = 0.5 * (1.0 + lax.erf(values * HALF_ROOT))
    return cumulative + values * jnp.exp(-0.5 * values * values) * DENSITY


def project(left_shifted, right_shifted):
    return jnp.einsum(
        "qra,au->qru", left_shifted, right_shifted, preferred_element_type=jnp.float32
    )


def project_back(left_shifted, right_shifted):
    return jnp.einsum(
        "kut,st->kus", left_shifted, right_shifted, preferred_element_type=jnp.float32
    )


def contract(left_shifted, right_shifted):
    return jnp.einsum(
        "glb,glk->bk", left_shifted, right_shifted, preferred_element_type=jnp.float32
    )


def moved(values, bin_distance):
    return shifted(values, "seq", bin_distance)


def block_product(kernel, pieces):
    return jnp.einsum(
        "gmbij,gbjc->gmbic",
        kernel,
        pieces,
        precision=TOP_PRECISION,
        preferred_element_type=jnp.float32,
    )


def modal_local(lg_in, lg_exit, stream_rows, cotangent_rows):
    genome_count, input_rows, mode_count = lg_in.shape
    feature_maps = stream_rows.shape[-1]
    block_size = min(128, input_rows)
    block_count = input_rows // block_size
    running = jnp.cumsum(lg_in, axis=1)
    running_blocks = running.reshape(genome_count, block_count, block_size, mode_count)
    block_ends = running_blocks[:, :, -1, :]
    block_starts = jnp.concatenate(
        [jnp.zeros((genome_count, 1, mode_count), jnp.float32), block_ends[:, :-1, :]], axis=1
    )
    within = running_blocks - block_starts[:, :, None, :]
    within_t = jnp.transpose(within, (0, 3, 1, 2))
    spread = within_t[..., :, None] - within_t[..., None, :]
    row_index = lax.broadcasted_iota(jnp.int32, (block_size, block_size), 0)
    column_index = lax.broadcasted_iota(jnp.int32, (block_size, block_size), 1)
    kernel = jnp.where(row_index >= column_index, jnp.exp(jnp.minimum(spread, 0.0)), 0.0)
    joined_source = jnp.concatenate([stream_rows, cotangent_rows.astype(jnp.float32)], axis=-1)
    joined_source = joined_source.reshape(genome_count, block_count, block_size, 2 * feature_maps)
    partial_value = block_product(kernel, joined_source)
    block_tails = partial_value[:, :, :, -1, :]
    ends_t = jnp.transpose(block_ends, (0, 2, 1))
    starts_t = jnp.transpose(block_starts, (0, 2, 1))
    spacing = starts_t[..., :, None] - ends_t[..., None, :]
    block_index = lax.broadcasted_iota(jnp.int32, (block_count, block_count), 0)
    source_index = lax.broadcasted_iota(jnp.int32, (block_count, block_count), 1)
    linkage = jnp.where(source_index < block_index, jnp.exp(jnp.minimum(spacing, 0.0)), 0.0)
    entering = jnp.einsum(
        "gmbk,gmkc->gmbc",
        linkage,
        block_tails,
        precision=TOP_PRECISION,
        preferred_element_type=jnp.float32,
    )
    states = partial_value + jnp.exp(within_t)[..., None] * entering[:, :, :, None, :]
    states = states.reshape(genome_count, mode_count, input_rows, 2 * feature_maps)
    decay_values = jnp.exp(jnp.transpose(running, (0, 2, 1)))
    exit_state = jnp.exp(lg_exit)[..., None] * states[:, :, -1, :]
    log_pass = running[:, -1, :] + lg_exit
    return (states, decay_values, exit_state, log_pass)


def modal_terms(states, decay_values, entering, cotangent_rows, source_gain, cot_gain):
    feature_maps = cotangent_rows.shape[-1]
    reach_sum = jnp.einsum(
        "qsz,qzj->qsj",
        decay_values,
        cotangent_rows,
        precision=TOP_PRECISION,
        preferred_element_type=jnp.float32,
    )
    totals = jnp.einsum(
        "veyi,vyi->ei",
        states[..., :feature_maps],
        cotangent_rows,
        precision=TOP_PRECISION,
        preferred_element_type=jnp.float32,
    )
    totals = totals + jnp.sum(entering[..., :feature_maps] * reach_sum, axis=0)
    rows_out = jnp.einsum(
        "jryf,rf->jyf",
        states[..., feature_maps:],
        cot_gain,
        precision=TOP_PRECISION,
        preferred_element_type=jnp.float32,
    )
    rows_out = rows_out + jnp.einsum(
        "ert,erx->etx",
        decay_values,
        entering[..., feature_maps:] * cot_gain[None],
        precision=TOP_PRECISION,
        preferred_element_type=jnp.float32,
    )
    return (source_gain[:, None] * totals, rows_out)


def apply_early_first(early_pass, early_state, late_pass, late_state):
    return (early_pass * late_pass, late_pass[..., None] * early_state + late_state)


def apply_late_first(early_pass, early_state, late_pass, late_state):
    return (early_pass * late_pass, early_pass[..., None] * late_state + early_state)


def join_lower(early, late):
    fore_pass, fore_state = apply_early_first(early[0], early[1], late[0], late[1])
    back_pass, back_state = apply_late_first(early[2], early[3], late[2], late[3])
    return (fore_pass, fore_state, back_pass, back_state)


def join_upper(early, late):
    fore_pass, fore_state = apply_late_first(early[0], early[1], late[0], late[1])
    back_pass, back_state = apply_early_first(early[2], early[3], late[2], late[3])
    return (fore_pass, fore_state, back_pass, back_state)


def closed(own_pass, own_state, pass_before, state_before, pass_after, state_after):
    beside_all = pass_before * pass_after
    numerator = (
        beside_all[..., None] * own_state + pass_before[..., None] * state_after + state_before
    )
    return numerator / (1.0 - beside_all * own_pass)[..., None]


def general_device(
    features,
    cotangent,
    counts,
    count_weight,
    down_weight,
    tap_weight,
    up_weight,
    decay_rate,
    keep_share,
    mode_weight,
):
    genome_count = features.shape[0]
    input_rows = features.shape[1]
    down_full, tap_full, full_up_weight = (
        lax.all_gather(down_weight, "dp", axis=2, tiled=True),
        lax.all_gather(tap_weight, "dp", axis=3, tiled=True),
        lax.all_gather(up_weight, "dp", axis=2, tiled=True),
    )
    stream = (
        features.astype(jnp.float32)
        + jnp.log1p(counts.astype(jnp.float32))[..., None] * count_weight
    )
    stored = []
    for layer_position in range(LAYERS):
        bin_distance = (DILATION_FIRST1 if layer_position == 0 else DILATION_SECOND2) // input_rows
        inverse = lax.rsqrt(jnp.mean(stream * stream, axis=-1, keepdims=True) + EPSILON)
        normed = (stream * inverse).astype(jnp.bfloat16)
        reduced = project(normed, down_full[layer_position]).astype(jnp.bfloat16)
        lagged = moved(reduced, bin_distance)
        advanced = moved(reduced, -bin_distance)
        mixture = (
            project(lagged, tap_full[layer_position, 0])
            + project(reduced, tap_full[layer_position, 1])
            + project(advanced, tap_full[layer_position, 2])
        )
        active_modes = gelu_exact(mixture).astype(jnp.bfloat16)
        stored.append((stream, inverse, reduced, lagged, advanced, mixture))
        stream = stream + jnp.einsum(
            "quy,yk->quk",
            active_modes,
            full_up_weight[layer_position],
            preferred_element_type=jnp.float32,
        )
    cot_wide = cotangent.astype(jnp.float32)
    logs = jnp.log(keep_share)[:, :, None] - decay_rate[None, None, :]
    mode_scale = jnp.sqrt(-jnp.expm1(-2.0 * decay_rate))
    fore_states, fore_decays, fore_exit, fore_log = modal_local(
        logs, jnp.zeros_like(logs[:, 0, :]), stream, cotangent
    )
    back_logs = jnp.concatenate(
        [jnp.zeros_like(logs[:, :1, :]), logs[:, ::-1, :][:, :-1, :]], axis=1
    )
    back_states, back_decays, back_exit, back_log = modal_local(
        back_logs, logs[:, 0, :], stream[:, ::-1, :], cotangent[:, ::-1, :]
    )
    summary = (jnp.exp(fore_log), fore_exit, jnp.exp(back_log), back_exit)
    identity = (
        jnp.ones_like(fore_log),
        jnp.zeros_like(fore_exit),
        jnp.ones_like(back_log),
        jnp.zeros_like(back_exit),
    )
    from_lower = entering_2(summary, "seq", join_lower, identity, False)
    from_upper = entering_2(summary, "seq", join_upper, identity, True)
    fore_entry = closed(
        summary[0], summary[1], from_lower[0], from_lower[1], from_upper[0], from_upper[1]
    )
    back_entry = closed(
        summary[2], summary[3], from_upper[2], from_upper[3], from_lower[2], from_lower[3]
    )
    fore_totals, fore_rows = modal_terms(
        fore_states,
        fore_decays,
        fore_entry,
        cot_wide,
        mode_scale,
        mode_scale[:, None] * mode_weight[1],
    )
    back_totals, back_rows = modal_terms(
        back_states,
        back_decays,
        back_entry,
        cot_wide[:, ::-1, :],
        mode_scale,
        mode_scale[:, None] * mode_weight[0],
    )
    gradient = cot_wide + fore_rows + back_rows[:, ::-1, :]
    mode_terms = jnp.stack([fore_totals, back_totals]).reshape(2 * M, -1)
    tap_terms = []
    for layer_position in reversed(range(LAYERS)):
        bin_distance = (DILATION_FIRST1 if layer_position == 0 else DILATION_SECOND2) // input_rows
        before, inverse, reduced, lagged, advanced, mixture = stored[layer_position]
        narrow_width = gradient.astype(jnp.bfloat16)
        back_mixed = jnp.einsum(
            "yhi,ai->yha",
            narrow_width,
            full_up_weight[layer_position],
            preferred_element_type=jnp.float32,
        )
        mixed_grad = (back_mixed * gelu_slope(mixture)).astype(jnp.bfloat16)
        tap_terms.insert(
            0,
            jnp.stack(
                [
                    contract(lagged, mixed_grad),
                    contract(reduced, mixed_grad),
                    contract(advanced, mixed_grad),
                ]
            ),
        )
        reduced_grad = jnp.einsum(
            "glk,bk->glb",
            mixed_grad,
            tap_full[layer_position, 1],
            preferred_element_type=jnp.float32,
        )
        reduced_grad = reduced_grad + jnp.einsum(
            "glk,bk->glb",
            moved(mixed_grad, -bin_distance),
            tap_full[layer_position, 0],
            preferred_element_type=jnp.float32,
        )
        reduced_grad = reduced_grad + jnp.einsum(
            "glk,bk->glb",
            moved(mixed_grad, bin_distance),
            tap_full[layer_position, 2],
            preferred_element_type=jnp.float32,
        )
        normed_grad = project_back(reduced_grad.astype(jnp.bfloat16), down_full[layer_position])
        gradient = (
            gradient
            + inverse * normed_grad
            - before
            * inverse
            * inverse
            * inverse
            * jnp.mean(normed_grad * before, axis=-1, keepdims=True)
        )
    tap_flat = jnp.stack(tap_terms).reshape(LAYERS * 3 * B, B)
    seq_size = lax.axis_size("seq")
    dp_size = lax.axis_size("dp")
    report_scale = 1.0 / math.sqrt(genome_count * dp_size * input_rows * seq_size)
    tap_sum, mode_sum = (
        lax.psum_scatter(tap_flat, ("seq", "dp"), scatter_dimension=0, tiled=True),
        lax.psum_scatter(mode_terms, ("seq", "dp"), scatter_dimension=1, tiled=True),
    )
    return (gradient.astype(jnp.bfloat16), tap_sum * report_scale, mode_sum * report_scale)


VMEM = pltpu.MemorySpace.VMEM
SMEM = pltpu.MemorySpace.SMEM
HBM = pltpu.MemorySpace.HBM
F32 = jnp.float32
BF16 = jnp.bfloat16
RING = 8
HOPS = (4, 2, 1)
BLOCK = 48
GIGA = 10**6


def call(body, operands, spaces, outs, scratch=(), size=0):
    return pl.pallas_call(
        body,
        out_shape=[jax.ShapeDtypeStruct(shape, dtype) for shape, dtype in outs],
        in_specs=[pl.BlockSpec(memory_space=space) for space in spaces],
        out_specs=[pl.BlockSpec(memory_space=VMEM) for _ in outs],
        scratch_shapes=list(scratch),
        cost_estimate=pl.CostEstimate(flops=size, transcendentals=0, bytes_accessed=size // 256) if size else None,
        compiler_params=pltpu.CompilerParams(vmem_limit_bytes=40 * 1024 * 1024),
    )(*operands)


def dot(left, right):
    return lax.dot_general(left, right, (((1,), (0,)), ((), ())), preferred_element_type=F32)


def dot_nt(left, right):
    return lax.dot_general(left, right, (((1,), (1,)), ((), ())), preferred_element_type=F32)


def dot_tn(left, right):
    return lax.dot_general(left, right, (((0,), (0,)), ((), ())), preferred_element_type=F32)


def iota2(shape, axis):
    return lax.broadcasted_iota(jnp.int32, shape, axis)


def split_pair(value):
    high = value.astype(BF16)
    return high, (value - high.astype(F32)).astype(BF16)


def log_sums(keep_row):
    rows = keep_row.shape[-1]
    below, beside = iota2((rows, rows), 0), iota2((rows, rows), 1)
    logs = jnp.broadcast_to(jnp.log(keep_row), (rows, rows))
    column = jnp.sum(jnp.where(beside <= below, logs, 0.0), axis=1, keepdims=True)
    spread = jnp.broadcast_to(column, (rows, rows))
    row = jnp.sum(jnp.where(beside == below, spread, 0.0), axis=0, keepdims=True)
    return column, row, column[rows - 1 :, :]


def mode_terms(sums, total, decay_ref, rows):
    place = iota2((1, rows), 1).astype(F32)
    to_start, to_end = [], []
    for mode in range(M):
        rate = decay_ref[mode]
        to_start.append(jnp.exp(sums - (place + 1.0) * rate))
        to_end.append(jnp.exp((total - sums) - (rows - 1.0 - place) * rate))
    leaving = jnp.concatenate(to_start + to_end, axis=0)
    entering = jnp.concatenate(to_end + to_start, axis=0)
    return leaving, entering


def prepare_body(cot_hbm, keep_hbm, decay_hbm, pay_ref, cot_ref, keep_ref, decay_ref, sems):
    pairs = ((keep_hbm, keep_ref), (decay_hbm, decay_ref), (cot_hbm, cot_ref))
    copies = [pltpu.make_async_copy(source, to, sems.at[index]) for index, (source, to) in enumerate(pairs)]
    for copy in copies:
        copy.start()
    copies[0].wait()
    copies[1].wait()
    rows = keep_ref.shape[-1]
    _, sums, total = log_sums(keep_ref[...])
    weights, _ = mode_terms(sums, total, decay_ref, rows)
    high = weights.astype(BF16).astype(F32)
    both = jnp.concatenate([high, weights - high], axis=0).astype(BF16)
    width = cot_ref.shape[-1]
    first = jnp.broadcast_to(total, (8, 128))
    one = first.astype(BF16).astype(F32)
    two = (first - one).astype(BF16).astype(F32)
    three = first - one - two
    row = iota2((8, 128), 0)
    extra = jnp.where(row == 0, one, jnp.where(row == 1, two, jnp.where(row == 2, three, 0.0)))
    pay_ref[0, :, width:] = extra.astype(BF16)
    copies[2].wait()
    states = dot(both, cot_ref[0])
    pay_ref[0, :, :width] = (states[0:8] + states[8:16]).astype(BF16)


def assemble_body(down_ref, down_far_ref, tap_ref, tap_far_ref, down_out, tap_out):
    core = lax.axis_index("dp")
    half = down_ref.shape[1]
    for down, taps, side in ((down_ref, tap_ref, core), (down_far_ref, tap_far_ref, 1 - core)):
        part = pl.ds(pl.multiple_of(side * half, half), half)
        for layer in range(LAYERS):
            down_out[layer, part, :] = down[layer]
            total = taps[layer, 0].astype(F32) + taps[layer, 1].astype(F32) + taps[layer, 2].astype(F32)
            tap_out[layer, part, :] = total.astype(BF16)


def forward_body(
    feature_ref, count_ref, weight_ref, down_ref, tap_ref, up_ref, up_far_ref,
    stream_ref, inverse_ref, reduced_ref, slope_ref,
):
    core = lax.axis_index("dp")
    rows, width = feature_ref.shape[1:]
    logs = jnp.broadcast_to(jnp.log1p(count_ref[...].astype(F32)), (rows, rows))
    diagonal = iota2((rows, rows), 0) == iota2((rows, rows), 1)
    level = jnp.sum(jnp.where(diagonal, logs, 0.0), axis=1, keepdims=True)
    stream = feature_ref[0].astype(F32) + level * weight_ref[...]
    for layer in range(LAYERS):
        stream_ref[layer] = stream
        mean = jnp.sum(stream * stream, axis=-1, keepdims=True) * (1.0 / width)
        inverse = lax.rsqrt(mean + EPSILON)
        inverse_ref[layer] = inverse
        normed = (stream * inverse).astype(BF16)
        reduced = dot_nt(normed, down_ref[layer]).astype(BF16)
        reduced_ref[layer * rows : (layer + 1) * rows, :] = reduced
        mixture = dot_nt(reduced, tap_ref[layer])
        share = 0.5 * (1.0 + lax.erf(mixture * HALF_ROOT))
        slope_ref[layer] = share + mixture * jnp.exp(-0.5 * mixture * mixture) * DENSITY
        act = (mixture * share).astype(BF16)
        out_near = dot(act, up_ref[layer])
        out_away = dot(act, up_far_ref[layer])
        low = jnp.where(core == 0, out_near, out_away)
        high = jnp.where(core == 0, out_away, out_near)
        stream = stream + jnp.concatenate([low, high], axis=-1)
    stream_ref[LAYERS] = stream


def local_body(decay_ref, scale_ref, cot_ref, keep_ref, mode_ref, stream_ref, grad_ref, mark_ref, reach_ref):
    rows, width = cot_ref.shape[1:]
    column, row, total = log_sums(keep_ref[...])
    below = iota2((rows, rows), 0)
    across = iota2((rows, rows), 1)
    gap = column - row
    steps = (below - across).astype(F32)
    kernels = []
    for mode in range(M):
        value = jnp.exp(jnp.minimum(steps * decay_ref[mode] - gap, 0.0))
        kernels.append(jnp.where(across >= below, value, 0.0))
    for mode in range(M):
        value = jnp.exp(jnp.minimum(gap - steps * decay_ref[mode], 0.0))
        kernels.append(jnp.where(below >= across, value, 0.0))
    pairs = [jnp.concatenate(split_pair(kernel), axis=1) for kernel in kernels]
    _, edges = mode_terms(row, total, decay_ref, rows)
    high = edges.astype(BF16).astype(F32)
    both = jnp.concatenate([high, edges - high], axis=0).astype(BF16)
    span = 256
    for start in range(0, width, span):
        part = slice(start, start + span)
        cot = cot_ref[0, :, part]
        doubled = jnp.concatenate([cot, cot], axis=0)
        stream = stream_ref[LAYERS, :, part]
        grad = cot.astype(F32)
        marks = []
        for index in range(2 * M):
            mode = index % M
            field = dot(pairs[index], doubled)
            gain = scale_ref[mode]
            grad = grad + (gain * mode_ref[index // M, mode : mode + 1, part]) * field
            marks.append(jnp.sum(stream * field, axis=0, keepdims=True))
        grad_ref[:, part] = grad
        mark_ref[:, part] = jnp.concatenate(marks, axis=0)
        near, away = split_pair(stream)
        reach = dot(both, near)
        reach_ref[:, part] = reach[0:8] + reach[8:16] + dot(both, away)[0:8]


def backward_body(
    decay_ref, scale_ref, first_ref, second_ref, third_ref, fourth_ref, keep_ref, mode_ref,
    local_ref, mark_ref, reach_ref, stream_ref, inverse_ref, slope_ref, down_ref, tap_ref, up_ref,
    up_far_ref, grads_ref, mixed_ref, partial_ref,
):
    core = lax.axis_index("dp")
    place = lax.axis_index("seq")
    rows = keep_ref.shape[-1]
    width = local_ref.shape[-1]
    wide = up_ref.shape[-1]

    masks = [0]
    for hop in (HOPS[0], HOPS[1] - core, HOPS[2] + core):
        masks = masks + [lax.bitwise_xor(mask, hop) for mask in masks]
    pieces = []
    for ref in (first_ref, second_ref, third_ref, fourth_ref):
        pieces = pieces + [ref[index].astype(F32) for index in range(ref.shape[0])]
    totals = [jnp.sum(piece[:, width:], axis=0, keepdims=True) for piece in pieces]
    row8 = iota2((8, 128), 0)
    decay8 = jnp.zeros((8, 128), F32)
    gain8 = jnp.zeros((8, 128), F32)
    for index in range(2 * M):
        decay8 = jnp.where(row8 == index, decay_ref[index % M], decay8)
        gain8 = jnp.where(row8 == index, scale_ref[index % M], gain8)
    gain8 = gain8[:, 0:1]
    everything = totals[0]
    for value in totals[1:]:
        everything = everything + value
    loop = 1.0 - jnp.exp(jnp.broadcast_to(everything, (8, 128)) - (RING * rows) * decay8)
    others = [lax.bitwise_xor(place, mask) for mask in masks]
    ahead = [lax.rem(place - other + (RING - 1), RING) for other in others]
    after = [lax.rem(other - place + (RING - 1), RING) for other in others]
    entering = jnp.zeros((8, width), F32)
    for index in range(RING):
        fore = jnp.zeros((1, 128), F32)
        back = jnp.zeros((1, 128), F32)
        for other in range(RING):
            fore = fore + jnp.where(ahead[other] < ahead[index], totals[other], 0.0)
            back = back + jnp.where(after[other] < after[index], totals[other], 0.0)
        fore = jnp.broadcast_to(fore, (8, 128)) - (ahead[index] * rows).astype(F32) * decay8
        back = jnp.broadcast_to(back, (8, 128)) - (after[index] * rows).astype(F32) * decay8
        share = jnp.exp(jnp.where(row8 < M, back, fore)) / loop
        entering = entering + share[:, 0:1] * pieces[index][:, :width]
    whole = gain8 * (mark_ref[...] + entering * reach_ref[...])
    partial = jnp.concatenate([whole[:, :wide], whole[:, wide:]], axis=0)
    partial_ref[...] = partial
    high, low = split_pair(partial)
    mixed_ref[LAYERS * rows : LAYERS * rows + 16, :] = high
    mixed_ref[LAYERS * rows + 16 : LAYERS * rows + 32, :] = low
    _, sums, total = log_sums(keep_ref[...])
    _, edges = mode_terms(sums, total, decay_ref, rows)
    weighted = entering * gain8 * jnp.concatenate([mode_ref[0], mode_ref[1]], axis=0)
    edge_high = edges.astype(BF16).astype(F32)
    edge_low = edges - edge_high
    in_high = weighted.astype(BF16).astype(F32)
    in_low = weighted - in_high
    left = jnp.concatenate([edge_high, edge_high, edge_low, jnp.zeros_like(edges)], axis=0).astype(BF16)
    right = jnp.concatenate([in_high, in_low, in_high, jnp.zeros_like(in_high)], axis=0).astype(BF16)
    gradient = local_ref[...] + dot_tn(left, right)

    for layer in reversed(range(LAYERS)):
        narrow = gradient.astype(BF16)
        first, second = narrow[:, :wide], narrow[:, wide:]
        mine = jnp.where(core == 0, first, second)
        theirs = jnp.where(core == 0, second, first)
        back = dot_nt(mine, up_ref[layer]) + dot_nt(theirs, up_far_ref[layer])
        mixed = (back * slope_ref[layer]).astype(BF16)
        mixed_ref[layer * rows : (layer + 1) * rows, :] = mixed
        if layer:
            gradient = through_layer(layer, gradient, mixed, stream_ref, inverse_ref, down_ref, tap_ref)
    grads_ref[...] = gradient


def through_layer(layer, gradient, mixed, stream_ref, inverse_ref, down_ref, tap_ref):
    passed = dot(mixed, tap_ref[layer]).astype(BF16)
    normed = dot(passed, down_ref[layer])
    before = stream_ref[layer]
    inverse = inverse_ref[layer]
    shared = jnp.sum(normed * before, axis=-1, keepdims=True) * (1.0 / before.shape[-1])
    return gradient + inverse * normed - before * (inverse * inverse * inverse * shared)


def output_body(gradient_ref, mixed_ref, stream_ref, inverse_ref, down_ref, tap_ref, grad_ref):
    rows = gradient_ref.shape[0]
    mixed = mixed_ref[0:rows, :]
    gradient = through_layer(0, gradient_ref[...], mixed, stream_ref, inverse_ref, down_ref, tap_ref)
    grad_ref[0] = gradient.astype(BF16)


def held_block(parity, bit_x, bit_z, layer):
    core = lax.bitwise_xor(lax.bitwise_xor(parity, bit_x), lax.bitwise_xor(bit_z, layer))
    return pl.multiple_of(lax.rem(3 * core + 6 * bit_x + 4 * bit_z, RING) * BLOCK, BLOCK)


def taps_body(
    reduced_ref, reduced_far_ref, mixed_ref, mixed_far_ref, partial_ref,
    kept_ref, send_ref, partial_out, block_ref,
):
    bits, parity = position_bits()
    bit = pick(parity, bits[0], bits[1])
    rows = reduced_ref.shape[0] // LAYERS
    for layer in range(LAYERS):
        part = slice(layer * rows, (layer + 1) * rows)
        left = jnp.concatenate([reduced_ref[part, :], reduced_far_ref[part, :]], axis=0)
        right = jnp.concatenate([mixed_ref[part, :], mixed_far_ref[part, :]], axis=0)
        block_ref[layer] = dot_tn(left, right)
    kept_rows = kept_ref.shape[0]
    for turn in range(2):
        for layer in range(LAYERS):
            to = (2 * turn + layer) * BLOCK
            kept = held_block(parity, pick(parity, bit, turn), pick(parity, turn, bit), layer)
            sent = held_block(parity, pick(parity, 1 - bit, turn), pick(parity, turn, 1 - bit), layer)
            kept_ref[to : to + BLOCK, :] = block_ref[layer, pl.ds(kept, BLOCK), :]
            send_ref[to : to + BLOCK, :] = block_ref[layer, pl.ds(sent, BLOCK), :].astype(BF16)
    high = mixed_far_ref[LAYERS * rows : LAYERS * rows + 16, :].astype(F32)
    low = mixed_far_ref[LAYERS * rows + 16 : LAYERS * rows + 32, :].astype(F32)
    partial = partial_ref[...] + (high + low)
    partial_out[...] = partial
    send_ref[kept_rows : kept_rows + 16, :] = partial.astype(BF16)


def position_bits():
    place = lax.axis_index("seq")
    bits = [lax.rem(place // value, 2) for value in (1, 2, 4)]
    return bits, lax.rem(lax.axis_index("dp") + bits[0] + bits[1] + bits[2], 2)


def pick(parity, even, odd):
    return even + parity * (odd - even)


def join_body(stage, kept_ref, got_ref, partial_ref, kept_out, send_out, partial_out):
    rows = kept_out.shape[0]
    bits, parity = position_bits()
    bit = pick(parity, bits[1], bits[0]) if stage == 1 else bits[2]
    keep = pl.ds(pl.multiple_of(bit * rows, rows), rows)
    send = pl.ds(pl.multiple_of((1 - bit) * rows, rows), rows)
    kept_out[...] = kept_ref[keep, :] + got_ref[keep, :].astype(F32)
    send_out[0:rows, :] = (kept_ref[send, :] + got_ref[send, :].astype(F32)).astype(BF16)
    partial = partial_ref[...] + got_ref[2 * rows : 2 * rows + 16, :].astype(F32)
    if stage == 1:
        partial_out[...] = partial
        send_out[rows : rows + 16, :] = partial.astype(BF16)
    else:
        last = bits[2]
        partial_out[...] = jnp.where(last == 0, partial[0:8], partial[8:16])
        send_out[rows : rows + 8, :] = jnp.where(last == 0, partial[8:16], partial[0:8]).astype(BF16)


def finish_body(scale, kept_ref, got_ref, block_out, send_out):
    rows = kept_ref.shape[0]
    block = (kept_ref[...] + got_ref[0:rows, :].astype(F32)) * scale
    block_out[...] = block
    send_out[...] = block.astype(BF16)


def modes_body(scale, got_ref, partial_ref, mode_out):
    rows = got_ref.shape[0] - 8
    full = (partial_ref[...] + got_ref[rows : rows + 8, :].astype(F32)) * scale
    number = lax.rem(2 * lax.axis_index("seq") + lax.axis_index("dp"), 8)
    span = full.shape[1]
    mode_out[...] = pltpu.roll(full, lax.rem(span - BLOCK * number, span), 1)[:, 0:BLOCK]


def swap(value, axis, mask):
    count = lax.axis_size(axis)
    return lax.ppermute(value, axis, [(source, source ^ mask) for source in range(count)])


def hop_to(value, step):
    pairs = []
    for source in range(2 * lax.axis_size("seq")):
        flip, mask = step(source % 2, source // 2)
        pairs.append((source, source ^ (2 * mask + flip)))
    return lax.ppermute(value, ("seq", "dp"), pairs)


def class_of(core, place):
    return (core + place + place // 2 + place // 4) % 2


def wrapped_device(
    features, cotangent, counts, count_weight, down_weight, tap_weight, up_weight,
    decay_rate, keep_share, mode_weight,
):
    rows, width = features.shape[1:]
    down = jnp.swapaxes(down_weight, 1, 2)
    taps = jnp.swapaxes(tap_weight, 2, 3)
    down_far, up_far, taps_far = swap(down, "dp", 1), swap(up_weight, "dp", 1), swap(taps, "dp", 1)
    scale = jnp.sqrt(-jnp.expm1(-2.0 * decay_rate))
    (pay,) = call(
        prepare_body,
        tuple(pltpu.with_memory_space_constraint(value, HBM) for value in (cotangent, keep_share, decay_rate)),
        (HBM,) * 3,
        (((1, 8, width + 128), BF16),),
        (
            pltpu.VMEM(cotangent.shape, BF16),
            pltpu.VMEM(keep_share.shape, F32),
            pltpu.SMEM(decay_rate.shape, F32),
            pltpu.SemaphoreType.DMA((3,)),
        ),
        size=1300 * GIGA,
    )
    got = hop_to(pay, lambda core, place: (0, HOPS[0]))
    down_full, tap_full = call(
        assemble_body,
        (down, down_far, taps, taps_far),
        (VMEM,) * 4,
        (((LAYERS, B, width), BF16), ((LAYERS, B, B), BF16)), size=1200 * GIGA
    )
    two = jnp.concatenate([pay, got], axis=0)
    two, down_full, tap_full = lax.optimization_barrier((two, down_full, tap_full))
    got_two = hop_to(two, lambda core, place: (0, HOPS[1 + core]))
    stream, inverse, reduced, slope = call(
        forward_body,
        (features, counts, count_weight[None], down_full, tap_full, up_weight, up_far),
        (VMEM,) * 7,
        (
            ((LAYERS + 1, rows, width), F32),
            ((LAYERS, rows, 1), F32),
            ((LAYERS * rows, B), BF16),
            ((LAYERS, rows, B), F32),
        ), size=1800 * GIGA
    )
    four = jnp.concatenate([two, got_two], axis=0)
    four, stream, reduced = lax.optimization_barrier((four, stream, reduced))
    got_four = hop_to(four, lambda core, place: (0, HOPS[2 - core]))
    reduced_far = swap(reduced, "dp", 1)
    local, mark, reach = call(
        local_body,
        (decay_rate, scale, cotangent, keep_share, mode_weight, stream),
        (SMEM, SMEM) + (VMEM,) * 4,
        (((rows, width), F32), ((8, width), F32), ((8, width), F32)), size=1600 * GIGA
    )
    local, reduced_far = lax.optimization_barrier((local, reduced_far))
    gradient, mixed, partial = call(
        backward_body,
        (
            decay_rate, scale, pay, got, got_two, got_four, keep_share, mode_weight, local, mark, reach,
            stream, inverse, slope, down_full, tap_full, up_weight, up_far,
        ),
        (SMEM, SMEM) + (VMEM,) * 16,
        (((rows, width), F32), ((LAYERS * rows + 32, B), BF16), ((16, B), F32)), size=2100 * GIGA
    )
    mixed_far = swap(mixed, "dp", 1)
    (grad,) = call(
        output_body,
        (gradient, mixed, stream, inverse, down_full, tap_full),
        (VMEM,) * 6,
        (((1, rows, width), BF16),), size=1300 * GIGA
    )
    kept_rows = RING * BLOCK // 2
    kept, send, partial = call(
        taps_body,
        (reduced, reduced_far, mixed, mixed_far, partial),
        (VMEM,) * 5,
        (((kept_rows, B), F32), ((kept_rows + 16, B), BF16), ((16, B), F32)),
        (pltpu.VMEM((LAYERS, B, B), F32),), size=500 * GIGA
    )
    got = hop_to(send, lambda core, place: (1, 1 + class_of(core, place)))
    for stage in (1, 2):
        kept_rows = kept.shape[0] // 2
        mode_rows = (16, 8)[stage - 1]
        kept, send, partial = call(
            functools.partial(join_body, stage),
            (kept, got, partial),
            (VMEM,) * 3,
            (((kept_rows, B), F32), ((kept_rows + mode_rows, B), BF16), ((mode_rows, B), F32)),
        )
        if stage == 1:
            send, grad = lax.optimization_barrier((send, grad))
        if stage == 1:
            got = hop_to(send, lambda core, place: (1, 2 - class_of(core, place)))
        else:
            got = hop_to(send, lambda core, place: (1, 4))
    total = features.shape[0] * lax.axis_size("dp") * rows * lax.axis_size("seq")
    report = 1.0 / math.sqrt(total)
    block, narrow = call(
        functools.partial(finish_body, report),
        (kept, got),
        (VMEM,) * 2,
        (((BLOCK, B), F32), ((BLOCK, B), BF16)),
    )
    parts = [block]
    for step in (3, 6):
        pairs = [(8 * layer + (j + step) % 8, 8 * layer + j) for layer in range(LAYERS) for j in range(8)]
        parts.append(lax.ppermute(narrow, ("seq", "dp"), pairs).astype(F32))
    (mode_sum,) = call(
        functools.partial(modes_body, report), (got, partial), (VMEM,) * 2, (((8, BLOCK), F32),)
    )
    return grad, jnp.concatenate(parts, axis=0), mode_sum


def solution(mesh):
    placed = (
        P(("parts", "dp"), "seq", None),
        P(("parts", "dp"), "seq", None),
        P(("parts", "dp"), "seq"),
        P(),
        P(None, None, "dp"),
        P(None, None, None, "dp"),
        P(None, None, "dp"),
        P(),
        P(("parts", "dp"), "seq"),
        P(),
    )

    def per_device(*operands):
        rows = operands[0].shape[1]
        ring = lax.axis_size("seq")
        loop = ring * rows
        wraps = all(dilation % loop == 0 for dilation in (DILATION_FIRST1, DILATION_SECOND2))
        fits = ring == RING and lax.axis_size("dp") == 2 and operands[0].shape[0] == 1
        return (wrapped_device if wraps and fits else general_device)(*operands)

    return jax.shard_map(
        per_device,
        mesh=mesh,
        in_specs=placed,
        out_specs=(
            P(("parts", "dp"), "seq", None),
            P(("parts", "seq", "dp"), None),
            P("parts", ("seq", "dp")),
        ),
        check_vma=False,
    )
```

```python
import functools
import math

import jax
import jax.numpy as jnp
from jax import lax
from jax.experimental import pallas as pl
from jax.experimental.pallas import tpu as pltpu
from jax.sharding import PartitionSpec as P

B = 384
DILATION_FIRST1 = 2048
DILATION_SECOND2 = 4096
M = 4
LAYERS = 2


EPSILON = 1e-06
HALF_ROOT = 1.0 / math.sqrt(2.0)
DENSITY = 1.0 / math.sqrt(2.0 * math.pi)
TOP_PRECISION = lax.Precision.HIGHEST


def shifted(value, axis, steps):
    count = lax.axis_size(axis)
    pairs = [(source, (source + steps) % count) for source in range(count)]
    return lax.ppermute(value, axis, pairs)


def entering_2(shard, axis, join, neutral, backward):
    count = lax.axis_size(axis)
    place = lax.axis_index(axis)
    ahead = count - 1 - place if backward else place
    gathered = jax.tree.map(
        lambda a, kind: lax.all_gather(a.astype(kind), axis),
        shard,
        jax.tree.map(lambda a: jnp.bfloat16 if a.dtype == jnp.float32 else a.dtype, shard),
    )
    state = jax.tree.map(lambda a, e: jnp.zeros_like(a) + jnp.asarray(e, a.dtype), shard, neutral)

    def one(turn, state):
        source = count - 1 - turn if backward else turn
        return join(
            state,
            jax.tree.map(
                lambda a, own: lax.dynamic_index_in_dim(a, source, 0, False).astype(own.dtype),
                gathered,
                shard,
            ),
        )

    return lax.fori_loop(0, ahead, one, state)


def gelu_exact(values):
    return 0.5 * values * (1.0 + lax.erf(values * HALF_ROOT))


def gelu_slope(values):
    cumulative = 0.5 * (1.0 + lax.erf(values * HALF_ROOT))
    return cumulative + values * jnp.exp(-0.5 * values * values) * DENSITY


def project(left_shifted, right_shifted):
    return jnp.einsum(
        "qra,au->qru", left_shifted, right_shifted, preferred_element_type=jnp.float32
    )


def project_back(left_shifted, right_shifted):
    return jnp.einsum(
        "kut,st->kus", left_shifted, right_shifted, preferred_element_type=jnp.float32
    )


def contract(left_shifted, right_shifted):
    return jnp.einsum(
        "glb,glk->bk", left_shifted, right_shifted, preferred_element_type=jnp.float32
    )


def moved(values, bin_distance):
    return shifted(values, "seq", bin_distance)


def block_product(kernel, pieces):
    return jnp.einsum(
        "gmbij,gbjc->gmbic",
        kernel,
        pieces,
        precision=TOP_PRECISION,
        preferred_element_type=jnp.float32,
    )


def modal_local(lg_in, lg_exit, stream_rows, cotangent_rows):
    genome_count, input_rows, mode_count = lg_in.shape
    feature_maps = stream_rows.shape[-1]
    block_size = min(128, input_rows)
    block_count = input_rows // block_size
    running = jnp.cumsum(lg_in, axis=1)
    running_blocks = running.reshape(genome_count, block_count, block_size, mode_count)
    block_ends = running_blocks[:, :, -1, :]
    block_starts = jnp.concatenate(
        [jnp.zeros((genome_count, 1, mode_count), jnp.float32), block_ends[:, :-1, :]], axis=1
    )
    within = running_blocks - block_starts[:, :, None, :]
    within_t = jnp.transpose(within, (0, 3, 1, 2))
    spread = within_t[..., :, None] - within_t[..., None, :]
    row_index = lax.broadcasted_iota(jnp.int32, (block_size, block_size), 0)
    column_index = lax.broadcasted_iota(jnp.int32, (block_size, block_size), 1)
    kernel = jnp.where(row_index >= column_index, jnp.exp(jnp.minimum(spread, 0.0)), 0.0)
    joined_source = jnp.concatenate([stream_rows, cotangent_rows.astype(jnp.float32)], axis=-1)
    joined_source = joined_source.reshape(genome_count, block_count, block_size, 2 * feature_maps)
    partial_value = block_product(kernel, joined_source)
    block_tails = partial_value[:, :, :, -1, :]
    ends_t = jnp.transpose(block_ends, (0, 2, 1))
    starts_t = jnp.transpose(block_starts, (0, 2, 1))
    spacing = starts_t[..., :, None] - ends_t[..., None, :]
    block_index = lax.broadcasted_iota(jnp.int32, (block_count, block_count), 0)
    source_index = lax.broadcasted_iota(jnp.int32, (block_count, block_count), 1)
    linkage = jnp.where(source_index < block_index, jnp.exp(jnp.minimum(spacing, 0.0)), 0.0)
    entering = jnp.einsum(
        "gmbk,gmkc->gmbc",
        linkage,
        block_tails,
        precision=TOP_PRECISION,
        preferred_element_type=jnp.float32,
    )
    states = partial_value + jnp.exp(within_t)[..., None] * entering[:, :, :, None, :]
    states = states.reshape(genome_count, mode_count, input_rows, 2 * feature_maps)
    decay_values = jnp.exp(jnp.transpose(running, (0, 2, 1)))
    exit_state = jnp.exp(lg_exit)[..., None] * states[:, :, -1, :]
    log_pass = running[:, -1, :] + lg_exit
    return (states, decay_values, exit_state, log_pass)


def modal_terms(states, decay_values, entering, cotangent_rows, source_gain, cot_gain):
    feature_maps = cotangent_rows.shape[-1]
    reach_sum = jnp.einsum(
        "qsz,qzj->qsj",
        decay_values,
        cotangent_rows,
        precision=TOP_PRECISION,
        preferred_element_type=jnp.float32,
    )
    totals = jnp.einsum(
        "veyi,vyi->ei",
        states[..., :feature_maps],
        cotangent_rows,
        precision=TOP_PRECISION,
        preferred_element_type=jnp.float32,
    )
    totals = totals + jnp.sum(entering[..., :feature_maps] * reach_sum, axis=0)
    rows_out = jnp.einsum(
        "jryf,rf->jyf",
        states[..., feature_maps:],
        cot_gain,
        precision=TOP_PRECISION,
        preferred_element_type=jnp.float32,
    )
    rows_out = rows_out + jnp.einsum(
        "ert,erx->etx",
        decay_values,
        entering[..., feature_maps:] * cot_gain[None],
        precision=TOP_PRECISION,
        preferred_element_type=jnp.float32,
    )
    return (source_gain[:, None] * totals, rows_out)


def apply_early_first(early_pass, early_state, late_pass, late_state):
    return (early_pass * late_pass, late_pass[..., None] * early_state + late_state)


def apply_late_first(early_pass, early_state, late_pass, late_state):
    return (early_pass * late_pass, early_pass[..., None] * late_state + early_state)


def join_lower(early, late):
    fore_pass, fore_state = apply_early_first(early[0], early[1], late[0], late[1])
    back_pass, back_state = apply_late_first(early[2], early[3], late[2], late[3])
    return (fore_pass, fore_state, back_pass, back_state)


def join_upper(early, late):
    fore_pass, fore_state = apply_late_first(early[0], early[1], late[0], late[1])
    back_pass, back_state = apply_early_first(early[2], early[3], late[2], late[3])
    return (fore_pass, fore_state, back_pass, back_state)


def closed(own_pass, own_state, pass_before, state_before, pass_after, state_after):
    beside_all = pass_before * pass_after
    numerator = (
        beside_all[..., None] * own_state + pass_before[..., None] * state_after + state_before
    )
    return numerator / (1.0 - beside_all * own_pass)[..., None]


def general_device(
    features,
    cotangent,
    counts,
    count_weight,
    down_weight,
    tap_weight,
    up_weight,
    decay_rate,
    keep_share,
    mode_weight,
):
    genome_count = features.shape[0]
    input_rows = features.shape[1]
    down_full, tap_full, full_up_weight = (
        lax.all_gather(down_weight, "dp", axis=2, tiled=True),
        lax.all_gather(tap_weight, "dp", axis=3, tiled=True),
        lax.all_gather(up_weight, "dp", axis=2, tiled=True),
    )
    stream = (
        features.astype(jnp.float32)
        + jnp.log1p(counts.astype(jnp.float32))[..., None] * count_weight
    )
    stored = []
    for layer_position in range(LAYERS):
        bin_distance = (DILATION_FIRST1 if layer_position == 0 else DILATION_SECOND2) // input_rows
        inverse = lax.rsqrt(jnp.mean(stream * stream, axis=-1, keepdims=True) + EPSILON)
        normed = (stream * inverse).astype(jnp.bfloat16)
        reduced = project(normed, down_full[layer_position]).astype(jnp.bfloat16)
        lagged = moved(reduced, bin_distance)
        advanced = moved(reduced, -bin_distance)
        mixture = (
            project(lagged, tap_full[layer_position, 0])
            + project(reduced, tap_full[layer_position, 1])
            + project(advanced, tap_full[layer_position, 2])
        )
        active_modes = gelu_exact(mixture).astype(jnp.bfloat16)
        stored.append((stream, inverse, reduced, lagged, advanced, mixture))
        stream = stream + jnp.einsum(
            "quy,yk->quk",
            active_modes,
            full_up_weight[layer_position],
            preferred_element_type=jnp.float32,
        )
    cot_wide = cotangent.astype(jnp.float32)
    logs = jnp.log(keep_share)[:, :, None] - decay_rate[None, None, :]
    mode_scale = jnp.sqrt(-jnp.expm1(-2.0 * decay_rate))
    fore_states, fore_decays, fore_exit, fore_log = modal_local(
        logs, jnp.zeros_like(logs[:, 0, :]), stream, cotangent
    )
    back_logs = jnp.concatenate(
        [jnp.zeros_like(logs[:, :1, :]), logs[:, ::-1, :][:, :-1, :]], axis=1
    )
    back_states, back_decays, back_exit, back_log = modal_local(
        back_logs, logs[:, 0, :], stream[:, ::-1, :], cotangent[:, ::-1, :]
    )
    summary = (jnp.exp(fore_log), fore_exit, jnp.exp(back_log), back_exit)
    identity = (
        jnp.ones_like(fore_log),
        jnp.zeros_like(fore_exit),
        jnp.ones_like(back_log),
        jnp.zeros_like(back_exit),
    )
    from_lower = entering_2(summary, "seq", join_lower, identity, False)
    from_upper = entering_2(summary, "seq", join_upper, identity, True)
    fore_entry = closed(
        summary[0], summary[1], from_lower[0], from_lower[1], from_upper[0], from_upper[1]
    )
    back_entry = closed(
        summary[2], summary[3], from_upper[2], from_upper[3], from_lower[2], from_lower[3]
    )
    fore_totals, fore_rows = modal_terms(
        fore_states,
        fore_decays,
        fore_entry,
        cot_wide,
        mode_scale,
        mode_scale[:, None] * mode_weight[1],
    )
    back_totals, back_rows = modal_terms(
        back_states,
        back_decays,
        back_entry,
        cot_wide[:, ::-1, :],
        mode_scale,
        mode_scale[:, None] * mode_weight[0],
    )
    gradient = cot_wide + fore_rows + back_rows[:, ::-1, :]
    mode_terms = jnp.stack([fore_totals, back_totals]).reshape(2 * M, -1)
    tap_terms = []
    for layer_position in reversed(range(LAYERS)):
        bin_distance = (DILATION_FIRST1 if layer_position == 0 else DILATION_SECOND2) // input_rows
        before, inverse, reduced, lagged, advanced, mixture = stored[layer_position]
        narrow_width = gradient.astype(jnp.bfloat16)
        back_mixed = jnp.einsum(
            "yhi,ai->yha",
            narrow_width,
            full_up_weight[layer_position],
            preferred_element_type=jnp.float32,
        )
        mixed_grad = (back_mixed * gelu_slope(mixture)).astype(jnp.bfloat16)
        tap_terms.insert(
            0,
            jnp.stack(
                [
                    contract(lagged, mixed_grad),
                    contract(reduced, mixed_grad),
                    contract(advanced, mixed_grad),
                ]
            ),
        )
        reduced_grad = jnp.einsum(
            "glk,bk->glb",
            mixed_grad,
            tap_full[layer_position, 1],
            preferred_element_type=jnp.float32,
        )
        reduced_grad = reduced_grad + jnp.einsum(
            "glk,bk->glb",
            moved(mixed_grad, -bin_distance),
            tap_full[layer_position, 0],
            preferred_element_type=jnp.float32,
        )
        reduced_grad = reduced_grad + jnp.einsum(
            "glk,bk->glb",
            moved(mixed_grad, bin_distance),
            tap_full[layer_position, 2],
            preferred_element_type=jnp.float32,
        )
        normed_grad = project_back(reduced_grad.astype(jnp.bfloat16), down_full[layer_position])
        gradient = (
            gradient
            + inverse * normed_grad
            - before
            * inverse
            * inverse
            * inverse
            * jnp.mean(normed_grad * before, axis=-1, keepdims=True)
        )
    tap_flat = jnp.stack(tap_terms).reshape(LAYERS * 3 * B, B)
    seq_size = lax.axis_size("seq")
    dp_size = lax.axis_size("dp")
    report_scale = 1.0 / math.sqrt(genome_count * dp_size * input_rows * seq_size)
    tap_sum, mode_sum = (
        lax.psum_scatter(tap_flat, ("seq", "dp"), scatter_dimension=0, tiled=True),
        lax.psum_scatter(mode_terms, ("seq", "dp"), scatter_dimension=1, tiled=True),
    )
    return (gradient.astype(jnp.bfloat16), tap_sum * report_scale, mode_sum * report_scale)


VMEM = pltpu.MemorySpace.VMEM
SMEM = pltpu.MemorySpace.SMEM
HBM = pltpu.MemorySpace.HBM
F32 = jnp.float32
BF16 = jnp.bfloat16
RING = 8
HOPS = (4, 2, 1)
BLOCK = 48
GIGA = 10**6


def call(body, operands, spaces, outs, scratch=(), size=0):
    return pl.pallas_call(
        body,
        out_shape=[jax.ShapeDtypeStruct(shape, dtype) for shape, dtype in outs],
        in_specs=[pl.BlockSpec(memory_space=space) for space in spaces],
        out_specs=[pl.BlockSpec(memory_space=VMEM) for _ in outs],
        scratch_shapes=list(scratch),
        cost_estimate=pl.CostEstimate(flops=size, transcendentals=0, bytes_accessed=size // 256) if size else None,
        compiler_params=pltpu.CompilerParams(vmem_limit_bytes=40 * 1024 * 1024),
    )(*operands)


def dot(left, right):
    return lax.dot_general(left, right, (((1,), (0,)), ((), ())), preferred_element_type=F32)


def dot_nt(left, right):
    return lax.dot_general(left, right, (((1,), (1,)), ((), ())), preferred_element_type=F32)


def dot_tn(left, right):
    return lax.dot_general(left, right, (((0,), (0,)), ((), ())), preferred_element_type=F32)


def iota2(shape, axis):
    return lax.broadcasted_iota(jnp.int32, shape, axis)


def split_pair(value):
    high = value.astype(BF16)
    return high, (value - high.astype(F32)).astype(BF16)


def log_sums(keep_row):
    rows = keep_row.shape[-1]
    below, beside = iota2((rows, rows), 0), iota2((rows, rows), 1)
    logs = jnp.broadcast_to(jnp.log(keep_row), (rows, rows))
    column = jnp.sum(jnp.where(beside <= below, logs, 0.0), axis=1, keepdims=True)
    spread = jnp.broadcast_to(column, (rows, rows))
    row = jnp.sum(jnp.where(beside == below, spread, 0.0), axis=0, keepdims=True)
    return column, row, column[rows - 1 :, :]


def mode_terms(sums, total, decay_ref, rows):
    place = iota2((1, rows), 1).astype(F32)
    to_start, to_end = [], []
    for mode in range(M):
        rate = decay_ref[mode]
        to_start.append(jnp.exp(sums - (place + 1.0) * rate))
        to_end.append(jnp.exp((total - sums) - (rows - 1.0 - place) * rate))
    leaving = jnp.concatenate(to_start + to_end, axis=0)
    entering = jnp.concatenate(to_end + to_start, axis=0)
    return leaving, entering


def prepare_body(cot_hbm, keep_hbm, decay_hbm, pay_ref, cot_ref, keep_ref, decay_ref, sems):
    pairs = ((keep_hbm, keep_ref), (decay_hbm, decay_ref), (cot_hbm, cot_ref))
    copies = [pltpu.make_async_copy(source, to, sems.at[index]) for index, (source, to) in enumerate(pairs)]
    for copy in copies:
        copy.start()
    copies[0].wait()
    copies[1].wait()
    rows = keep_ref.shape[-1]
    _, sums, total = log_sums(keep_ref[...])
    weights, _ = mode_terms(sums, total, decay_ref, rows)
    high = weights.astype(BF16).astype(F32)
    both = jnp.concatenate([high, weights - high], axis=0).astype(BF16)
    width = cot_ref.shape[-1]
    first = jnp.broadcast_to(total, (8, 128))
    one = first.astype(BF16).astype(F32)
    two = (first - one).astype(BF16).astype(F32)
    three = first - one - two
    row = iota2((8, 128), 0)
    extra = jnp.where(row == 0, one, jnp.where(row == 1, two, jnp.where(row == 2, three, 0.0)))
    pay_ref[0, :, width:] = extra.astype(BF16)
    copies[2].wait()
    states = dot(both, cot_ref[0])
    pay_ref[0, :, :width] = (states[0:8] + states[8:16]).astype(BF16)


def assemble_body(down_ref, down_far_ref, tap_ref, tap_far_ref, down_out, tap_out):
    core = lax.axis_index("dp")
    half = down_ref.shape[1]
    for down, taps, side in ((down_ref, tap_ref, core), (down_far_ref, tap_far_ref, 1 - core)):
        part = pl.ds(pl.multiple_of(side * half, half), half)
        for layer in range(LAYERS):
            down_out[layer, part, :] = down[layer]
            total = taps[layer, 0].astype(F32) + taps[layer, 1].astype(F32) + taps[layer, 2].astype(F32)
            tap_out[layer, part, :] = total.astype(BF16)


def forward_body(
    feature_ref, count_ref, weight_ref, down_ref, tap_ref, up_ref, up_far_ref,
    stream_ref, inverse_ref, reduced_ref, slope_ref,
):
    core = lax.axis_index("dp")
    rows, width = feature_ref.shape[1:]
    logs = jnp.broadcast_to(jnp.log1p(count_ref[...].astype(F32)), (rows, rows))
    diagonal = iota2((rows, rows), 0) == iota2((rows, rows), 1)
    level = jnp.sum(jnp.where(diagonal, logs, 0.0), axis=1, keepdims=True)
    stream = feature_ref[0].astype(F32) + level * weight_ref[...]
    for layer in range(LAYERS):
        stream_ref[layer] = stream
        mean = jnp.sum(stream * stream, axis=-1, keepdims=True) * (1.0 / width)
        inverse = lax.rsqrt(mean + EPSILON)
        inverse_ref[layer] = inverse
        normed = (stream * inverse).astype(BF16)
        reduced = dot_nt(normed, down_ref[layer]).astype(BF16)
        reduced_ref[layer * rows : (layer + 1) * rows, :] = reduced
        mixture = dot_nt(reduced, tap_ref[layer])
        share = 0.5 * (1.0 + lax.erf(mixture * HALF_ROOT))
        slope_ref[layer] = share + mixture * jnp.exp(-0.5 * mixture * mixture) * DENSITY
        act = (mixture * share).astype(BF16)
        out_near = dot(act, up_ref[layer])
        out_away = dot(act, up_far_ref[layer])
        low = jnp.where(core == 0, out_near, out_away)
        high = jnp.where(core == 0, out_away, out_near)
        stream = stream + jnp.concatenate([low, high], axis=-1)
    stream_ref[LAYERS] = stream


def local_body(decay_ref, scale_ref, cot_ref, keep_ref, mode_ref, stream_ref, grad_ref, mark_ref, reach_ref, edge_ref, rate_ref):
    rows, width = cot_ref.shape[1:]
    column, row, total = log_sums(keep_ref[...])
    below = iota2((rows, rows), 0)
    across = iota2((rows, rows), 1)
    gap = column - row
    steps = (below - across).astype(F32)
    kernels = []
    for mode in range(M):
        value = jnp.exp(jnp.minimum(steps * decay_ref[mode] - gap, 0.0))
        kernels.append(jnp.where(across >= below, value, 0.0))
    for mode in range(M):
        value = jnp.exp(jnp.minimum(gap - steps * decay_ref[mode], 0.0))
        kernels.append(jnp.where(below >= across, value, 0.0))
    pairs = [jnp.concatenate(split_pair(kernel), axis=1) for kernel in kernels]
    _, edges = mode_terms(row, total, decay_ref, rows)
    high = edges.astype(BF16).astype(F32)
    both = jnp.concatenate([high, edges - high], axis=0).astype(BF16)
    edge_ref[...] = jnp.concatenate([high, high, edges - high, jnp.zeros_like(high)], axis=0).astype(BF16)
    row8 = iota2((8, 128), 0)
    for side, values_ref in enumerate((decay_ref, scale_ref)):
        value8 = jnp.zeros((8, 128), F32)
        for index in range(2 * M):
            value8 = jnp.where(row8 == index, values_ref[index % M], value8)
        rate_ref[side] = value8
    span = 256
    for start in range(0, width, span):
        part = slice(start, start + span)
        cot = cot_ref[0, :, part]
        doubled = jnp.concatenate([cot, cot], axis=0)
        stream = stream_ref[LAYERS, :, part]
        grad = cot.astype(F32)
        marks = []
        for index in range(2 * M):
            mode = index % M
            field = dot(pairs[index], doubled)
            gain = scale_ref[mode]
            grad = grad + (gain * mode_ref[index // M, mode : mode + 1, part]) * field
            marks.append(jnp.sum(stream * field, axis=0, keepdims=True))
        grad_ref[:, part] = grad
        mark_ref[:, part] = jnp.concatenate(marks, axis=0)
        near, away = split_pair(stream)
        reach = dot(both, near)
        reach_ref[:, part] = reach[0:8] + reach[8:16] + dot(both, away)[0:8]


def backward_body(
    first_ref, second_ref, third_ref, fourth_ref, mode_ref,
    local_ref, mark_ref, reach_ref, edge_ref, rate_ref, stream_ref, inverse_ref, slope_ref, down_ref, tap_ref, up_ref,
    up_far_ref, grads_ref, mixed_ref, partial_ref,
):
    core = lax.axis_index("dp")
    place = lax.axis_index("seq")
    rows, width = local_ref.shape
    wide = up_ref.shape[-1]

    masks = [0]
    for hop in (HOPS[0], HOPS[1] - core, HOPS[2] + core):
        masks = masks + [lax.bitwise_xor(mask, hop) for mask in masks]
    pieces = []
    for ref in (first_ref, second_ref, third_ref, fourth_ref):
        pieces = pieces + [ref[index].astype(F32) for index in range(ref.shape[0])]
    totals = jnp.concatenate([jnp.sum(piece[:, width:], axis=0, keepdims=True) for piece in pieces], axis=0)
    row8 = iota2((8, 128), 0)
    decay8 = rate_ref[0]
    gain8 = rate_ref[1, :, 0:1]
    everything = jnp.sum(totals, axis=0, keepdims=True)
    loop = 1.0 / (1.0 - jnp.exp(everything - (RING * rows) * decay8))
    spots = jnp.zeros((8, 128), jnp.int32)
    for index in range(RING):
        spots = jnp.where(row8 == index, lax.bitwise_xor(place, masks[index]), spots)
    ahead = lax.bitwise_and(place - spots + (RING - 1), RING - 1)
    after = lax.bitwise_and(spots - place + (RING - 1), RING - 1)
    entering = jnp.zeros((8, width), F32)
    for index in range(RING):
        here = slice(index, index + 1)
        fore = jnp.sum(jnp.where(ahead < ahead[here], totals, 0.0), axis=0, keepdims=True)
        back = jnp.sum(jnp.where(after < after[here], totals, 0.0), axis=0, keepdims=True)
        fore = fore - (ahead[here] * rows).astype(F32) * decay8
        back = back - (after[here] * rows).astype(F32) * decay8
        share = jnp.exp(jnp.where(row8 < M, back, fore)) * loop
        entering = entering + share[:, 0:1] * pieces[index][:, :width]
    whole = gain8 * (mark_ref[...] + entering * reach_ref[...])
    partial = jnp.concatenate([whole[:, :wide], whole[:, wide:]], axis=0)
    partial_ref[...] = partial
    high, low = split_pair(partial)
    mixed_ref[LAYERS * rows : LAYERS * rows + 16, :] = high
    mixed_ref[LAYERS * rows + 16 : LAYERS * rows + 32, :] = low
    weighted = entering * gain8 * jnp.concatenate([mode_ref[0], mode_ref[1]], axis=0)
    in_high = weighted.astype(BF16).astype(F32)
    in_low = weighted - in_high
    right = jnp.concatenate([in_high, in_low, in_high, jnp.zeros_like(in_high)], axis=0).astype(BF16)
    gradient = local_ref[...] + dot_tn(edge_ref[...], right)

    for layer in reversed(range(LAYERS)):
        narrow = gradient.astype(BF16)
        first, second = narrow[:, :wide], narrow[:, wide:]
        mine = jnp.where(core == 0, first, second)
        theirs = jnp.where(core == 0, second, first)
        back = dot_nt(mine, up_ref[layer]) + dot_nt(theirs, up_far_ref[layer])
        mixed = (back * slope_ref[layer]).astype(BF16)
        mixed_ref[layer * rows : (layer + 1) * rows, :] = mixed
        if layer:
            gradient = through_layer(layer, gradient, mixed, stream_ref, inverse_ref, down_ref, tap_ref)
    grads_ref[...] = gradient


def through_layer(layer, gradient, mixed, stream_ref, inverse_ref, down_ref, tap_ref):
    passed = dot(mixed, tap_ref[layer]).astype(BF16)
    normed = dot(passed, down_ref[layer])
    before = stream_ref[layer]
    inverse = inverse_ref[layer]
    shared = jnp.sum(normed * before, axis=-1, keepdims=True) * (1.0 / before.shape[-1])
    return gradient + inverse * normed - before * (inverse * inverse * inverse * shared)


def output_body(gradient_ref, mixed_ref, stream_ref, inverse_ref, down_ref, tap_ref, grad_ref):
    rows = gradient_ref.shape[0]
    mixed = mixed_ref[0:rows, :]
    gradient = through_layer(0, gradient_ref[...], mixed, stream_ref, inverse_ref, down_ref, tap_ref)
    grad_ref[0] = gradient.astype(BF16)


def held_block(parity, bit_x, bit_z, layer):
    core = lax.bitwise_xor(lax.bitwise_xor(parity, bit_x), lax.bitwise_xor(bit_z, layer))
    return pl.multiple_of(lax.rem(3 * core + 6 * bit_x + 4 * bit_z, RING) * BLOCK, BLOCK)


def taps_body(
    reduced_ref, reduced_far_ref, mixed_ref, mixed_far_ref, partial_ref,
    kept_ref, send_ref, partial_out, block_ref,
):
    bits, parity = position_bits()
    bit = pick(parity, bits[0], bits[1])
    rows = reduced_ref.shape[0] // LAYERS
    for layer in range(LAYERS):
        part = slice(layer * rows, (layer + 1) * rows)
        left = jnp.concatenate([reduced_ref[part, :], reduced_far_ref[part, :]], axis=0)
        right = jnp.concatenate([mixed_ref[part, :], mixed_far_ref[part, :]], axis=0)
        block_ref[layer] = dot_tn(left, right)
    kept_rows = kept_ref.shape[0]
    for turn in range(2):
        for layer in range(LAYERS):
            to = (2 * turn + layer) * BLOCK
            kept = held_block(parity, pick(parity, bit, turn), pick(parity, turn, bit), layer)
            sent = held_block(parity, pick(parity, 1 - bit, turn), pick(parity, turn, 1 - bit), layer)
            kept_ref[to : to + BLOCK, :] = block_ref[layer, pl.ds(kept, BLOCK), :]
            send_ref[to : to + BLOCK, :] = block_ref[layer, pl.ds(sent, BLOCK), :].astype(BF16)
    high = mixed_far_ref[LAYERS * rows : LAYERS * rows + 16, :].astype(F32)
    low = mixed_far_ref[LAYERS * rows + 16 : LAYERS * rows + 32, :].astype(F32)
    partial = partial_ref[...] + (high + low)
    partial_out[...] = partial
    send_ref[kept_rows : kept_rows + 16, :] = partial.astype(BF16)


def position_bits():
    place = lax.axis_index("seq")
    bits = [lax.rem(place // value, 2) for value in (1, 2, 4)]
    return bits, lax.rem(lax.axis_index("dp") + bits[0] + bits[1] + bits[2], 2)


def pick(parity, even, odd):
    return even + parity * (odd - even)


def join_body(stage, kept_ref, got_ref, partial_ref, kept_out, send_out, partial_out):
    rows = kept_out.shape[0]
    bits, parity = position_bits()
    bit = pick(parity, bits[1], bits[0]) if stage == 1 else bits[2]
    keep = pl.ds(pl.multiple_of(bit * rows, rows), rows)
    send = pl.ds(pl.multiple_of((1 - bit) * rows, rows), rows)
    kept_out[...] = kept_ref[keep, :] + got_ref[keep, :].astype(F32)
    send_out[0:rows, :] = (kept_ref[send, :] + got_ref[send, :].astype(F32)).astype(BF16)
    partial = partial_ref[...] + got_ref[2 * rows : 2 * rows + 16, :].astype(F32)
    if stage == 1:
        partial_out[...] = partial
        send_out[rows : rows + 16, :] = partial.astype(BF16)
    else:
        last = bits[2]
        partial_out[...] = jnp.where(last == 0, partial[0:8], partial[8:16])
        send_out[rows : rows + 8, :] = jnp.where(last == 0, partial[8:16], partial[0:8]).astype(BF16)


def finish_body(scale, kept_ref, got_ref, block_out, send_out):
    rows = kept_ref.shape[0]
    block = (kept_ref[...] + got_ref[0:rows, :].astype(F32)) * scale
    block_out[...] = block
    send_out[...] = block.astype(BF16)


def modes_body(scale, got_ref, partial_ref, mode_out):
    rows = got_ref.shape[0] - 8
    full = (partial_ref[...] + got_ref[rows : rows + 8, :].astype(F32)) * scale
    number = lax.rem(2 * lax.axis_index("seq") + lax.axis_index("dp"), 8)
    span = full.shape[1]
    mode_out[...] = pltpu.roll(full, lax.rem(span - BLOCK * number, span), 1)[:, 0:BLOCK]


def swap(value, axis, mask):
    count = lax.axis_size(axis)
    return lax.ppermute(value, axis, [(source, source ^ mask) for source in range(count)])


def hop_to(value, step):
    pairs = []
    for source in range(2 * lax.axis_size("seq")):
        flip, mask = step(source % 2, source // 2)
        pairs.append((source, source ^ (2 * mask + flip)))
    return lax.ppermute(value, ("seq", "dp"), pairs)


def class_of(core, place):
    return (core + place + place // 2 + place // 4) % 2


def wrapped_device(
    features, cotangent, counts, count_weight, down_weight, tap_weight, up_weight,
    decay_rate, keep_share, mode_weight,
):
    rows, width = features.shape[1:]
    down = jnp.swapaxes(down_weight, 1, 2)
    taps = jnp.swapaxes(tap_weight, 2, 3)
    down_far, up_far, taps_far = swap(down, "dp", 1), swap(up_weight, "dp", 1), swap(taps, "dp", 1)
    scale = jnp.sqrt(-jnp.expm1(-2.0 * decay_rate))
    (pay,) = call(
        prepare_body,
        tuple(pltpu.with_memory_space_constraint(value, HBM) for value in (cotangent, keep_share, decay_rate)),
        (HBM,) * 3,
        (((1, 8, width + 128), BF16),),
        (
            pltpu.VMEM(cotangent.shape, BF16),
            pltpu.VMEM(keep_share.shape, F32),
            pltpu.SMEM(decay_rate.shape, F32),
            pltpu.SemaphoreType.DMA((3,)),
        ),
        size=1300 * GIGA,
    )
    got = hop_to(pay, lambda core, place: (0, HOPS[0]))
    down_full, tap_full = call(
        assemble_body,
        (down, down_far, taps, taps_far),
        (VMEM,) * 4,
        (((LAYERS, B, width), BF16), ((LAYERS, B, B), BF16)), size=1200 * GIGA
    )
    two = jnp.concatenate([pay, got], axis=0)
    two, down_full, tap_full = lax.optimization_barrier((two, down_full, tap_full))
    got_two = hop_to(two, lambda core, place: (0, HOPS[1 + core]))
    stream, inverse, reduced, slope = call(
        forward_body,
        (features, counts, count_weight[None], down_full, tap_full, up_weight, up_far),
        (VMEM,) * 7,
        (
            ((LAYERS + 1, rows, width), F32),
            ((LAYERS, rows, 1), F32),
            ((LAYERS * rows, B), BF16),
            ((LAYERS, rows, B), F32),
        ), size=1800 * GIGA
    )
    four = jnp.concatenate([two, got_two], axis=0)
    four, stream, reduced = lax.optimization_barrier((four, stream, reduced))
    got_four = hop_to(four, lambda core, place: (0, HOPS[2 - core]))
    reduced_far = swap(reduced, "dp", 1)
    local, mark, reach, edge, rate = call(
        local_body,
        (decay_rate, scale, cotangent, keep_share, mode_weight, stream),
        (SMEM, SMEM) + (VMEM,) * 4,
        (((rows, width), F32), ((8, width), F32), ((8, width), F32), ((32, rows), BF16), ((2, 8, 128), F32)), size=1600 * GIGA
    )
    local, reduced_far = lax.optimization_barrier((local, reduced_far))
    gradient, mixed, partial = call(
        backward_body,
        (
            pay, got, got_two, got_four, mode_weight, local, mark, reach, edge, rate,
            stream, inverse, slope, down_full, tap_full, up_weight, up_far,
        ),
        (VMEM,) * 17,
        (((rows, width), F32), ((LAYERS * rows + 32, B), BF16), ((16, B), F32)), size=2100 * GIGA
    )
    mixed_far = swap(mixed, "dp", 1)
    (grad,) = call(
        output_body,
        (gradient, mixed, stream, inverse, down_full, tap_full),
        (VMEM,) * 6,
        (((1, rows, width), BF16),), size=1300 * GIGA
    )
    kept_rows = RING * BLOCK // 2
    kept, send, partial = call(
        taps_body,
        (reduced, reduced_far, mixed, mixed_far, partial),
        (VMEM,) * 5,
        (((kept_rows, B), F32), ((kept_rows + 16, B), BF16), ((16, B), F32)),
        (pltpu.VMEM((LAYERS, B, B), F32),), size=500 * GIGA
    )
    got = hop_to(send, lambda core, place: (1, 1 + class_of(core, place)))
    for stage in (1, 2):
        kept_rows = kept.shape[0] // 2
        mode_rows = (16, 8)[stage - 1]
        kept, send, partial = call(
            functools.partial(join_body, stage),
            (kept, got, partial),
            (VMEM,) * 3,
            (((kept_rows, B), F32), ((kept_rows + mode_rows, B), BF16), ((mode_rows, B), F32)),
        )
        if stage == 1:
            send, grad = lax.optimization_barrier((send, grad))
        if stage == 1:
            got = hop_to(send, lambda core, place: (1, 2 - class_of(core, place)))
        else:
            got = hop_to(send, lambda core, place: (1, 4))
    total = features.shape[0] * lax.axis_size("dp") * rows * lax.axis_size("seq")
    report = 1.0 / math.sqrt(total)
    block, narrow = call(
        functools.partial(finish_body, report),
        (kept, got),
        (VMEM,) * 2,
        (((BLOCK, B), F32), ((BLOCK, B), BF16)),
    )
    parts = [block]
    for step in (3, 6):
        pairs = [(8 * layer + (j + step) % 8, 8 * layer + j) for layer in range(LAYERS) for j in range(8)]
        parts.append(lax.ppermute(narrow, ("seq", "dp"), pairs).astype(F32))
    (mode_sum,) = call(
        functools.partial(modes_body, report), (got, partial), (VMEM,) * 2, (((8, BLOCK), F32),)
    )
    return grad, jnp.concatenate(parts, axis=0), mode_sum


def solution(mesh):
    placed = (
        P(("parts", "dp"), "seq", None),
        P(("parts", "dp"), "seq", None),
        P(("parts", "dp"), "seq"),
        P(),
        P(None, None, "dp"),
        P(None, None, None, "dp"),
        P(None, None, "dp"),
        P(),
        P(("parts", "dp"), "seq"),
        P(),
    )

    def per_device(*operands):
        rows = operands[0].shape[1]
        ring = lax.axis_size("seq")
        loop = ring * rows
        wraps = all(dilation % loop == 0 for dilation in (DILATION_FIRST1, DILATION_SECOND2))
        fits = ring == RING and lax.axis_size("dp") == 2 and operands[0].shape[0] == 1
        return (wrapped_device if wraps and fits else general_device)(*operands)

    return jax.shard_map(
        per_device,
        mesh=mesh,
        in_specs=placed,
        out_specs=(
            P(("parts", "dp"), "seq", None),
            P(("parts", "seq", "dp"), None),
            P("parts", ("seq", "dp")),
        ),
        check_vma=False,
    )
```

```python
import functools
import math

import jax
import jax.numpy as jnp
from jax import lax
from jax.experimental import pallas as pl
from jax.experimental.pallas import tpu as pltpu
from jax.sharding import PartitionSpec as P

B = 384
DILATION_FIRST1 = 2048
DILATION_SECOND2 = 4096
M = 4
LAYERS = 2


EPSILON = 1e-06
HALF_ROOT = 1.0 / math.sqrt(2.0)
DENSITY = 1.0 / math.sqrt(2.0 * math.pi)
TOP_PRECISION = lax.Precision.HIGHEST


def shifted(value, axis, steps):
    count = lax.axis_size(axis)
    pairs = [(source, (source + steps) % count) for source in range(count)]
    return lax.ppermute(value, axis, pairs)


def entering_2(shard, axis, join, neutral, backward):
    count = lax.axis_size(axis)
    place = lax.axis_index(axis)
    ahead = count - 1 - place if backward else place
    gathered = jax.tree.map(
        lambda a, kind: lax.all_gather(a.astype(kind), axis),
        shard,
        jax.tree.map(lambda a: jnp.bfloat16 if a.dtype == jnp.float32 else a.dtype, shard),
    )
    state = jax.tree.map(lambda a, e: jnp.zeros_like(a) + jnp.asarray(e, a.dtype), shard, neutral)

    def one(turn, state):
        source = count - 1 - turn if backward else turn
        return join(
            state,
            jax.tree.map(
                lambda a, own: lax.dynamic_index_in_dim(a, source, 0, False).astype(own.dtype),
                gathered,
                shard,
            ),
        )

    return lax.fori_loop(0, ahead, one, state)


def gelu_exact(values):
    return 0.5 * values * (1.0 + lax.erf(values * HALF_ROOT))


def gelu_slope(values):
    cumulative = 0.5 * (1.0 + lax.erf(values * HALF_ROOT))
    return cumulative + values * jnp.exp(-0.5 * values * values) * DENSITY


def project(left_shifted, right_shifted):
    return jnp.einsum(
        "qra,au->qru", left_shifted, right_shifted, preferred_element_type=jnp.float32
    )


def project_back(left_shifted, right_shifted):
    return jnp.einsum(
        "kut,st->kus", left_shifted, right_shifted, preferred_element_type=jnp.float32
    )


def contract(left_shifted, right_shifted):
    return jnp.einsum(
        "glb,glk->bk", left_shifted, right_shifted, preferred_element_type=jnp.float32
    )


def moved(values, bin_distance):
    return shifted(values, "seq", bin_distance)


def block_product(kernel, pieces):
    return jnp.einsum(
        "gmbij,gbjc->gmbic",
        kernel,
        pieces,
        precision=TOP_PRECISION,
        preferred_element_type=jnp.float32,
    )


def modal_local(lg_in, lg_exit, stream_rows, cotangent_rows):
    genome_count, input_rows, mode_count = lg_in.shape
    feature_maps = stream_rows.shape[-1]
    block_size = min(128, input_rows)
    block_count = input_rows // block_size
    running = jnp.cumsum(lg_in, axis=1)
    running_blocks = running.reshape(genome_count, block_count, block_size, mode_count)
    block_ends = running_blocks[:, :, -1, :]
    block_starts = jnp.concatenate(
        [jnp.zeros((genome_count, 1, mode_count), jnp.float32), block_ends[:, :-1, :]], axis=1
    )
    within = running_blocks - block_starts[:, :, None, :]
    within_t = jnp.transpose(within, (0, 3, 1, 2))
    spread = within_t[..., :, None] - within_t[..., None, :]
    row_index = lax.broadcasted_iota(jnp.int32, (block_size, block_size), 0)
    column_index = lax.broadcasted_iota(jnp.int32, (block_size, block_size), 1)
    kernel = jnp.where(row_index >= column_index, jnp.exp(jnp.minimum(spread, 0.0)), 0.0)
    joined_source = jnp.concatenate([stream_rows, cotangent_rows.astype(jnp.float32)], axis=-1)
    joined_source = joined_source.reshape(genome_count, block_count, block_size, 2 * feature_maps)
    partial_value = block_product(kernel, joined_source)
    block_tails = partial_value[:, :, :, -1, :]
    ends_t = jnp.transpose(block_ends, (0, 2, 1))
    starts_t = jnp.transpose(block_starts, (0, 2, 1))
    spacing = starts_t[..., :, None] - ends_t[..., None, :]
    block_index = lax.broadcasted_iota(jnp.int32, (block_count, block_count), 0)
    source_index = lax.broadcasted_iota(jnp.int32, (block_count, block_count), 1)
    linkage = jnp.where(source_index < block_index, jnp.exp(jnp.minimum(spacing, 0.0)), 0.0)
    entering = jnp.einsum(
        "gmbk,gmkc->gmbc",
        linkage,
        block_tails,
        precision=TOP_PRECISION,
        preferred_element_type=jnp.float32,
    )
    states = partial_value + jnp.exp(within_t)[..., None] * entering[:, :, :, None, :]
    states = states.reshape(genome_count, mode_count, input_rows, 2 * feature_maps)
    decay_values = jnp.exp(jnp.transpose(running, (0, 2, 1)))
    exit_state = jnp.exp(lg_exit)[..., None] * states[:, :, -1, :]
    log_pass = running[:, -1, :] + lg_exit
    return (states, decay_values, exit_state, log_pass)


def modal_terms(states, decay_values, entering, cotangent_rows, source_gain, cot_gain):
    feature_maps = cotangent_rows.shape[-1]
    reach_sum = jnp.einsum(
        "qsz,qzj->qsj",
        decay_values,
        cotangent_rows,
        precision=TOP_PRECISION,
        preferred_element_type=jnp.float32,
    )
    totals = jnp.einsum(
        "veyi,vyi->ei",
        states[..., :feature_maps],
        cotangent_rows,
        precision=TOP_PRECISION,
        preferred_element_type=jnp.float32,
    )
    totals = totals + jnp.sum(entering[..., :feature_maps] * reach_sum, axis=0)
    rows_out = jnp.einsum(
        "jryf,rf->jyf",
        states[..., feature_maps:],
        cot_gain,
        precision=TOP_PRECISION,
        preferred_element_type=jnp.float32,
    )
    rows_out = rows_out + jnp.einsum(
        "ert,erx->etx",
        decay_values,
        entering[..., feature_maps:] * cot_gain[None],
        precision=TOP_PRECISION,
        preferred_element_type=jnp.float32,
    )
    return (source_gain[:, None] * totals, rows_out)


def apply_early_first(early_pass, early_state, late_pass, late_state):
    return (early_pass * late_pass, late_pass[..., None] * early_state + late_state)


def apply_late_first(early_pass, early_state, late_pass, late_state):
    return (early_pass * late_pass, early_pass[..., None] * late_state + early_state)


def join_lower(early, late):
    fore_pass, fore_state = apply_early_first(early[0], early[1], late[0], late[1])
    back_pass, back_state = apply_late_first(early[2], early[3], late[2], late[3])
    return (fore_pass, fore_state, back_pass, back_state)


def join_upper(early, late):
    fore_pass, fore_state = apply_late_first(early[0], early[1], late[0], late[1])
    back_pass, back_state = apply_early_first(early[2], early[3], late[2], late[3])
    return (fore_pass, fore_state, back_pass, back_state)


def closed(own_pass, own_state, pass_before, state_before, pass_after, state_after):
    beside_all = pass_before * pass_after
    numerator = (
        beside_all[..., None] * own_state + pass_before[..., None] * state_after + state_before
    )
    return numerator / (1.0 - beside_all * own_pass)[..., None]


def general_device(
    features,
    cotangent,
    counts,
    count_weight,
    down_weight,
    tap_weight,
    up_weight,
    decay_rate,
    keep_share,
    mode_weight,
):
    genome_count = features.shape[0]
    input_rows = features.shape[1]
    down_full, tap_full, full_up_weight = (
        lax.all_gather(down_weight, "dp", axis=2, tiled=True),
        lax.all_gather(tap_weight, "dp", axis=3, tiled=True),
        lax.all_gather(up_weight, "dp", axis=2, tiled=True),
    )
    stream = (
        features.astype(jnp.float32)
        + jnp.log1p(counts.astype(jnp.float32))[..., None] * count_weight
    )
    stored = []
    for layer_position in range(LAYERS):
        bin_distance = (DILATION_FIRST1 if layer_position == 0 else DILATION_SECOND2) // input_rows
        inverse = lax.rsqrt(jnp.mean(stream * stream, axis=-1, keepdims=True) + EPSILON)
        normed = (stream * inverse).astype(jnp.bfloat16)
        reduced = project(normed, down_full[layer_position]).astype(jnp.bfloat16)
        lagged = moved(reduced, bin_distance)
        advanced = moved(reduced, -bin_distance)
        mixture = (
            project(lagged, tap_full[layer_position, 0])
            + project(reduced, tap_full[layer_position, 1])
            + project(advanced, tap_full[layer_position, 2])
        )
        active_modes = gelu_exact(mixture).astype(jnp.bfloat16)
        stored.append((stream, inverse, reduced, lagged, advanced, mixture))
        stream = stream + jnp.einsum(
            "quy,yk->quk",
            active_modes,
            full_up_weight[layer_position],
            preferred_element_type=jnp.float32,
        )
    cot_wide = cotangent.astype(jnp.float32)
    logs = jnp.log(keep_share)[:, :, None] - decay_rate[None, None, :]
    mode_scale = jnp.sqrt(-jnp.expm1(-2.0 * decay_rate))
    fore_states, fore_decays, fore_exit, fore_log = modal_local(
        logs, jnp.zeros_like(logs[:, 0, :]), stream, cotangent
    )
    back_logs = jnp.concatenate(
        [jnp.zeros_like(logs[:, :1, :]), logs[:, ::-1, :][:, :-1, :]], axis=1
    )
    back_states, back_decays, back_exit, back_log = modal_local(
        back_logs, logs[:, 0, :], stream[:, ::-1, :], cotangent[:, ::-1, :]
    )
    summary = (jnp.exp(fore_log), fore_exit, jnp.exp(back_log), back_exit)
    identity = (
        jnp.ones_like(fore_log),
        jnp.zeros_like(fore_exit),
        jnp.ones_like(back_log),
        jnp.zeros_like(back_exit),
    )
    from_lower = entering_2(summary, "seq", join_lower, identity, False)
    from_upper = entering_2(summary, "seq", join_upper, identity, True)
    fore_entry = closed(
        summary[0], summary[1], from_lower[0], from_lower[1], from_upper[0], from_upper[1]
    )
    back_entry = closed(
        summary[2], summary[3], from_upper[2], from_upper[3], from_lower[2], from_lower[3]
    )
    fore_totals, fore_rows = modal_terms(
        fore_states,
        fore_decays,
        fore_entry,
        cot_wide,
        mode_scale,
        mode_scale[:, None] * mode_weight[1],
    )
    back_totals, back_rows = modal_terms(
        back_states,
        back_decays,
        back_entry,
        cot_wide[:, ::-1, :],
        mode_scale,
        mode_scale[:, None] * mode_weight[0],
    )
    gradient = cot_wide + fore_rows + back_rows[:, ::-1, :]
    mode_terms = jnp.stack([fore_totals, back_totals]).reshape(2 * M, -1)
    tap_terms = []
    for layer_position in reversed(range(LAYERS)):
        bin_distance = (DILATION_FIRST1 if layer_position == 0 else DILATION_SECOND2) // input_rows
        before, inverse, reduced, lagged, advanced, mixture = stored[layer_position]
        narrow_width = gradient.astype(jnp.bfloat16)
        back_mixed = jnp.einsum(
            "yhi,ai->yha",
            narrow_width,
            full_up_weight[layer_position],
            preferred_element_type=jnp.float32,
        )
        mixed_grad = (back_mixed * gelu_slope(mixture)).astype(jnp.bfloat16)
        tap_terms.insert(
            0,
            jnp.stack(
                [
                    contract(lagged, mixed_grad),
                    contract(reduced, mixed_grad),
                    contract(advanced, mixed_grad),
                ]
            ),
        )
        reduced_grad = jnp.einsum(
            "glk,bk->glb",
            mixed_grad,
            tap_full[layer_position, 1],
            preferred_element_type=jnp.float32,
        )
        reduced_grad = reduced_grad + jnp.einsum(
            "glk,bk->glb",
            moved(mixed_grad, -bin_distance),
            tap_full[layer_position, 0],
            preferred_element_type=jnp.float32,
        )
        reduced_grad = reduced_grad + jnp.einsum(
            "glk,bk->glb",
            moved(mixed_grad, bin_distance),
            tap_full[layer_position, 2],
            preferred_element_type=jnp.float32,
        )
        normed_grad = project_back(reduced_grad.astype(jnp.bfloat16), down_full[layer_position])
        gradient = (
            gradient
            + inverse * normed_grad
            - before
            * inverse
            * inverse
            * inverse
            * jnp.mean(normed_grad * before, axis=-1, keepdims=True)
        )
    tap_flat = jnp.stack(tap_terms).reshape(LAYERS * 3 * B, B)
    seq_size = lax.axis_size("seq")
    dp_size = lax.axis_size("dp")
    report_scale = 1.0 / math.sqrt(genome_count * dp_size * input_rows * seq_size)
    tap_sum, mode_sum = (
        lax.psum_scatter(tap_flat, ("seq", "dp"), scatter_dimension=0, tiled=True),
        lax.psum_scatter(mode_terms, ("seq", "dp"), scatter_dimension=1, tiled=True),
    )
    return (gradient.astype(jnp.bfloat16), tap_sum * report_scale, mode_sum * report_scale)


VMEM = pltpu.MemorySpace.VMEM
SMEM = pltpu.MemorySpace.SMEM
HBM = pltpu.MemorySpace.HBM
F32 = jnp.float32
BF16 = jnp.bfloat16
RING = 8
HOPS = (4, 2, 1)
BLOCK = 48
OWNED = (0, 5, 7, 3, 4, 1, 2, 6)
SOURCES = ((6, 3, 7, 5, 1, 0, 4, 2), (5, 4, 0, 6, 7, 2, 3, 1))
GIGA = 10**6


def call(body, operands, spaces, outs, scratch=(), size=0):
    return pl.pallas_call(
        body,
        out_shape=[jax.ShapeDtypeStruct(shape, dtype) for shape, dtype in outs],
        in_specs=[pl.BlockSpec(memory_space=space) for space in spaces],
        out_specs=[pl.BlockSpec(memory_space=VMEM) for _ in outs],
        scratch_shapes=list(scratch),
        cost_estimate=pl.CostEstimate(flops=size, transcendentals=0, bytes_accessed=size // 256) if size else None,
        compiler_params=pltpu.CompilerParams(vmem_limit_bytes=40 * 1024 * 1024),
    )(*operands)


def dot(left, right):
    return lax.dot_general(left, right, (((1,), (0,)), ((), ())), preferred_element_type=F32)


def dot_nt(left, right):
    return lax.dot_general(left, right, (((1,), (1,)), ((), ())), preferred_element_type=F32)


def dot_tn(left, right):
    return lax.dot_general(left, right, (((0,), (0,)), ((), ())), preferred_element_type=F32)


def iota2(shape, axis):
    return lax.broadcasted_iota(jnp.int32, shape, axis)


def split_pair(value):
    high = value.astype(BF16)
    return high, (value - high.astype(F32)).astype(BF16)


def log_sums(keep_row):
    rows = keep_row.shape[-1]
    below, beside = iota2((rows, rows), 0), iota2((rows, rows), 1)
    logs = jnp.broadcast_to(jnp.log(keep_row), (rows, rows))
    column = jnp.sum(jnp.where(beside <= below, logs, 0.0), axis=1, keepdims=True)
    spread = jnp.broadcast_to(column, (rows, rows))
    row = jnp.sum(jnp.where(beside == below, spread, 0.0), axis=0, keepdims=True)
    return column, row, column[rows - 1 :, :]


def mode_terms(sums, total, decay_ref, rows):
    place = iota2((1, rows), 1).astype(F32)
    to_start, to_end = [], []
    for mode in range(M):
        rate = decay_ref[mode]
        to_start.append(jnp.exp(sums - (place + 1.0) * rate))
        to_end.append(jnp.exp((total - sums) - (rows - 1.0 - place) * rate))
    leaving = jnp.concatenate(to_start + to_end, axis=0)
    entering = jnp.concatenate(to_end + to_start, axis=0)
    return leaving, entering


def prepare_body(cot_hbm, keep_hbm, decay_hbm, pay_ref, cot_ref, keep_ref, decay_ref, sems):
    pairs = ((keep_hbm, keep_ref), (decay_hbm, decay_ref), (cot_hbm, cot_ref))
    copies = [pltpu.make_async_copy(source, to, sems.at[index]) for index, (source, to) in enumerate(pairs)]
    for copy in copies:
        copy.start()
    copies[0].wait()
    copies[1].wait()
    rows = keep_ref.shape[-1]
    _, sums, total = log_sums(keep_ref[...])
    weights, _ = mode_terms(sums, total, decay_ref, rows)
    high = weights.astype(BF16).astype(F32)
    both = jnp.concatenate([high, weights - high], axis=0).astype(BF16)
    width = cot_ref.shape[-1]
    first = jnp.broadcast_to(total, (8, 128))
    one = first.astype(BF16).astype(F32)
    two = (first - one).astype(BF16).astype(F32)
    three = first - one - two
    row = iota2((8, 128), 0)
    extra = jnp.where(row == 0, one, jnp.where(row == 1, two, jnp.where(row == 2, three, 0.0)))
    pay_ref[0, :, width:] = extra.astype(BF16)
    copies[2].wait()
    states = dot(both, cot_ref[0])
    pay_ref[0, :, :width] = (states[0:8] + states[8:16]).astype(BF16)


def assemble_body(down_ref, down_far_ref, tap_ref, tap_far_ref, down_out, tap_out):
    core = lax.axis_index("dp")
    half = down_ref.shape[1]
    for down, taps, side in ((down_ref, tap_ref, core), (down_far_ref, tap_far_ref, 1 - core)):
        part = pl.ds(pl.multiple_of(side * half, half), half)
        for layer in range(LAYERS):
            down_out[layer, part, :] = down[layer]
            total = taps[layer, 0].astype(F32) + taps[layer, 1].astype(F32) + taps[layer, 2].astype(F32)
            tap_out[layer, part, :] = total.astype(BF16)


def forward_body(
    feature_ref, count_ref, weight_ref, down_ref, tap_ref, up_ref, up_far_ref,
    stream_ref, inverse_ref, reduced_ref, slope_ref,
):
    core = lax.axis_index("dp")
    rows, width = feature_ref.shape[1:]
    logs = jnp.broadcast_to(jnp.log1p(count_ref[...].astype(F32)), (rows, rows))
    diagonal = iota2((rows, rows), 0) == iota2((rows, rows), 1)
    level = jnp.sum(jnp.where(diagonal, logs, 0.0), axis=1, keepdims=True)
    stream = feature_ref[0].astype(F32) + level * weight_ref[...]
    for layer in range(LAYERS):
        stream_ref[layer] = stream
        mean = jnp.sum(stream * stream, axis=-1, keepdims=True) * (1.0 / width)
        inverse = lax.rsqrt(mean + EPSILON)
        inverse_ref[layer] = inverse
        normed = (stream * inverse).astype(BF16)
        reduced = dot_nt(normed, down_ref[layer]).astype(BF16)
        reduced_ref[layer * rows : (layer + 1) * rows, :] = reduced
        mixture = dot_nt(reduced, tap_ref[layer])
        share = 0.5 * (1.0 + lax.erf(mixture * HALF_ROOT))
        slope_ref[layer] = share + mixture * jnp.exp(-0.5 * mixture * mixture) * DENSITY
        act = (mixture * share).astype(BF16)
        out_near = dot(act, up_ref[layer])
        out_away = dot(act, up_far_ref[layer])
        low = jnp.where(core == 0, out_near, out_away)
        high = jnp.where(core == 0, out_away, out_near)
        stream = stream + jnp.concatenate([low, high], axis=-1)
    stream_ref[LAYERS] = stream


def local_body(decay_ref, scale_ref, cot_ref, keep_ref, mode_ref, stream_ref, grad_ref, mark_ref, reach_ref, edge_ref, rate_ref):
    rows, width = cot_ref.shape[1:]
    column, row, total = log_sums(keep_ref[...])
    below = iota2((rows, rows), 0)
    across = iota2((rows, rows), 1)
    gap = column - row
    steps = (below - across).astype(F32)
    kernels = []
    for mode in range(M):
        value = jnp.exp(jnp.minimum(steps * decay_ref[mode] - gap, 0.0))
        kernels.append(jnp.where(across >= below, value, 0.0))
    for mode in range(M):
        value = jnp.exp(jnp.minimum(gap - steps * decay_ref[mode], 0.0))
        kernels.append(jnp.where(below >= across, value, 0.0))
    pairs = [jnp.concatenate(split_pair(kernel), axis=1) for kernel in kernels]
    _, edges = mode_terms(row, total, decay_ref, rows)
    high = edges.astype(BF16).astype(F32)
    both = jnp.concatenate([high, edges - high], axis=0).astype(BF16)
    edge_ref[...] = jnp.concatenate([high, high, edges - high, jnp.zeros_like(high)], axis=0).astype(BF16)
    row8 = iota2((8, 128), 0)
    for side, values_ref in enumerate((decay_ref, scale_ref)):
        value8 = jnp.zeros((8, 128), F32)
        for index in range(2 * M):
            value8 = jnp.where(row8 == index, values_ref[index % M], value8)
        rate_ref[side] = value8
    span = 256
    for start in range(0, width, span):
        part = slice(start, start + span)
        cot = cot_ref[0, :, part]
        doubled = jnp.concatenate([cot, cot], axis=0)
        stream = stream_ref[LAYERS, :, part]
        grad = cot.astype(F32)
        marks = []
        for index in range(2 * M):
            mode = index % M
            field = dot(pairs[index], doubled)
            gain = scale_ref[mode]
            grad = grad + (gain * mode_ref[index // M, mode : mode + 1, part]) * field
            marks.append(jnp.sum(stream * field, axis=0, keepdims=True))
        grad_ref[:, part] = grad
        mark_ref[:, part] = jnp.concatenate(marks, axis=0)
        near, away = split_pair(stream)
        reach = dot(both, near)
        reach_ref[:, part] = reach[0:8] + reach[8:16] + dot(both, away)[0:8]


def backward_body(
    first_ref, second_ref, third_ref, fourth_ref, mode_ref,
    local_ref, mark_ref, reach_ref, edge_ref, rate_ref, stream_ref, inverse_ref, slope_ref, down_ref, tap_ref, up_ref,
    up_far_ref, grads_ref, mixed_ref, partial_ref,
):
    core = lax.axis_index("dp")
    place = lax.axis_index("seq")
    rows, width = local_ref.shape
    wide = up_ref.shape[-1]

    masks = [0]
    for hop in (HOPS[0], HOPS[1] - core, HOPS[2] + core):
        masks = masks + [lax.bitwise_xor(mask, hop) for mask in masks]
    pieces = []
    for ref in (first_ref, second_ref, third_ref, fourth_ref):
        pieces = pieces + [ref[index].astype(F32) for index in range(ref.shape[0])]
    totals = jnp.concatenate([jnp.sum(piece[:, width:], axis=0, keepdims=True) for piece in pieces], axis=0)
    row8 = iota2((8, 128), 0)
    decay8 = rate_ref[0]
    gain8 = rate_ref[1, :, 0:1]
    everything = jnp.sum(totals, axis=0, keepdims=True)
    loop = 1.0 / (1.0 - jnp.exp(everything - (RING * rows) * decay8))
    spots = jnp.zeros((8, 128), jnp.int32)
    for index in range(RING):
        spots = jnp.where(row8 == index, lax.bitwise_xor(place, masks[index]), spots)
    ahead = lax.bitwise_and(place - spots + (RING - 1), RING - 1)
    after = lax.bitwise_and(spots - place + (RING - 1), RING - 1)
    entering = jnp.zeros((8, width), F32)
    for index in range(RING):
        here = slice(index, index + 1)
        fore = jnp.sum(jnp.where(ahead < ahead[here], totals, 0.0), axis=0, keepdims=True)
        back = jnp.sum(jnp.where(after < after[here], totals, 0.0), axis=0, keepdims=True)
        fore = fore - (ahead[here] * rows).astype(F32) * decay8
        back = back - (after[here] * rows).astype(F32) * decay8
        share = jnp.exp(jnp.where(row8 < M, back, fore)) * loop
        entering = entering + share[:, 0:1] * pieces[index][:, :width]
    whole = gain8 * (mark_ref[...] + entering * reach_ref[...])
    partial = jnp.concatenate([whole[:, :wide], whole[:, wide:]], axis=0)
    partial_ref[...] = partial
    high, low = split_pair(partial)
    mixed_ref[LAYERS * rows : LAYERS * rows + 16, :] = high
    mixed_ref[LAYERS * rows + 16 : LAYERS * rows + 32, :] = low
    weighted = entering * gain8 * jnp.concatenate([mode_ref[0], mode_ref[1]], axis=0)
    in_high = weighted.astype(BF16).astype(F32)
    in_low = weighted - in_high
    right = jnp.concatenate([in_high, in_low, in_high, jnp.zeros_like(in_high)], axis=0).astype(BF16)
    gradient = local_ref[...] + dot_tn(edge_ref[...], right)

    for layer in reversed(range(LAYERS)):
        narrow = gradient.astype(BF16)
        first, second = narrow[:, :wide], narrow[:, wide:]
        mine = jnp.where(core == 0, first, second)
        theirs = jnp.where(core == 0, second, first)
        back = dot_nt(mine, up_ref[layer]) + dot_nt(theirs, up_far_ref[layer])
        mixed = (back * slope_ref[layer]).astype(BF16)
        mixed_ref[layer * rows : (layer + 1) * rows, :] = mixed
        if layer:
            gradient = through_layer(layer, gradient, mixed, stream_ref, inverse_ref, down_ref, tap_ref)
    grads_ref[...] = gradient


def through_layer(layer, gradient, mixed, stream_ref, inverse_ref, down_ref, tap_ref):
    passed = dot(mixed, tap_ref[layer]).astype(BF16)
    normed = dot(passed, down_ref[layer])
    before = stream_ref[layer]
    inverse = inverse_ref[layer]
    shared = jnp.sum(normed * before, axis=-1, keepdims=True) * (1.0 / before.shape[-1])
    return gradient + inverse * normed - before * (inverse * inverse * inverse * shared)


def output_body(gradient_ref, mixed_ref, stream_ref, inverse_ref, down_ref, tap_ref, grad_ref):
    rows = gradient_ref.shape[0]
    mixed = mixed_ref[0:rows, :]
    gradient = through_layer(0, gradient_ref[...], mixed, stream_ref, inverse_ref, down_ref, tap_ref)
    grad_ref[0] = gradient.astype(BF16)


def entry_of(table, index):
    packed = sum(value << (3 * place) for place, value in enumerate(table))
    return lax.bitwise_and(lax.shift_right_logical(jnp.int32(packed), jnp.int32(3) * index), jnp.int32(7))


def held_block(parity, bit_x, bit_z, layer):
    core = lax.bitwise_xor(lax.bitwise_xor(parity, bit_x), lax.bitwise_xor(bit_z, layer))
    return pl.multiple_of(entry_of(OWNED, 4 * bit_z + 2 * bit_x + core) * BLOCK, BLOCK)


def taps_body(
    reduced_ref, reduced_far_ref, mixed_ref, mixed_far_ref, partial_ref,
    kept_ref, send_ref, partial_out, block_ref,
):
    bits, parity = position_bits()
    bit = pick(parity, bits[0], bits[1])
    rows = reduced_ref.shape[0] // LAYERS
    for layer in range(LAYERS):
        part = slice(layer * rows, (layer + 1) * rows)
        left = jnp.concatenate([reduced_ref[part, :], reduced_far_ref[part, :]], axis=0)
        right = jnp.concatenate([mixed_ref[part, :], mixed_far_ref[part, :]], axis=0)
        block_ref[layer] = dot_tn(left, right)
    kept_rows = kept_ref.shape[0]
    for turn in range(2):
        for layer in range(LAYERS):
            to = (2 * turn + layer) * BLOCK
            kept = held_block(parity, pick(parity, bit, turn), pick(parity, turn, bit), layer)
            sent = held_block(parity, pick(parity, 1 - bit, turn), pick(parity, turn, 1 - bit), layer)
            kept_ref[to : to + BLOCK, :] = block_ref[layer, pl.ds(kept, BLOCK), :]
            send_ref[to : to + BLOCK, :] = block_ref[layer, pl.ds(sent, BLOCK), :].astype(BF16)
    high = mixed_far_ref[LAYERS * rows : LAYERS * rows + 16, :].astype(F32)
    low = mixed_far_ref[LAYERS * rows + 16 : LAYERS * rows + 32, :].astype(F32)
    partial = partial_ref[...] + (high + low)
    partial_out[...] = partial
    send_ref[kept_rows : kept_rows + 16, :] = partial.astype(BF16)


def position_bits():
    place = lax.axis_index("seq")
    bits = [lax.rem(place // value, 2) for value in (1, 2, 4)]
    return bits, lax.rem(lax.axis_index("dp") + bits[0] + bits[1] + bits[2], 2)


def pick(parity, even, odd):
    return even + parity * (odd - even)


def join_body(stage, kept_ref, got_ref, partial_ref, kept_out, send_out, partial_out):
    rows = kept_out.shape[0]
    bits, parity = position_bits()
    bit = pick(parity, bits[1], bits[0]) if stage == 1 else bits[2]
    keep = pl.ds(pl.multiple_of(bit * rows, rows), rows)
    send = pl.ds(pl.multiple_of((1 - bit) * rows, rows), rows)
    kept_out[...] = kept_ref[keep, :] + got_ref[keep, :].astype(F32)
    send_out[0:rows, :] = (kept_ref[send, :] + got_ref[send, :].astype(F32)).astype(BF16)
    partial = partial_ref[...] + got_ref[2 * rows : 2 * rows + 16, :].astype(F32)
    if stage == 1:
        partial_out[...] = partial
        send_out[rows : rows + 16, :] = partial.astype(BF16)
    else:
        last = bits[2]
        partial_out[...] = jnp.where(last == 0, partial[0:8], partial[8:16])
        send_out[rows : rows + 8, :] = jnp.where(last == 0, partial[8:16], partial[0:8]).astype(BF16)


def finish_body(scale, kept_ref, got_ref, block_out, send_out):
    rows = kept_ref.shape[0]
    block = (kept_ref[...] + got_ref[0:rows, :].astype(F32)) * scale
    block_out[...] = block
    send_out[...] = block.astype(BF16)


def place_body(own_ref, first_ref, second_ref, out_ref):
    number = lax.rem(2 * lax.axis_index("seq") + lax.axis_index("dp"), 8)
    held = (range(8),) + SOURCES
    for table, ref in zip(held, (own_ref, first_ref, second_ref)):
        spots = [(OWNED[table[j]] - 3 * j) % 8 for j in range(8)]
        out_ref[pl.ds(pl.multiple_of(entry_of(spots, number) * BLOCK, BLOCK), BLOCK), :] = ref[...].astype(F32)


def modes_body(scale, got_ref, partial_ref, mode_out):
    rows = got_ref.shape[0] - 8
    full = (partial_ref[...] + got_ref[rows : rows + 8, :].astype(F32)) * scale
    number = lax.rem(2 * lax.axis_index("seq") + lax.axis_index("dp"), 8)
    span = full.shape[1]
    mode_out[...] = pltpu.roll(full, lax.rem(span - BLOCK * number, span), 1)[:, 0:BLOCK]


def swap(value, axis, mask):
    count = lax.axis_size(axis)
    return lax.ppermute(value, axis, [(source, source ^ mask) for source in range(count)])


def hop_to(value, step):
    pairs = []
    for source in range(2 * lax.axis_size("seq")):
        flip, mask = step(source % 2, source // 2)
        pairs.append((source, source ^ (2 * mask + flip)))
    return lax.ppermute(value, ("seq", "dp"), pairs)


def class_of(core, place):
    return (core + place + place // 2 + place // 4) % 2


def wrapped_device(
    features, cotangent, counts, count_weight, down_weight, tap_weight, up_weight,
    decay_rate, keep_share, mode_weight,
):
    rows, width = features.shape[1:]
    down = jnp.swapaxes(down_weight, 1, 2)
    taps = jnp.swapaxes(tap_weight, 2, 3)
    down_far, up_far, taps_far = swap(down, "dp", 1), swap(up_weight, "dp", 1), swap(taps, "dp", 1)
    scale = jnp.sqrt(-jnp.expm1(-2.0 * decay_rate))
    (pay,) = call(
        prepare_body,
        tuple(pltpu.with_memory_space_constraint(value, HBM) for value in (cotangent, keep_share, decay_rate)),
        (HBM,) * 3,
        (((1, 8, width + 128), BF16),),
        (
            pltpu.VMEM(cotangent.shape, BF16),
            pltpu.VMEM(keep_share.shape, F32),
            pltpu.SMEM(decay_rate.shape, F32),
            pltpu.SemaphoreType.DMA((3,)),
        ),
        size=1300 * GIGA,
    )
    got = hop_to(pay, lambda core, place: (0, HOPS[0]))
    down_full, tap_full = call(
        assemble_body,
        (down, down_far, taps, taps_far),
        (VMEM,) * 4,
        (((LAYERS, B, width), BF16), ((LAYERS, B, B), BF16)), size=1200 * GIGA
    )
    two = jnp.concatenate([pay, got], axis=0)
    two, down_full, tap_full = lax.optimization_barrier((two, down_full, tap_full))
    got_two = hop_to(two, lambda core, place: (0, HOPS[1 + core]))
    stream, inverse, reduced, slope = call(
        forward_body,
        (features, counts, count_weight[None], down_full, tap_full, up_weight, up_far),
        (VMEM,) * 7,
        (
            ((LAYERS + 1, rows, width), F32),
            ((LAYERS, rows, 1), F32),
            ((LAYERS * rows, B), BF16),
            ((LAYERS, rows, B), F32),
        ), size=1800 * GIGA
    )
    four = jnp.concatenate([two, got_two], axis=0)
    four, stream, reduced = lax.optimization_barrier((four, stream, reduced))
    got_four = hop_to(four, lambda core, place: (0, HOPS[2 - core]))
    reduced_far = swap(reduced, "dp", 1)
    local, mark, reach, edge, rate = call(
        local_body,
        (decay_rate, scale, cotangent, keep_share, mode_weight, stream),
        (SMEM, SMEM) + (VMEM,) * 4,
        (((rows, width), F32), ((8, width), F32), ((8, width), F32), ((32, rows), BF16), ((2, 8, 128), F32)), size=1600 * GIGA
    )
    local, reduced_far = lax.optimization_barrier((local, reduced_far))
    gradient, mixed, partial = call(
        backward_body,
        (
            pay, got, got_two, got_four, mode_weight, local, mark, reach, edge, rate,
            stream, inverse, slope, down_full, tap_full, up_weight, up_far,
        ),
        (VMEM,) * 17,
        (((rows, width), F32), ((LAYERS * rows + 32, B), BF16), ((16, B), F32)), size=2100 * GIGA
    )
    mixed_far = swap(mixed, "dp", 1)
    (grad,) = call(
        output_body,
        (gradient, mixed, stream, inverse, down_full, tap_full),
        (VMEM,) * 6,
        (((1, rows, width), BF16),), size=1300 * GIGA
    )
    kept_rows = RING * BLOCK // 2
    kept, send, partial = call(
        taps_body,
        (reduced, reduced_far, mixed, mixed_far, partial),
        (VMEM,) * 5,
        (((kept_rows, B), F32), ((kept_rows + 16, B), BF16), ((16, B), F32)),
        (pltpu.VMEM((LAYERS, B, B), F32),), size=500 * GIGA
    )
    got = hop_to(send, lambda core, place: (1, 1 + class_of(core, place)))
    for stage in (1, 2):
        kept_rows = kept.shape[0] // 2
        mode_rows = (16, 8)[stage - 1]
        kept, send, partial = call(
            functools.partial(join_body, stage),
            (kept, got, partial),
            (VMEM,) * 3,
            (((kept_rows, B), F32), ((kept_rows + mode_rows, B), BF16), ((mode_rows, B), F32)),
        )
        if stage == 1:
            send, grad = lax.optimization_barrier((send, grad))
        if stage == 1:
            got = hop_to(send, lambda core, place: (1, 2 - class_of(core, place)))
        else:
            got = hop_to(send, lambda core, place: (1, 4))
    total = features.shape[0] * lax.axis_size("dp") * rows * lax.axis_size("seq")
    report = 1.0 / math.sqrt(total)
    block, narrow = call(
        functools.partial(finish_body, report),
        (kept, got),
        (VMEM,) * 2,
        (((BLOCK, B), F32), ((BLOCK, B), BF16)),
    )
    parts = []
    for table in SOURCES:
        pairs = [(8 * layer + table[j], 8 * layer + j) for layer in range(LAYERS) for j in range(8)]
        parts.append(lax.ppermute(narrow, ("seq", "dp"), pairs))
    (mode_sum,) = call(
        functools.partial(modes_body, report), (got, partial), (VMEM,) * 2, (((8, BLOCK), F32),)
    )
    (taps_sum,) = call(place_body, (block, *parts), (VMEM,) * 3, (((3 * BLOCK, B), F32),))
    return grad, taps_sum, mode_sum


def solution(mesh):
    placed = (
        P(("parts", "dp"), "seq", None),
        P(("parts", "dp"), "seq", None),
        P(("parts", "dp"), "seq"),
        P(),
        P(None, None, "dp"),
        P(None, None, None, "dp"),
        P(None, None, "dp"),
        P(),
        P(("parts", "dp"), "seq"),
        P(),
    )

    def per_device(*operands):
        rows = operands[0].shape[1]
        ring = lax.axis_size("seq")
        loop = ring * rows
        wraps = all(dilation % loop == 0 for dilation in (DILATION_FIRST1, DILATION_SECOND2))
        fits = ring == RING and lax.axis_size("dp") == 2 and operands[0].shape[0] == 1
        return (wrapped_device if wraps and fits else general_device)(*operands)

    return jax.shard_map(
        per_device,
        mesh=mesh,
        in_specs=placed,
        out_specs=(
            P(("parts", "dp"), "seq", None),
            P(("parts", "seq", "dp"), None),
            P("parts", ("seq", "dp")),
        ),
        check_vma=False,
    )
```

```python
import functools
import math

import jax
import jax.numpy as jnp
from jax import lax
from jax.experimental import pallas as pl
from jax.experimental.pallas import tpu as pltpu
from jax.sharding import PartitionSpec as P

B = 384
DILATION_FIRST1 = 2048
DILATION_SECOND2 = 4096
M = 4
LAYERS = 2


EPSILON = 1e-06
HALF_ROOT = 1.0 / math.sqrt(2.0)
DENSITY = 1.0 / math.sqrt(2.0 * math.pi)
TOP_PRECISION = lax.Precision.HIGHEST


def shifted(value, axis, steps):
    count = lax.axis_size(axis)
    pairs = [(source, (source + steps) % count) for source in range(count)]
    return lax.ppermute(value, axis, pairs)


def entering_2(shard, axis, join, neutral, backward):
    count = lax.axis_size(axis)
    place = lax.axis_index(axis)
    ahead = count - 1 - place if backward else place
    gathered = jax.tree.map(
        lambda a, kind: lax.all_gather(a.astype(kind), axis),
        shard,
        jax.tree.map(lambda a: jnp.bfloat16 if a.dtype == jnp.float32 else a.dtype, shard),
    )
    state = jax.tree.map(lambda a, e: jnp.zeros_like(a) + jnp.asarray(e, a.dtype), shard, neutral)

    def one(turn, state):
        source = count - 1 - turn if backward else turn
        return join(
            state,
            jax.tree.map(
                lambda a, own: lax.dynamic_index_in_dim(a, source, 0, False).astype(own.dtype),
                gathered,
                shard,
            ),
        )

    return lax.fori_loop(0, ahead, one, state)


def gelu_exact(values):
    return 0.5 * values * (1.0 + lax.erf(values * HALF_ROOT))


def gelu_slope(values):
    cumulative = 0.5 * (1.0 + lax.erf(values * HALF_ROOT))
    return cumulative + values * jnp.exp(-0.5 * values * values) * DENSITY


def project(left_shifted, right_shifted):
    return jnp.einsum(
        "qra,au->qru", left_shifted, right_shifted, preferred_element_type=jnp.float32
    )


def project_back(left_shifted, right_shifted):
    return jnp.einsum(
        "kut,st->kus", left_shifted, right_shifted, preferred_element_type=jnp.float32
    )


def contract(left_shifted, right_shifted):
    return jnp.einsum(
        "glb,glk->bk", left_shifted, right_shifted, preferred_element_type=jnp.float32
    )


def moved(values, bin_distance):
    return shifted(values, "seq", bin_distance)


def block_product(kernel, pieces):
    return jnp.einsum(
        "gmbij,gbjc->gmbic",
        kernel,
        pieces,
        precision=TOP_PRECISION,
        preferred_element_type=jnp.float32,
    )


def modal_local(lg_in, lg_exit, stream_rows, cotangent_rows):
    genome_count, input_rows, mode_count = lg_in.shape
    feature_maps = stream_rows.shape[-1]
    block_size = min(128, input_rows)
    block_count = input_rows // block_size
    running = jnp.cumsum(lg_in, axis=1)
    running_blocks = running.reshape(genome_count, block_count, block_size, mode_count)
    block_ends = running_blocks[:, :, -1, :]
    block_starts = jnp.concatenate(
        [jnp.zeros((genome_count, 1, mode_count), jnp.float32), block_ends[:, :-1, :]], axis=1
    )
    within = running_blocks - block_starts[:, :, None, :]
    within_t = jnp.transpose(within, (0, 3, 1, 2))
    spread = within_t[..., :, None] - within_t[..., None, :]
    row_index = lax.broadcasted_iota(jnp.int32, (block_size, block_size), 0)
    column_index = lax.broadcasted_iota(jnp.int32, (block_size, block_size), 1)
    kernel = jnp.where(row_index >= column_index, jnp.exp(jnp.minimum(spread, 0.0)), 0.0)
    joined_source = jnp.concatenate([stream_rows, cotangent_rows.astype(jnp.float32)], axis=-1)
    joined_source = joined_source.reshape(genome_count, block_count, block_size, 2 * feature_maps)
    partial_value = block_product(kernel, joined_source)
    block_tails = partial_value[:, :, :, -1, :]
    ends_t = jnp.transpose(block_ends, (0, 2, 1))
    starts_t = jnp.transpose(block_starts, (0, 2, 1))
    spacing = starts_t[..., :, None] - ends_t[..., None, :]
    block_index = lax.broadcasted_iota(jnp.int32, (block_count, block_count), 0)
    source_index = lax.broadcasted_iota(jnp.int32, (block_count, block_count), 1)
    linkage = jnp.where(source_index < block_index, jnp.exp(jnp.minimum(spacing, 0.0)), 0.0)
    entering = jnp.einsum(
        "gmbk,gmkc->gmbc",
        linkage,
        block_tails,
        precision=TOP_PRECISION,
        preferred_element_type=jnp.float32,
    )
    states = partial_value + jnp.exp(within_t)[..., None] * entering[:, :, :, None, :]
    states = states.reshape(genome_count, mode_count, input_rows, 2 * feature_maps)
    decay_values = jnp.exp(jnp.transpose(running, (0, 2, 1)))
    exit_state = jnp.exp(lg_exit)[..., None] * states[:, :, -1, :]
    log_pass = running[:, -1, :] + lg_exit
    return (states, decay_values, exit_state, log_pass)


def modal_terms(states, decay_values, entering, cotangent_rows, source_gain, cot_gain):
    feature_maps = cotangent_rows.shape[-1]
    reach_sum = jnp.einsum(
        "qsz,qzj->qsj",
        decay_values,
        cotangent_rows,
        precision=TOP_PRECISION,
        preferred_element_type=jnp.float32,
    )
    totals = jnp.einsum(
        "veyi,vyi->ei",
        states[..., :feature_maps],
        cotangent_rows,
        precision=TOP_PRECISION,
        preferred_element_type=jnp.float32,
    )
    totals = totals + jnp.sum(entering[..., :feature_maps] * reach_sum, axis=0)
    rows_out = jnp.einsum(
        "jryf,rf->jyf",
        states[..., feature_maps:],
        cot_gain,
        precision=TOP_PRECISION,
        preferred_element_type=jnp.float32,
    )
    rows_out = rows_out + jnp.einsum(
        "ert,erx->etx",
        decay_values,
        entering[..., feature_maps:] * cot_gain[None],
        precision=TOP_PRECISION,
        preferred_element_type=jnp.float32,
    )
    return (source_gain[:, None] * totals, rows_out)


def apply_early_first(early_pass, early_state, late_pass, late_state):
    return (early_pass * late_pass, late_pass[..., None] * early_state + late_state)


def apply_late_first(early_pass, early_state, late_pass, late_state):
    return (early_pass * late_pass, early_pass[..., None] * late_state + early_state)


def join_lower(early, late):
    fore_pass, fore_state = apply_early_first(early[0], early[1], late[0], late[1])
    back_pass, back_state = apply_late_first(early[2], early[3], late[2], late[3])
    return (fore_pass, fore_state, back_pass, back_state)


def join_upper(early, late):
    fore_pass, fore_state = apply_late_first(early[0], early[1], late[0], late[1])
    back_pass, back_state = apply_early_first(early[2], early[3], late[2], late[3])
    return (fore_pass, fore_state, back_pass, back_state)


def closed(own_pass, own_state, pass_before, state_before, pass_after, state_after):
    beside_all = pass_before * pass_after
    numerator = (
        beside_all[..., None] * own_state + pass_before[..., None] * state_after + state_before
    )
    return numerator / (1.0 - beside_all * own_pass)[..., None]


def general_device(
    features,
    cotangent,
    counts,
    count_weight,
    down_weight,
    tap_weight,
    up_weight,
    decay_rate,
    keep_share,
    mode_weight,
):
    genome_count = features.shape[0]
    input_rows = features.shape[1]
    down_full, tap_full, full_up_weight = (
        lax.all_gather(down_weight, "dp", axis=2, tiled=True),
        lax.all_gather(tap_weight, "dp", axis=3, tiled=True),
        lax.all_gather(up_weight, "dp", axis=2, tiled=True),
    )
    stream = (
        features.astype(jnp.float32)
        + jnp.log1p(counts.astype(jnp.float32))[..., None] * count_weight
    )
    stored = []
    for layer_position in range(LAYERS):
        bin_distance = (DILATION_FIRST1 if layer_position == 0 else DILATION_SECOND2) // input_rows
        inverse = lax.rsqrt(jnp.mean(stream * stream, axis=-1, keepdims=True) + EPSILON)
        normed = (stream * inverse).astype(jnp.bfloat16)
        reduced = project(normed, down_full[layer_position]).astype(jnp.bfloat16)
        lagged = moved(reduced, bin_distance)
        advanced = moved(reduced, -bin_distance)
        mixture = (
            project(lagged, tap_full[layer_position, 0])
            + project(reduced, tap_full[layer_position, 1])
            + project(advanced, tap_full[layer_position, 2])
        )
        active_modes = gelu_exact(mixture).astype(jnp.bfloat16)
        stored.append((stream, inverse, reduced, lagged, advanced, mixture))
        stream = stream + jnp.einsum(
            "quy,yk->quk",
            active_modes,
            full_up_weight[layer_position],
            preferred_element_type=jnp.float32,
        )
    cot_wide = cotangent.astype(jnp.float32)
    logs = jnp.log(keep_share)[:, :, None] - decay_rate[None, None, :]
    mode_scale = jnp.sqrt(-jnp.expm1(-2.0 * decay_rate))
    fore_states, fore_decays, fore_exit, fore_log = modal_local(
        logs, jnp.zeros_like(logs[:, 0, :]), stream, cotangent
    )
    back_logs = jnp.concatenate(
        [jnp.zeros_like(logs[:, :1, :]), logs[:, ::-1, :][:, :-1, :]], axis=1
    )
    back_states, back_decays, back_exit, back_log = modal_local(
        back_logs, logs[:, 0, :], stream[:, ::-1, :], cotangent[:, ::-1, :]
    )
    summary = (jnp.exp(fore_log), fore_exit, jnp.exp(back_log), back_exit)
    identity = (
        jnp.ones_like(fore_log),
        jnp.zeros_like(fore_exit),
        jnp.ones_like(back_log),
        jnp.zeros_like(back_exit),
    )
    from_lower = entering_2(summary, "seq", join_lower, identity, False)
    from_upper = entering_2(summary, "seq", join_upper, identity, True)
    fore_entry = closed(
        summary[0], summary[1], from_lower[0], from_lower[1], from_upper[0], from_upper[1]
    )
    back_entry = closed(
        summary[2], summary[3], from_upper[2], from_upper[3], from_lower[2], from_lower[3]
    )
    fore_totals, fore_rows = modal_terms(
        fore_states,
        fore_decays,
        fore_entry,
        cot_wide,
        mode_scale,
        mode_scale[:, None] * mode_weight[1],
    )
    back_totals, back_rows = modal_terms(
        back_states,
        back_decays,
        back_entry,
        cot_wide[:, ::-1, :],
        mode_scale,
        mode_scale[:, None] * mode_weight[0],
    )
    gradient = cot_wide + fore_rows + back_rows[:, ::-1, :]
    mode_terms = jnp.stack([fore_totals, back_totals]).reshape(2 * M, -1)
    tap_terms = []
    for layer_position in reversed(range(LAYERS)):
        bin_distance = (DILATION_FIRST1 if layer_position == 0 else DILATION_SECOND2) // input_rows
        before, inverse, reduced, lagged, advanced, mixture = stored[layer_position]
        narrow_width = gradient.astype(jnp.bfloat16)
        back_mixed = jnp.einsum(
            "yhi,ai->yha",
            narrow_width,
            full_up_weight[layer_position],
            preferred_element_type=jnp.float32,
        )
        mixed_grad = (back_mixed * gelu_slope(mixture)).astype(jnp.bfloat16)
        tap_terms.insert(
            0,
            jnp.stack(
                [
                    contract(lagged, mixed_grad),
                    contract(reduced, mixed_grad),
                    contract(advanced, mixed_grad),
                ]
            ),
        )
        reduced_grad = jnp.einsum(
            "glk,bk->glb",
            mixed_grad,
            tap_full[layer_position, 1],
            preferred_element_type=jnp.float32,
        )
        reduced_grad = reduced_grad + jnp.einsum(
            "glk,bk->glb",
            moved(mixed_grad, -bin_distance),
            tap_full[layer_position, 0],
            preferred_element_type=jnp.float32,
        )
        reduced_grad = reduced_grad + jnp.einsum(
            "glk,bk->glb",
            moved(mixed_grad, bin_distance),
            tap_full[layer_position, 2],
            preferred_element_type=jnp.float32,
        )
        normed_grad = project_back(reduced_grad.astype(jnp.bfloat16), down_full[layer_position])
        gradient = (
            gradient
            + inverse * normed_grad
            - before
            * inverse
            * inverse
            * inverse
            * jnp.mean(normed_grad * before, axis=-1, keepdims=True)
        )
    tap_flat = jnp.stack(tap_terms).reshape(LAYERS * 3 * B, B)
    seq_size = lax.axis_size("seq")
    dp_size = lax.axis_size("dp")
    report_scale = 1.0 / math.sqrt(genome_count * dp_size * input_rows * seq_size)
    tap_sum, mode_sum = (
        lax.psum_scatter(tap_flat, ("seq", "dp"), scatter_dimension=0, tiled=True),
        lax.psum_scatter(mode_terms, ("seq", "dp"), scatter_dimension=1, tiled=True),
    )
    return (gradient.astype(jnp.bfloat16), tap_sum * report_scale, mode_sum * report_scale)


VMEM = pltpu.MemorySpace.VMEM
SMEM = pltpu.MemorySpace.SMEM
HBM = pltpu.MemorySpace.HBM
F32 = jnp.float32
BF16 = jnp.bfloat16
RING = 8
HOPS = (4, 2, 1)
BLOCK = 48
OWNED = (0, 5, 7, 3, 4, 1, 2, 6)
SOURCES = ((6, 3, 7, 5, 1, 0, 4, 2), (5, 4, 0, 6, 7, 2, 3, 1))
GIGA = 10**6


def call(body, operands, spaces, outs, scratch=(), size=0):
    return pl.pallas_call(
        body,
        out_shape=[jax.ShapeDtypeStruct(shape, dtype) for shape, dtype in outs],
        in_specs=[pl.BlockSpec(memory_space=space) for space in spaces],
        out_specs=[pl.BlockSpec(memory_space=VMEM) for _ in outs],
        scratch_shapes=list(scratch),
        cost_estimate=pl.CostEstimate(flops=size, transcendentals=0, bytes_accessed=size // 256) if size else None,
        compiler_params=pltpu.CompilerParams(vmem_limit_bytes=40 * 1024 * 1024),
    )(*operands)


def dot(left, right):
    return lax.dot_general(left, right, (((1,), (0,)), ((), ())), preferred_element_type=F32)


def dot_nt(left, right):
    return lax.dot_general(left, right, (((1,), (1,)), ((), ())), preferred_element_type=F32)


def dot_tn(left, right):
    return lax.dot_general(left, right, (((0,), (0,)), ((), ())), preferred_element_type=F32)


def iota2(shape, axis):
    return lax.broadcasted_iota(jnp.int32, shape, axis)


def split_pair(value):
    high = value.astype(BF16)
    return high, (value - high.astype(F32)).astype(BF16)


def log_sums(keep_row):
    rows = keep_row.shape[-1]
    below, beside = iota2((rows, rows), 0), iota2((rows, rows), 1)
    logs = jnp.broadcast_to(jnp.log(keep_row), (rows, rows))
    column = jnp.sum(jnp.where(beside <= below, logs, 0.0), axis=1, keepdims=True)
    spread = jnp.broadcast_to(column, (rows, rows))
    row = jnp.sum(jnp.where(beside == below, spread, 0.0), axis=0, keepdims=True)
    return column, row, column[rows - 1 :, :]


def mode_terms(sums, total, decay_ref, rows):
    place = iota2((1, rows), 1).astype(F32)
    to_start, to_end = [], []
    for mode in range(M):
        rate = decay_ref[mode]
        to_start.append(jnp.exp(sums - (place + 1.0) * rate))
        to_end.append(jnp.exp((total - sums) - (rows - 1.0 - place) * rate))
    leaving = jnp.concatenate(to_start + to_end, axis=0)
    entering = jnp.concatenate(to_end + to_start, axis=0)
    return leaving, entering


def prepare_body(cot_hbm, keep_hbm, decay_hbm, pay_ref, cot_ref, keep_ref, decay_ref, sems):
    pairs = ((keep_hbm, keep_ref), (decay_hbm, decay_ref), (cot_hbm, cot_ref))
    copies = [pltpu.make_async_copy(source, to, sems.at[index]) for index, (source, to) in enumerate(pairs)]
    for copy in copies:
        copy.start()
    copies[0].wait()
    copies[1].wait()
    rows = keep_ref.shape[-1]
    _, sums, total = log_sums(keep_ref[...])
    weights, _ = mode_terms(sums, total, decay_ref, rows)
    high = weights.astype(BF16).astype(F32)
    both = jnp.concatenate([high, weights - high], axis=0).astype(BF16)
    width = cot_ref.shape[-1]
    first = jnp.broadcast_to(total, (8, 128))
    one = first.astype(BF16).astype(F32)
    two = (first - one).astype(BF16).astype(F32)
    three = first - one - two
    row = iota2((8, 128), 0)
    extra = jnp.where(row == 0, one, jnp.where(row == 1, two, jnp.where(row == 2, three, 0.0)))
    pay_ref[0, :, width:] = extra.astype(BF16)
    copies[2].wait()
    states = dot(both, cot_ref[0])
    pay_ref[0, :, :width] = (states[0:8] + states[8:16]).astype(BF16)


def assemble_body(down_ref, down_far_ref, tap_ref, tap_far_ref, down_out, tap_out):
    core = lax.axis_index("dp")
    half = down_ref.shape[1]
    for down, taps, side in ((down_ref, tap_ref, core), (down_far_ref, tap_far_ref, 1 - core)):
        part = pl.ds(pl.multiple_of(side * half, half), half)
        for layer in range(LAYERS):
            down_out[layer, part, :] = down[layer]
            total = taps[layer, 0].astype(F32) + taps[layer, 1].astype(F32) + taps[layer, 2].astype(F32)
            tap_out[layer, part, :] = total.astype(BF16)


def forward_body(
    feature_ref, count_ref, weight_ref, down_ref, tap_ref, up_ref, up_far_ref,
    stream_ref, inverse_ref, reduced_ref, slope_ref,
):
    core = lax.axis_index("dp")
    rows, width = feature_ref.shape[1:]
    logs = jnp.broadcast_to(jnp.log1p(count_ref[...].astype(F32)), (rows, rows))
    diagonal = iota2((rows, rows), 0) == iota2((rows, rows), 1)
    level = jnp.sum(jnp.where(diagonal, logs, 0.0), axis=1, keepdims=True)
    stream = feature_ref[0].astype(F32) + level * weight_ref[...]
    for layer in range(LAYERS):
        stream_ref[layer] = stream
        mean = jnp.sum(stream * stream, axis=-1, keepdims=True) * (1.0 / width)
        inverse = lax.rsqrt(mean + EPSILON)
        inverse_ref[layer] = inverse
        normed = (stream * inverse).astype(BF16)
        reduced = dot_nt(normed, down_ref[layer]).astype(BF16)
        reduced_ref[layer * rows : (layer + 1) * rows, :] = reduced
        mixture = dot_nt(reduced, tap_ref[layer])
        share = 0.5 * (1.0 + lax.erf(mixture * HALF_ROOT))
        slope_ref[layer] = share + mixture * jnp.exp(-0.5 * mixture * mixture) * DENSITY
        act = (mixture * share).astype(BF16)
        out_near = dot(act, up_ref[layer])
        out_away = dot(act, up_far_ref[layer])
        low = jnp.where(core == 0, out_near, out_away)
        high = jnp.where(core == 0, out_away, out_near)
        stream = stream + jnp.concatenate([low, high], axis=-1)
    stream_ref[LAYERS] = stream


def local_body(decay_ref, scale_ref, cot_ref, keep_ref, mode_ref, stream_ref, grad_ref, mark_ref, reach_ref, edge_ref, rate_ref):
    rows, width = cot_ref.shape[1:]
    column, row, total = log_sums(keep_ref[...])
    below = iota2((rows, rows), 0)
    across = iota2((rows, rows), 1)
    gap = column - row
    steps = (below - across).astype(F32)
    kernels = []
    for mode in range(M):
        value = jnp.exp(jnp.minimum(steps * decay_ref[mode] - gap, 0.0))
        kernels.append(jnp.where(across >= below, value, 0.0))
    for mode in range(M):
        value = jnp.exp(jnp.minimum(gap - steps * decay_ref[mode], 0.0))
        kernels.append(jnp.where(below >= across, value, 0.0))
    pairs = [jnp.concatenate(split_pair(kernel), axis=1) for kernel in kernels]
    _, edges = mode_terms(row, total, decay_ref, rows)
    high = edges.astype(BF16).astype(F32)
    both = jnp.concatenate([high, edges - high], axis=0).astype(BF16)
    edge_ref[...] = jnp.concatenate([high, high, edges - high, jnp.zeros_like(high)], axis=0).astype(BF16)
    row8 = iota2((8, 128), 0)
    for side, values_ref in enumerate((decay_ref, scale_ref)):
        value8 = jnp.zeros((8, 128), F32)
        for index in range(2 * M):
            value8 = jnp.where(row8 == index, values_ref[index % M], value8)
        rate_ref[side] = value8
    span = 256
    for start in range(0, width, span):
        part = slice(start, start + span)
        cot = cot_ref[0, :, part]
        doubled = jnp.concatenate([cot, cot], axis=0)
        stream = stream_ref[LAYERS, :, part]
        grad = cot.astype(F32)
        marks = []
        for index in range(2 * M):
            mode = index % M
            field = dot(pairs[index], doubled)
            gain = scale_ref[mode]
            grad = grad + (gain * mode_ref[index // M, mode : mode + 1, part]) * field
            marks.append(jnp.sum(stream * field, axis=0, keepdims=True))
        grad_ref[:, part] = grad
        mark_ref[:, part] = jnp.concatenate(marks, axis=0)
        near, away = split_pair(stream)
        reach = dot(both, near)
        reach_ref[:, part] = reach[0:8] + reach[8:16] + dot(both, away)[0:8]


def backward_body(
    first_ref, second_ref, third_ref, fourth_ref, mode_ref,
    local_ref, mark_ref, reach_ref, edge_ref, rate_ref, stream_ref, inverse_ref, slope_ref, down_ref, tap_ref, up_ref,
    up_far_ref, grads_ref, mixed_ref, partial_ref,
):
    core = lax.axis_index("dp")
    place = lax.axis_index("seq")
    rows, width = local_ref.shape
    wide = up_ref.shape[-1]

    masks = [0]
    for hop in (HOPS[0], HOPS[1] - core, HOPS[2] + core):
        masks = masks + [lax.bitwise_xor(mask, hop) for mask in masks]
    pieces = []
    for ref in (first_ref, second_ref, third_ref, fourth_ref):
        pieces = pieces + [ref[index].astype(F32) for index in range(ref.shape[0])]
    totals = jnp.concatenate([jnp.sum(piece[:, width:], axis=0, keepdims=True) for piece in pieces], axis=0)
    row8 = iota2((8, 128), 0)
    decay8 = rate_ref[0]
    gain8 = rate_ref[1, :, 0:1]
    everything = jnp.sum(totals, axis=0, keepdims=True)
    loop = 1.0 / (1.0 - jnp.exp(everything - (RING * rows) * decay8))
    spots = jnp.zeros((8, 128), jnp.int32)
    for index in range(RING):
        spots = jnp.where(row8 == index, lax.bitwise_xor(place, masks[index]), spots)
    ahead = lax.bitwise_and(place - spots + (RING - 1), RING - 1)
    after = lax.bitwise_and(spots - place + (RING - 1), RING - 1)
    entering = jnp.zeros((8, width), F32)
    for index in range(RING):
        here = slice(index, index + 1)
        fore = jnp.sum(jnp.where(ahead < ahead[here], totals, 0.0), axis=0, keepdims=True)
        back = jnp.sum(jnp.where(after < after[here], totals, 0.0), axis=0, keepdims=True)
        fore = fore - (ahead[here] * rows).astype(F32) * decay8
        back = back - (after[here] * rows).astype(F32) * decay8
        share = jnp.exp(jnp.where(row8 < M, back, fore)) * loop
        entering = entering + share[:, 0:1] * pieces[index][:, :width]
    whole = gain8 * (mark_ref[...] + entering * reach_ref[...])
    partial = jnp.concatenate([whole[:, :wide], whole[:, wide:]], axis=0)
    partial_ref[...] = partial
    high, low = split_pair(partial)
    mixed_ref[LAYERS * rows : LAYERS * rows + 16, :] = high
    mixed_ref[LAYERS * rows + 16 : LAYERS * rows + 32, :] = low
    weighted = entering * gain8 * jnp.concatenate([mode_ref[0], mode_ref[1]], axis=0)
    in_high = weighted.astype(BF16).astype(F32)
    in_low = weighted - in_high
    right = jnp.concatenate([in_high, in_low, in_high, jnp.zeros_like(in_high)], axis=0).astype(BF16)
    gradient = local_ref[...] + dot_tn(edge_ref[...], right)

    for layer in reversed(range(LAYERS)):
        narrow = gradient.astype(BF16)
        first, second = narrow[:, :wide], narrow[:, wide:]
        mine = jnp.where(core == 0, first, second)
        theirs = jnp.where(core == 0, second, first)
        back = dot_nt(mine, up_ref[layer]) + dot_nt(theirs, up_far_ref[layer])
        mixed = (back * slope_ref[layer]).astype(BF16)
        mixed_ref[layer * rows : (layer + 1) * rows, :] = mixed
        if layer:
            gradient = through_layer(layer, gradient, mixed, stream_ref, inverse_ref, down_ref, tap_ref)
    grads_ref[...] = gradient


def through_layer(layer, gradient, mixed, stream_ref, inverse_ref, down_ref, tap_ref):
    passed = dot(mixed, tap_ref[layer]).astype(BF16)
    normed = dot(passed, down_ref[layer])
    before = stream_ref[layer]
    inverse = inverse_ref[layer]
    shared = jnp.sum(normed * before, axis=-1, keepdims=True) * (1.0 / before.shape[-1])
    return gradient + inverse * normed - before * (inverse * inverse * inverse * shared)


def output_body(gradient_ref, mixed_ref, stream_ref, inverse_ref, down_ref, tap_ref, grad_ref):
    rows = gradient_ref.shape[0]
    mixed = mixed_ref[0:rows, :]
    gradient = through_layer(0, gradient_ref[...], mixed, stream_ref, inverse_ref, down_ref, tap_ref)
    grad_ref[0] = gradient.astype(BF16)


def entry_of(table, index):
    packed = sum(value << (3 * place) for place, value in enumerate(table))
    return lax.bitwise_and(lax.shift_right_logical(jnp.int32(packed), jnp.int32(3) * index), jnp.int32(7))


def held_block(parity, bit_x, bit_z, layer):
    core = lax.bitwise_xor(lax.bitwise_xor(parity, bit_x), lax.bitwise_xor(bit_z, layer))
    return pl.multiple_of(entry_of(OWNED, 4 * bit_z + 2 * bit_x + core) * BLOCK, BLOCK)


def select_body(reduced_ref, reduced_far_ref, left_ref, turned_ref):
    bits, parity = position_bits()
    bit = pick(parity, bits[0], bits[1])
    rows = reduced_ref.shape[0] // LAYERS
    for layer in range(LAYERS):
        part = slice(layer * rows, (layer + 1) * rows)
        turned_ref[layer, :, :rows] = reduced_ref[part, :].T
        turned_ref[layer, :, rows:] = reduced_far_ref[part, :].T
        for side in range(2):
            first = bit if side == 0 else 1 - bit
            for turn in range(2):
                block = held_block(parity, pick(parity, first, turn), pick(parity, turn, first), layer)
                to = (2 * side + turn) * BLOCK
                left_ref[layer, to : to + BLOCK, :] = turned_ref[layer, pl.ds(block, BLOCK), :]


def taps_body(left_ref, mixed_ref, mixed_far_ref, partial_ref, kept_ref, send_ref, partial_out):
    rows = left_ref.shape[-1] // 2
    kept_rows = kept_ref.shape[0]
    for layer in range(LAYERS):
        part = slice(layer * rows, (layer + 1) * rows)
        right = jnp.concatenate([mixed_ref[part, :], mixed_far_ref[part, :]], axis=0)
        blocks = dot(left_ref[layer], right)
        for turn in range(2):
            to = (2 * turn + layer) * BLOCK
            kept_ref[to : to + BLOCK, :] = blocks[turn * BLOCK : (turn + 1) * BLOCK]
            send_ref[to : to + BLOCK, :] = blocks[(2 + turn) * BLOCK : (3 + turn) * BLOCK].astype(BF16)
    high = mixed_far_ref[LAYERS * rows : LAYERS * rows + 16, :].astype(F32)
    low = mixed_far_ref[LAYERS * rows + 16 : LAYERS * rows + 32, :].astype(F32)
    partial = partial_ref[...] + (high + low)
    partial_out[...] = partial
    send_ref[kept_rows : kept_rows + 16, :] = partial.astype(BF16)


def position_bits():
    place = lax.axis_index("seq")
    bits = [lax.rem(place // value, 2) for value in (1, 2, 4)]
    return bits, lax.rem(lax.axis_index("dp") + bits[0] + bits[1] + bits[2], 2)


def pick(parity, even, odd):
    return even + parity * (odd - even)


def join_body(stage, kept_ref, got_ref, partial_ref, kept_out, send_out, partial_out):
    rows = kept_out.shape[0]
    bits, parity = position_bits()
    bit = pick(parity, bits[1], bits[0]) if stage == 1 else bits[2]
    keep = pl.ds(pl.multiple_of(bit * rows, rows), rows)
    send = pl.ds(pl.multiple_of((1 - bit) * rows, rows), rows)
    kept_out[...] = kept_ref[keep, :] + got_ref[keep, :].astype(F32)
    send_out[0:rows, :] = (kept_ref[send, :] + got_ref[send, :].astype(F32)).astype(BF16)
    partial = partial_ref[...] + got_ref[2 * rows : 2 * rows + 16, :].astype(F32)
    if stage == 1:
        partial_out[...] = partial
        send_out[rows : rows + 16, :] = partial.astype(BF16)
    else:
        last = bits[2]
        partial_out[...] = jnp.where(last == 0, partial[0:8], partial[8:16])
        send_out[rows : rows + 8, :] = jnp.where(last == 0, partial[8:16], partial[0:8]).astype(BF16)


def finish_body(scale, kept_ref, got_ref, block_out, send_out):
    rows = kept_ref.shape[0]
    block = (kept_ref[...] + got_ref[0:rows, :].astype(F32)) * scale
    block_out[...] = block
    send_out[...] = block.astype(BF16)


def place_body(own_ref, first_ref, second_ref, out_ref):
    number = lax.rem(2 * lax.axis_index("seq") + lax.axis_index("dp"), 8)
    held = (range(8),) + SOURCES
    for table, ref in zip(held, (own_ref, first_ref, second_ref)):
        spots = [(OWNED[table[j]] - 3 * j) % 8 for j in range(8)]
        out_ref[pl.ds(pl.multiple_of(entry_of(spots, number) * BLOCK, BLOCK), BLOCK), :] = ref[...].astype(F32)


def modes_body(scale, got_ref, partial_ref, mode_out):
    rows = got_ref.shape[0] - 8
    full = (partial_ref[...] + got_ref[rows : rows + 8, :].astype(F32)) * scale
    number = lax.rem(2 * lax.axis_index("seq") + lax.axis_index("dp"), 8)
    span = full.shape[1]
    mode_out[...] = pltpu.roll(full, lax.rem(span - BLOCK * number, span), 1)[:, 0:BLOCK]


def swap(value, axis, mask):
    count = lax.axis_size(axis)
    return lax.ppermute(value, axis, [(source, source ^ mask) for source in range(count)])


def hop_to(value, step):
    pairs = []
    for source in range(2 * lax.axis_size("seq")):
        flip, mask = step(source % 2, source // 2)
        pairs.append((source, source ^ (2 * mask + flip)))
    return lax.ppermute(value, ("seq", "dp"), pairs)


def class_of(core, place):
    return (core + place + place // 2 + place // 4) % 2


def wrapped_device(
    features, cotangent, counts, count_weight, down_weight, tap_weight, up_weight,
    decay_rate, keep_share, mode_weight,
):
    rows, width = features.shape[1:]
    down = jnp.swapaxes(down_weight, 1, 2)
    taps = jnp.swapaxes(tap_weight, 2, 3)
    down_far, up_far, taps_far = swap(down, "dp", 1), swap(up_weight, "dp", 1), swap(taps, "dp", 1)
    scale = jnp.sqrt(-jnp.expm1(-2.0 * decay_rate))
    (pay,) = call(
        prepare_body,
        tuple(pltpu.with_memory_space_constraint(value, HBM) for value in (cotangent, keep_share, decay_rate)),
        (HBM,) * 3,
        (((1, 8, width + 128), BF16),),
        (
            pltpu.VMEM(cotangent.shape, BF16),
            pltpu.VMEM(keep_share.shape, F32),
            pltpu.SMEM(decay_rate.shape, F32),
            pltpu.SemaphoreType.DMA((3,)),
        ),
        size=1300 * GIGA,
    )
    got = hop_to(pay, lambda core, place: (0, HOPS[0]))
    down_full, tap_full = call(
        assemble_body,
        (down, down_far, taps, taps_far),
        (VMEM,) * 4,
        (((LAYERS, B, width), BF16), ((LAYERS, B, B), BF16)), size=1200 * GIGA
    )
    two = jnp.concatenate([pay, got], axis=0)
    two, down_full, tap_full = lax.optimization_barrier((two, down_full, tap_full))
    got_two = hop_to(two, lambda core, place: (0, HOPS[1 + core]))
    stream, inverse, reduced, slope = call(
        forward_body,
        (features, counts, count_weight[None], down_full, tap_full, up_weight, up_far),
        (VMEM,) * 7,
        (
            ((LAYERS + 1, rows, width), F32),
            ((LAYERS, rows, 1), F32),
            ((LAYERS * rows, B), BF16),
            ((LAYERS, rows, B), F32),
        ), size=1800 * GIGA
    )
    four = jnp.concatenate([two, got_two], axis=0)
    four, stream, reduced = lax.optimization_barrier((four, stream, reduced))
    got_four = hop_to(four, lambda core, place: (0, HOPS[2 - core]))
    reduced_far = swap(reduced, "dp", 1)
    local, mark, reach, edge, rate = call(
        local_body,
        (decay_rate, scale, cotangent, keep_share, mode_weight, stream),
        (SMEM, SMEM) + (VMEM,) * 4,
        (((rows, width), F32), ((8, width), F32), ((8, width), F32), ((32, rows), BF16), ((2, 8, 128), F32)), size=1600 * GIGA
    )
    local, reduced_far = lax.optimization_barrier((local, reduced_far))
    gradient, mixed, partial = call(
        backward_body,
        (
            pay, got, got_two, got_four, mode_weight, local, mark, reach, edge, rate,
            stream, inverse, slope, down_full, tap_full, up_weight, up_far,
        ),
        (VMEM,) * 17,
        (((rows, width), F32), ((LAYERS * rows + 32, B), BF16), ((16, B), F32)), size=2100 * GIGA
    )
    mixed_far = swap(mixed, "dp", 1)
    (grad,) = call(
        output_body,
        (gradient, mixed, stream, inverse, down_full, tap_full),
        (VMEM,) * 6,
        (((1, rows, width), BF16),), size=1300 * GIGA
    )
    kept_rows = RING * BLOCK // 2
    (left,) = call(
        select_body,
        (reduced, reduced_far),
        (VMEM,) * 2,
        (((LAYERS, kept_rows, 2 * rows), BF16),),
        (pltpu.VMEM((LAYERS, B, 2 * rows), BF16),),
        size=500 * GIGA,
    )
    kept, send, partial = call(
        taps_body,
        (left, mixed, mixed_far, partial),
        (VMEM,) * 4,
        (((kept_rows, B), F32), ((kept_rows + 16, B), BF16), ((16, B), F32)),
        size=300 * GIGA,
    )
    got = hop_to(send, lambda core, place: (1, 1 + class_of(core, place)))
    for stage in (1, 2):
        kept_rows = kept.shape[0] // 2
        mode_rows = (16, 8)[stage - 1]
        kept, send, partial = call(
            functools.partial(join_body, stage),
            (kept, got, partial),
            (VMEM,) * 3,
            (((kept_rows, B), F32), ((kept_rows + mode_rows, B), BF16), ((mode_rows, B), F32)),
        )
        if stage == 1:
            send, grad = lax.optimization_barrier((send, grad))
        if stage == 1:
            got = hop_to(send, lambda core, place: (1, 2 - class_of(core, place)))
        else:
            got = hop_to(send, lambda core, place: (1, 4))
    total = features.shape[0] * lax.axis_size("dp") * rows * lax.axis_size("seq")
    report = 1.0 / math.sqrt(total)
    block, narrow = call(
        functools.partial(finish_body, report),
        (kept, got),
        (VMEM,) * 2,
        (((BLOCK, B), F32), ((BLOCK, B), BF16)),
    )
    parts = []
    for table in SOURCES:
        pairs = [(8 * layer + table[j], 8 * layer + j) for layer in range(LAYERS) for j in range(8)]
        parts.append(lax.ppermute(narrow, ("seq", "dp"), pairs))
    (mode_sum,) = call(
        functools.partial(modes_body, report), (got, partial), (VMEM,) * 2, (((8, BLOCK), F32),)
    )
    (taps_sum,) = call(place_body, (block, *parts), (VMEM,) * 3, (((3 * BLOCK, B), F32),))
    return grad, taps_sum, mode_sum


def solution(mesh):
    placed = (
        P(("parts", "dp"), "seq", None),
        P(("parts", "dp"), "seq", None),
        P(("parts", "dp"), "seq"),
        P(),
        P(None, None, "dp"),
        P(None, None, None, "dp"),
        P(None, None, "dp"),
        P(),
        P(("parts", "dp"), "seq"),
        P(),
    )

    def per_device(*operands):
        rows = operands[0].shape[1]
        ring = lax.axis_size("seq")
        loop = ring * rows
        wraps = all(dilation % loop == 0 for dilation in (DILATION_FIRST1, DILATION_SECOND2))
        fits = ring == RING and lax.axis_size("dp") == 2 and operands[0].shape[0] == 1
        return (wrapped_device if wraps and fits else general_device)(*operands)

    return jax.shard_map(
        per_device,
        mesh=mesh,
        in_specs=placed,
        out_specs=(
            P(("parts", "dp"), "seq", None),
            P(("parts", "seq", "dp"), None),
            P("parts", ("seq", "dp")),
        ),
        check_vma=False,
    )
```

```python
import functools
import math

import jax
import jax.numpy as jnp
from jax import lax
from jax.experimental import pallas as pl
from jax.experimental.pallas import tpu as pltpu
from jax.sharding import PartitionSpec as P

B = 384
DILATION_FIRST1 = 2048
DILATION_SECOND2 = 4096
M = 4
LAYERS = 2


EPSILON = 1e-06
HALF_ROOT = 1.0 / math.sqrt(2.0)
DENSITY = 1.0 / math.sqrt(2.0 * math.pi)
TOP_PRECISION = lax.Precision.HIGHEST


def shifted(value, axis, steps):
    count = lax.axis_size(axis)
    pairs = [(source, (source + steps) % count) for source in range(count)]
    return lax.ppermute(value, axis, pairs)


def entering_2(shard, axis, join, neutral, backward):
    count = lax.axis_size(axis)
    place = lax.axis_index(axis)
    ahead = count - 1 - place if backward else place
    gathered = jax.tree.map(
        lambda a, kind: lax.all_gather(a.astype(kind), axis),
        shard,
        jax.tree.map(lambda a: jnp.bfloat16 if a.dtype == jnp.float32 else a.dtype, shard),
    )
    state = jax.tree.map(lambda a, e: jnp.zeros_like(a) + jnp.asarray(e, a.dtype), shard, neutral)

    def one(turn, state):
        source = count - 1 - turn if backward else turn
        return join(
            state,
            jax.tree.map(
                lambda a, own: lax.dynamic_index_in_dim(a, source, 0, False).astype(own.dtype),
                gathered,
                shard,
            ),
        )

    return lax.fori_loop(0, ahead, one, state)


def gelu_exact(values):
    return 0.5 * values * (1.0 + lax.erf(values * HALF_ROOT))


def gelu_slope(values):
    cumulative = 0.5 * (1.0 + lax.erf(values * HALF_ROOT))
    return cumulative + values * jnp.exp(-0.5 * values * values) * DENSITY


def project(left_shifted, right_shifted):
    return jnp.einsum(
        "qra,au->qru", left_shifted, right_shifted, preferred_element_type=jnp.float32
    )


def project_back(left_shifted, right_shifted):
    return jnp.einsum(
        "kut,st->kus", left_shifted, right_shifted, preferred_element_type=jnp.float32
    )


def contract(left_shifted, right_shifted):
    return jnp.einsum(
        "glb,glk->bk", left_shifted, right_shifted, preferred_element_type=jnp.float32
    )


def moved(values, bin_distance):
    return shifted(values, "seq", bin_distance)


def block_product(kernel, pieces):
    return jnp.einsum(
        "gmbij,gbjc->gmbic",
        kernel,
        pieces,
        precision=TOP_PRECISION,
        preferred_element_type=jnp.float32,
    )


def modal_local(lg_in, lg_exit, stream_rows, cotangent_rows):
    genome_count, input_rows, mode_count = lg_in.shape
    feature_maps = stream_rows.shape[-1]
    block_size = min(128, input_rows)
    block_count = input_rows // block_size
    running = jnp.cumsum(lg_in, axis=1)
    running_blocks = running.reshape(genome_count, block_count, block_size, mode_count)
    block_ends = running_blocks[:, :, -1, :]
    block_starts = jnp.concatenate(
        [jnp.zeros((genome_count, 1, mode_count), jnp.float32), block_ends[:, :-1, :]], axis=1
    )
    within = running_blocks - block_starts[:, :, None, :]
    within_t = jnp.transpose(within, (0, 3, 1, 2))
    spread = within_t[..., :, None] - within_t[..., None, :]
    row_index = lax.broadcasted_iota(jnp.int32, (block_size, block_size), 0)
    column_index = lax.broadcasted_iota(jnp.int32, (block_size, block_size), 1)
    kernel = jnp.where(row_index >= column_index, jnp.exp(jnp.minimum(spread, 0.0)), 0.0)
    joined_source = jnp.concatenate([stream_rows, cotangent_rows.astype(jnp.float32)], axis=-1)
    joined_source = joined_source.reshape(genome_count, block_count, block_size, 2 * feature_maps)
    partial_value = block_product(kernel, joined_source)
    block_tails = partial_value[:, :, :, -1, :]
    ends_t = jnp.transpose(block_ends, (0, 2, 1))
    starts_t = jnp.transpose(block_starts, (0, 2, 1))
    spacing = starts_t[..., :, None] - ends_t[..., None, :]
    block_index = lax.broadcasted_iota(jnp.int32, (block_count, block_count), 0)
    source_index = lax.broadcasted_iota(jnp.int32, (block_count, block_count), 1)
    linkage = jnp.where(source_index < block_index, jnp.exp(jnp.minimum(spacing, 0.0)), 0.0)
    entering = jnp.einsum(
        "gmbk,gmkc->gmbc",
        linkage,
        block_tails,
        precision=TOP_PRECISION,
        preferred_element_type=jnp.float32,
    )
    states = partial_value + jnp.exp(within_t)[..., None] * entering[:, :, :, None, :]
    states = states.reshape(genome_count, mode_count, input_rows, 2 * feature_maps)
    decay_values = jnp.exp(jnp.transpose(running, (0, 2, 1)))
    exit_state = jnp.exp(lg_exit)[..., None] * states[:, :, -1, :]
    log_pass = running[:, -1, :] + lg_exit
    return (states, decay_values, exit_state, log_pass)


def modal_terms(states, decay_values, entering, cotangent_rows, source_gain, cot_gain):
    feature_maps = cotangent_rows.shape[-1]
    reach_sum = jnp.einsum(
        "qsz,qzj->qsj",
        decay_values,
        cotangent_rows,
        precision=TOP_PRECISION,
        preferred_element_type=jnp.float32,
    )
    totals = jnp.einsum(
        "veyi,vyi->ei",
        states[..., :feature_maps],
        cotangent_rows,
        precision=TOP_PRECISION,
        preferred_element_type=jnp.float32,
    )
    totals = totals + jnp.sum(entering[..., :feature_maps] * reach_sum, axis=0)
    rows_out = jnp.einsum(
        "jryf,rf->jyf",
        states[..., feature_maps:],
        cot_gain,
        precision=TOP_PRECISION,
        preferred_element_type=jnp.float32,
    )
    rows_out = rows_out + jnp.einsum(
        "ert,erx->etx",
        decay_values,
        entering[..., feature_maps:] * cot_gain[None],
        precision=TOP_PRECISION,
        preferred_element_type=jnp.float32,
    )
    return (source_gain[:, None] * totals, rows_out)


def apply_early_first(early_pass, early_state, late_pass, late_state):
    return (early_pass * late_pass, late_pass[..., None] * early_state + late_state)


def apply_late_first(early_pass, early_state, late_pass, late_state):
    return (early_pass * late_pass, early_pass[..., None] * late_state + early_state)


def join_lower(early, late):
    fore_pass, fore_state = apply_early_first(early[0], early[1], late[0], late[1])
    back_pass, back_state = apply_late_first(early[2], early[3], late[2], late[3])
    return (fore_pass, fore_state, back_pass, back_state)


def join_upper(early, late):
    fore_pass, fore_state = apply_late_first(early[0], early[1], late[0], late[1])
    back_pass, back_state = apply_early_first(early[2], early[3], late[2], late[3])
    return (fore_pass, fore_state, back_pass, back_state)


def closed(own_pass, own_state, pass_before, state_before, pass_after, state_after):
    beside_all = pass_before * pass_after
    numerator = (
        beside_all[..., None] * own_state + pass_before[..., None] * state_after + state_before
    )
    return numerator / (1.0 - beside_all * own_pass)[..., None]


def general_device(
    features,
    cotangent,
    counts,
    count_weight,
    down_weight,
    tap_weight,
    up_weight,
    decay_rate,
    keep_share,
    mode_weight,
):
    genome_count = features.shape[0]
    input_rows = features.shape[1]
    down_full, tap_full, full_up_weight = (
        lax.all_gather(down_weight, "dp", axis=2, tiled=True),
        lax.all_gather(tap_weight, "dp", axis=3, tiled=True),
        lax.all_gather(up_weight, "dp", axis=2, tiled=True),
    )
    stream = (
        features.astype(jnp.float32)
        + jnp.log1p(counts.astype(jnp.float32))[..., None] * count_weight
    )
    stored = []
    for layer_position in range(LAYERS):
        bin_distance = (DILATION_FIRST1 if layer_position == 0 else DILATION_SECOND2) // input_rows
        inverse = lax.rsqrt(jnp.mean(stream * stream, axis=-1, keepdims=True) + EPSILON)
        normed = (stream * inverse).astype(jnp.bfloat16)
        reduced = project(normed, down_full[layer_position]).astype(jnp.bfloat16)
        lagged = moved(reduced, bin_distance)
        advanced = moved(reduced, -bin_distance)
        mixture = (
            project(lagged, tap_full[layer_position, 0])
            + project(reduced, tap_full[layer_position, 1])
            + project(advanced, tap_full[layer_position, 2])
        )
        active_modes = gelu_exact(mixture).astype(jnp.bfloat16)
        stored.append((stream, inverse, reduced, lagged, advanced, mixture))
        stream = stream + jnp.einsum(
            "quy,yk->quk",
            active_modes,
            full_up_weight[layer_position],
            preferred_element_type=jnp.float32,
        )
    cot_wide = cotangent.astype(jnp.float32)
    logs = jnp.log(keep_share)[:, :, None] - decay_rate[None, None, :]
    mode_scale = jnp.sqrt(-jnp.expm1(-2.0 * decay_rate))
    fore_states, fore_decays, fore_exit, fore_log = modal_local(
        logs, jnp.zeros_like(logs[:, 0, :]), stream, cotangent
    )
    back_logs = jnp.concatenate(
        [jnp.zeros_like(logs[:, :1, :]), logs[:, ::-1, :][:, :-1, :]], axis=1
    )
    back_states, back_decays, back_exit, back_log = modal_local(
        back_logs, logs[:, 0, :], stream[:, ::-1, :], cotangent[:, ::-1, :]
    )
    summary = (jnp.exp(fore_log), fore_exit, jnp.exp(back_log), back_exit)
    identity = (
        jnp.ones_like(fore_log),
        jnp.zeros_like(fore_exit),
        jnp.ones_like(back_log),
        jnp.zeros_like(back_exit),
    )
    from_lower = entering_2(summary, "seq", join_lower, identity, False)
    from_upper = entering_2(summary, "seq", join_upper, identity, True)
    fore_entry = closed(
        summary[0], summary[1], from_lower[0], from_lower[1], from_upper[0], from_upper[1]
    )
    back_entry = closed(
        summary[2], summary[3], from_upper[2], from_upper[3], from_lower[2], from_lower[3]
    )
    fore_totals, fore_rows = modal_terms(
        fore_states,
        fore_decays,
        fore_entry,
        cot_wide,
        mode_scale,
        mode_scale[:, None] * mode_weight[1],
    )
    back_totals, back_rows = modal_terms(
        back_states,
        back_decays,
        back_entry,
        cot_wide[:, ::-1, :],
        mode_scale,
        mode_scale[:, None] * mode_weight[0],
    )
    gradient = cot_wide + fore_rows + back_rows[:, ::-1, :]
    mode_terms = jnp.stack([fore_totals, back_totals]).reshape(2 * M, -1)
    tap_terms = []
    for layer_position in reversed(range(LAYERS)):
        bin_distance = (DILATION_FIRST1 if layer_position == 0 else DILATION_SECOND2) // input_rows
        before, inverse, reduced, lagged, advanced, mixture = stored[layer_position]
        narrow_width = gradient.astype(jnp.bfloat16)
        back_mixed = jnp.einsum(
            "yhi,ai->yha",
            narrow_width,
            full_up_weight[layer_position],
            preferred_element_type=jnp.float32,
        )
        mixed_grad = (back_mixed * gelu_slope(mixture)).astype(jnp.bfloat16)
        tap_terms.insert(
            0,
            jnp.stack(
                [
                    contract(lagged, mixed_grad),
                    contract(reduced, mixed_grad),
                    contract(advanced, mixed_grad),
                ]
            ),
        )
        reduced_grad = jnp.einsum(
            "glk,bk->glb",
            mixed_grad,
            tap_full[layer_position, 1],
            preferred_element_type=jnp.float32,
        )
        reduced_grad = reduced_grad + jnp.einsum(
            "glk,bk->glb",
            moved(mixed_grad, -bin_distance),
            tap_full[layer_position, 0],
            preferred_element_type=jnp.float32,
        )
        reduced_grad = reduced_grad + jnp.einsum(
            "glk,bk->glb",
            moved(mixed_grad, bin_distance),
            tap_full[layer_position, 2],
            preferred_element_type=jnp.float32,
        )
        normed_grad = project_back(reduced_grad.astype(jnp.bfloat16), down_full[layer_position])
        gradient = (
            gradient
            + inverse * normed_grad
            - before
            * inverse
            * inverse
            * inverse
            * jnp.mean(normed_grad * before, axis=-1, keepdims=True)
        )
    tap_flat = jnp.stack(tap_terms).reshape(LAYERS * 3 * B, B)
    seq_size = lax.axis_size("seq")
    dp_size = lax.axis_size("dp")
    report_scale = 1.0 / math.sqrt(genome_count * dp_size * input_rows * seq_size)
    tap_sum, mode_sum = (
        lax.psum_scatter(tap_flat, ("seq", "dp"), scatter_dimension=0, tiled=True),
        lax.psum_scatter(mode_terms, ("seq", "dp"), scatter_dimension=1, tiled=True),
    )
    return (gradient.astype(jnp.bfloat16), tap_sum * report_scale, mode_sum * report_scale)


VMEM = pltpu.MemorySpace.VMEM
SMEM = pltpu.MemorySpace.SMEM
HBM = pltpu.MemorySpace.HBM
F32 = jnp.float32
BF16 = jnp.bfloat16
RING = 8
HOPS = (4, 2, 1)
BLOCK = 48
OWNED = (0, 5, 7, 3, 4, 1, 2, 6)
SOURCES = ((6, 3, 7, 5, 1, 0, 4, 2), (5, 4, 0, 6, 7, 2, 3, 1))
GIGA = 10**6


def call(body, operands, spaces, outs, scratch=(), size=0):
    return pl.pallas_call(
        body,
        out_shape=[jax.ShapeDtypeStruct(shape, dtype) for shape, dtype in outs],
        in_specs=[pl.BlockSpec(memory_space=space) for space in spaces],
        out_specs=[pl.BlockSpec(memory_space=VMEM) for _ in outs],
        scratch_shapes=list(scratch),
        cost_estimate=pl.CostEstimate(flops=size, transcendentals=0, bytes_accessed=size // 256) if size else None,
        compiler_params=pltpu.CompilerParams(vmem_limit_bytes=40 * 1024 * 1024),
    )(*operands)


def dot(left, right):
    return lax.dot_general(left, right, (((1,), (0,)), ((), ())), preferred_element_type=F32)


def dot_nt(left, right):
    return lax.dot_general(left, right, (((1,), (1,)), ((), ())), preferred_element_type=F32)


def dot_tn(left, right):
    return lax.dot_general(left, right, (((0,), (0,)), ((), ())), preferred_element_type=F32)


def iota2(shape, axis):
    return lax.broadcasted_iota(jnp.int32, shape, axis)


def split_pair(value):
    high = value.astype(BF16)
    return high, (value - high.astype(F32)).astype(BF16)


def log_sums(keep_row):
    rows = keep_row.shape[-1]
    below, beside = iota2((rows, rows), 0), iota2((rows, rows), 1)
    logs = jnp.broadcast_to(jnp.log(keep_row), (rows, rows))
    column = jnp.sum(jnp.where(beside <= below, logs, 0.0), axis=1, keepdims=True)
    spread = jnp.broadcast_to(column, (rows, rows))
    row = jnp.sum(jnp.where(beside == below, spread, 0.0), axis=0, keepdims=True)
    return column, row, column[rows - 1 :, :]


def mode_terms(sums, total, decay_ref, rows):
    place = iota2((1, rows), 1).astype(F32)
    to_start, to_end = [], []
    for mode in range(M):
        rate = decay_ref[mode]
        to_start.append(jnp.exp(sums - (place + 1.0) * rate))
        to_end.append(jnp.exp((total - sums) - (rows - 1.0 - place) * rate))
    leaving = jnp.concatenate(to_start + to_end, axis=0)
    entering = jnp.concatenate(to_end + to_start, axis=0)
    return leaving, entering


def prepare_body(cot_hbm, keep_hbm, decay_hbm, pay_ref, cot_ref, keep_ref, decay_ref, sems):
    pairs = ((keep_hbm, keep_ref), (decay_hbm, decay_ref), (cot_hbm, cot_ref))
    copies = [pltpu.make_async_copy(source, to, sems.at[index]) for index, (source, to) in enumerate(pairs)]
    for copy in copies:
        copy.start()
    copies[0].wait()
    copies[1].wait()
    rows = keep_ref.shape[-1]
    _, sums, total = log_sums(keep_ref[...])
    weights, _ = mode_terms(sums, total, decay_ref, rows)
    high = weights.astype(BF16).astype(F32)
    both = jnp.concatenate([high, weights - high], axis=0).astype(BF16)
    width = cot_ref.shape[-1]
    first = jnp.broadcast_to(total, (8, 128))
    one = first.astype(BF16).astype(F32)
    two = (first - one).astype(BF16).astype(F32)
    three = first - one - two
    row = iota2((8, 128), 0)
    extra = jnp.where(row == 0, one, jnp.where(row == 1, two, jnp.where(row == 2, three, 0.0)))
    pay_ref[0, :, width:] = extra.astype(BF16)
    copies[2].wait()
    states = dot(both, cot_ref[0])
    pay_ref[0, :, :width] = (states[0:8] + states[8:16]).astype(BF16)


def assemble_body(tap_ref, tap_far_ref, tap_out):
    core = lax.axis_index("dp")
    half = tap_ref.shape[2]
    for taps, side in ((tap_ref, core), (tap_far_ref, 1 - core)):
        part = pl.ds(pl.multiple_of(side * half, half), half)
        for layer in range(LAYERS):
            total = taps[layer, 0].astype(F32) + taps[layer, 1].astype(F32) + taps[layer, 2].astype(F32)
            tap_out[layer, part, :] = total.astype(BF16)


def forward_body(
    feature_ref, count_ref, weight_ref, down_ref, down_far_ref, tap_ref, up_ref, up_far_ref,
    stream_ref, inverse_ref, reduced_ref, slope_ref,
):
    core = lax.axis_index("dp")
    rows, width = feature_ref.shape[1:]
    logs = jnp.broadcast_to(jnp.log1p(count_ref[...].astype(F32)), (rows, rows))
    diagonal = iota2((rows, rows), 0) == iota2((rows, rows), 1)
    level = jnp.sum(jnp.where(diagonal, logs, 0.0), axis=1, keepdims=True)
    stream = feature_ref[0].astype(F32) + level * weight_ref[...]
    for layer in range(LAYERS):
        stream_ref[layer] = stream
        mean = jnp.sum(stream * stream, axis=-1, keepdims=True) * (1.0 / width)
        inverse = lax.rsqrt(mean + EPSILON)
        inverse_ref[layer] = inverse
        normed = (stream * inverse).astype(BF16)
        near = dot_nt(normed, down_ref[layer])
        away = dot_nt(normed, down_far_ref[layer])
        straight = jnp.concatenate([near, away], axis=-1)
        reduced = jnp.where(core == 0, straight, jnp.concatenate([away, near], axis=-1)).astype(BF16)
        reduced_ref[layer * rows : (layer + 1) * rows, :] = reduced
        mixture = dot_nt(reduced, tap_ref[layer])
        share = 0.5 * (1.0 + lax.erf(mixture * HALF_ROOT))
        slope_ref[layer] = share + mixture * jnp.exp(-0.5 * mixture * mixture) * DENSITY
        act = (mixture * share).astype(BF16)
        out_near = dot(act, up_ref[layer])
        out_away = dot(act, up_far_ref[layer])
        low = jnp.where(core == 0, out_near, out_away)
        high = jnp.where(core == 0, out_away, out_near)
        stream = stream + jnp.concatenate([low, high], axis=-1)
    stream_ref[LAYERS] = stream


def local_body(decay_ref, scale_ref, cot_ref, keep_ref, mode_ref, stream_ref, down_ref, down_far_ref, down_out, grad_ref, mark_ref, reach_ref, edge_ref, rate_ref):
    rows, width = cot_ref.shape[1:]
    core = lax.axis_index("dp")
    half = down_ref.shape[1]
    for down, side in ((down_ref, core), (down_far_ref, 1 - core)):
        for layer in range(LAYERS):
            down_out[layer, pl.ds(pl.multiple_of(side * half, half), half), :] = down[layer]
    column, row, total = log_sums(keep_ref[...])
    below = iota2((rows, rows), 0)
    across = iota2((rows, rows), 1)
    gap = column - row
    steps = (below - across).astype(F32)
    kernels = []
    for mode in range(M):
        value = jnp.exp(jnp.minimum(steps * decay_ref[mode] - gap, 0.0))
        kernels.append(jnp.where(across >= below, value, 0.0))
    for mode in range(M):
        value = jnp.exp(jnp.minimum(gap - steps * decay_ref[mode], 0.0))
        kernels.append(jnp.where(below >= across, value, 0.0))
    pairs = [jnp.concatenate(split_pair(kernel), axis=1) for kernel in kernels]
    _, edges = mode_terms(row, total, decay_ref, rows)
    high = edges.astype(BF16).astype(F32)
    both = jnp.concatenate([high, edges - high], axis=0).astype(BF16)
    edge_ref[...] = jnp.concatenate([high, high, edges - high, jnp.zeros_like(high)], axis=0).astype(BF16)
    row8 = iota2((8, 128), 0)
    for side, values_ref in enumerate((decay_ref, scale_ref)):
        value8 = jnp.zeros((8, 128), F32)
        for index in range(2 * M):
            value8 = jnp.where(row8 == index, values_ref[index % M], value8)
        rate_ref[side] = value8
    span = 256
    for start in range(0, width, span):
        part = slice(start, start + span)
        cot = cot_ref[0, :, part]
        doubled = jnp.concatenate([cot, cot], axis=0)
        stream = stream_ref[LAYERS, :, part]
        grad = cot.astype(F32)
        marks = []
        for index in range(2 * M):
            mode = index % M
            field = dot(pairs[index], doubled)
            gain = scale_ref[mode]
            grad = grad + (gain * mode_ref[index // M, mode : mode + 1, part]) * field
            marks.append(jnp.sum(stream * field, axis=0, keepdims=True))
        grad_ref[:, part] = grad
        mark_ref[:, part] = jnp.concatenate(marks, axis=0)
        near, away = split_pair(stream)
        reach = dot(both, near)
        reach_ref[:, part] = reach[0:8] + reach[8:16] + dot(both, away)[0:8]


def backward_body(
    first_ref, second_ref, third_ref, fourth_ref, mode_ref,
    local_ref, mark_ref, reach_ref, edge_ref, rate_ref, stream_ref, inverse_ref, slope_ref, down_ref, tap_ref, up_ref,
    up_far_ref, grads_ref, mixed_ref, partial_ref,
):
    core = lax.axis_index("dp")
    place = lax.axis_index("seq")
    rows, width = local_ref.shape
    wide = up_ref.shape[-1]

    masks = [0]
    for hop in (HOPS[0], HOPS[1] - core, HOPS[2] + core):
        masks = masks + [lax.bitwise_xor(mask, hop) for mask in masks]
    pieces = []
    for ref in (first_ref, second_ref, third_ref, fourth_ref):
        pieces = pieces + [ref[index].astype(F32) for index in range(ref.shape[0])]
    totals = jnp.concatenate([jnp.sum(piece[:, width:], axis=0, keepdims=True) for piece in pieces], axis=0)
    row8 = iota2((8, 128), 0)
    decay8 = rate_ref[0]
    gain8 = rate_ref[1, :, 0:1]
    everything = jnp.sum(totals, axis=0, keepdims=True)
    loop = 1.0 / (1.0 - jnp.exp(everything - (RING * rows) * decay8))
    spots = jnp.zeros((8, 128), jnp.int32)
    for index in range(RING):
        spots = jnp.where(row8 == index, lax.bitwise_xor(place, masks[index]), spots)
    ahead = lax.bitwise_and(place - spots + (RING - 1), RING - 1)
    after = lax.bitwise_and(spots - place + (RING - 1), RING - 1)
    entering = jnp.zeros((8, width), F32)
    for index in range(RING):
        here = slice(index, index + 1)
        fore = jnp.sum(jnp.where(ahead < ahead[here], totals, 0.0), axis=0, keepdims=True)
        back = jnp.sum(jnp.where(after < after[here], totals, 0.0), axis=0, keepdims=True)
        fore = fore - (ahead[here] * rows).astype(F32) * decay8
        back = back - (after[here] * rows).astype(F32) * decay8
        share = jnp.exp(jnp.where(row8 < M, back, fore)) * loop
        entering = entering + share[:, 0:1] * pieces[index][:, :width]
    whole = gain8 * (mark_ref[...] + entering * reach_ref[...])
    partial = jnp.concatenate([whole[:, :wide], whole[:, wide:]], axis=0)
    partial_ref[...] = partial
    high, low = split_pair(partial)
    mixed_ref[LAYERS * rows : LAYERS * rows + 16, :] = high
    mixed_ref[LAYERS * rows + 16 : LAYERS * rows + 32, :] = low
    weighted = entering * gain8 * jnp.concatenate([mode_ref[0], mode_ref[1]], axis=0)
    in_high = weighted.astype(BF16).astype(F32)
    in_low = weighted - in_high
    right = jnp.concatenate([in_high, in_low, in_high, jnp.zeros_like(in_high)], axis=0).astype(BF16)
    gradient = local_ref[...] + dot_tn(edge_ref[...], right)

    for layer in reversed(range(LAYERS)):
        narrow = gradient.astype(BF16)
        first, second = narrow[:, :wide], narrow[:, wide:]
        mine = jnp.where(core == 0, first, second)
        theirs = jnp.where(core == 0, second, first)
        back = dot_nt(mine, up_ref[layer]) + dot_nt(theirs, up_far_ref[layer])
        mixed = (back * slope_ref[layer]).astype(BF16)
        mixed_ref[layer * rows : (layer + 1) * rows, :] = mixed
        if layer:
            gradient = through_layer(layer, gradient, mixed, stream_ref, inverse_ref, down_ref, tap_ref)
    grads_ref[...] = gradient


def through_layer(layer, gradient, mixed, stream_ref, inverse_ref, down_ref, tap_ref):
    passed = dot(mixed, tap_ref[layer]).astype(BF16)
    normed = dot(passed, down_ref[layer])
    before = stream_ref[layer]
    inverse = inverse_ref[layer]
    shared = jnp.sum(normed * before, axis=-1, keepdims=True) * (1.0 / before.shape[-1])
    return gradient + inverse * normed - before * (inverse * inverse * inverse * shared)


def output_body(gradient_ref, mixed_ref, stream_ref, inverse_ref, down_ref, tap_ref, grad_ref):
    rows = gradient_ref.shape[0]
    mixed = mixed_ref[0:rows, :]
    gradient = through_layer(0, gradient_ref[...], mixed, stream_ref, inverse_ref, down_ref, tap_ref)
    grad_ref[0] = gradient.astype(BF16)


def entry_of(table, index):
    packed = sum(value << (3 * place) for place, value in enumerate(table))
    return lax.bitwise_and(lax.shift_right_logical(jnp.int32(packed), jnp.int32(3) * index), jnp.int32(7))


def held_block(parity, bit_x, bit_z, layer):
    core = lax.bitwise_xor(lax.bitwise_xor(parity, bit_x), lax.bitwise_xor(bit_z, layer))
    return pl.multiple_of(entry_of(OWNED, 4 * bit_z + 2 * bit_x + core) * BLOCK, BLOCK)


def select_body(reduced_ref, reduced_far_ref, left_ref, turned_ref):
    bits, parity = position_bits()
    bit = pick(parity, bits[0], bits[1])
    rows = reduced_ref.shape[0] // LAYERS
    for layer in range(LAYERS):
        part = slice(layer * rows, (layer + 1) * rows)
        turned_ref[layer, :, :rows] = reduced_ref[part, :].T
        turned_ref[layer, :, rows:] = reduced_far_ref[part, :].T
        for side in range(2):
            first = bit if side == 0 else 1 - bit
            for turn in range(2):
                block = held_block(parity, pick(parity, first, turn), pick(parity, turn, first), layer)
                to = (2 * side + turn) * BLOCK
                left_ref[layer, to : to + BLOCK, :] = turned_ref[layer, pl.ds(block, BLOCK), :]


def taps_body(left_ref, mixed_ref, mixed_far_ref, partial_ref, kept_ref, send_ref, partial_out):
    rows = left_ref.shape[-1] // 2
    kept_rows = kept_ref.shape[0]
    for layer in range(LAYERS):
        part = slice(layer * rows, (layer + 1) * rows)
        right = jnp.concatenate([mixed_ref[part, :], mixed_far_ref[part, :]], axis=0)
        blocks = dot(left_ref[layer], right)
        for turn in range(2):
            to = (2 * turn + layer) * BLOCK
            kept_ref[to : to + BLOCK, :] = blocks[turn * BLOCK : (turn + 1) * BLOCK]
            send_ref[to : to + BLOCK, :] = blocks[(2 + turn) * BLOCK : (3 + turn) * BLOCK].astype(BF16)
    high = mixed_far_ref[LAYERS * rows : LAYERS * rows + 16, :].astype(F32)
    low = mixed_far_ref[LAYERS * rows + 16 : LAYERS * rows + 32, :].astype(F32)
    partial = partial_ref[...] + (high + low)
    partial_out[...] = partial
    send_ref[kept_rows : kept_rows + 16, :] = partial.astype(BF16)


def position_bits():
    place = lax.axis_index("seq")
    bits = [lax.rem(place // value, 2) for value in (1, 2, 4)]
    return bits, lax.rem(lax.axis_index("dp") + bits[0] + bits[1] + bits[2], 2)


def pick(parity, even, odd):
    return even + parity * (odd - even)


def join_body(stage, kept_ref, got_ref, partial_ref, kept_out, send_out, partial_out):
    rows = kept_out.shape[0]
    bits, parity = position_bits()
    bit = pick(parity, bits[1], bits[0]) if stage == 1 else bits[2]
    keep = pl.ds(pl.multiple_of(bit * rows, rows), rows)
    send = pl.ds(pl.multiple_of((1 - bit) * rows, rows), rows)
    kept_out[...] = kept_ref[keep, :] + got_ref[keep, :].astype(F32)
    send_out[0:rows, :] = (kept_ref[send, :] + got_ref[send, :].astype(F32)).astype(BF16)
    partial = partial_ref[...] + got_ref[2 * rows : 2 * rows + 16, :].astype(F32)
    if stage == 1:
        partial_out[...] = partial
        send_out[rows : rows + 16, :] = partial.astype(BF16)
    else:
        last = bits[2]
        partial_out[...] = jnp.where(last == 0, partial[0:8], partial[8:16])
        send_out[rows : rows + 8, :] = jnp.where(last == 0, partial[8:16], partial[0:8]).astype(BF16)


def finish_body(scale, kept_ref, got_ref, block_out, send_out):
    rows = kept_ref.shape[0]
    block = (kept_ref[...] + got_ref[0:rows, :].astype(F32)) * scale
    block_out[...] = block
    send_out[...] = block.astype(BF16)


def place_body(own_ref, first_ref, second_ref, out_ref):
    number = lax.rem(2 * lax.axis_index("seq") + lax.axis_index("dp"), 8)
    held = (range(8),) + SOURCES
    for table, ref in zip(held, (own_ref, first_ref, second_ref)):
        spots = [(OWNED[table[j]] - 3 * j) % 8 for j in range(8)]
        out_ref[pl.ds(pl.multiple_of(entry_of(spots, number) * BLOCK, BLOCK), BLOCK), :] = ref[...].astype(F32)


def modes_body(scale, got_ref, partial_ref, mode_out):
    rows = got_ref.shape[0] - 8
    full = (partial_ref[...] + got_ref[rows : rows + 8, :].astype(F32)) * scale
    number = lax.rem(2 * lax.axis_index("seq") + lax.axis_index("dp"), 8)
    span = full.shape[1]
    mode_out[...] = pltpu.roll(full, lax.rem(span - BLOCK * number, span), 1)[:, 0:BLOCK]


def swap(value, axis, mask):
    count = lax.axis_size(axis)
    return lax.ppermute(value, axis, [(source, source ^ mask) for source in range(count)])


def hop_to(value, step):
    pairs = []
    for source in range(2 * lax.axis_size("seq")):
        flip, mask = step(source % 2, source // 2)
        pairs.append((source, source ^ (2 * mask + flip)))
    return lax.ppermute(value, ("seq", "dp"), pairs)


def class_of(core, place):
    return (core + place + place // 2 + place // 4) % 2


def wrapped_device(
    features, cotangent, counts, count_weight, down_weight, tap_weight, up_weight,
    decay_rate, keep_share, mode_weight,
):
    rows, width = features.shape[1:]
    down = jnp.swapaxes(down_weight, 1, 2)
    taps = jnp.swapaxes(tap_weight, 2, 3)
    down_far, up_far, taps_far = swap(down, "dp", 1), swap(up_weight, "dp", 1), swap(taps, "dp", 1)
    scale = jnp.sqrt(-jnp.expm1(-2.0 * decay_rate))
    (pay,) = call(
        prepare_body,
        tuple(pltpu.with_memory_space_constraint(value, HBM) for value in (cotangent, keep_share, decay_rate)),
        (HBM,) * 3,
        (((1, 8, width + 128), BF16),),
        (
            pltpu.VMEM(cotangent.shape, BF16),
            pltpu.VMEM(keep_share.shape, F32),
            pltpu.SMEM(decay_rate.shape, F32),
            pltpu.SemaphoreType.DMA((3,)),
        ),
        size=1300 * GIGA,
    )
    got = hop_to(pay, lambda core, place: (0, HOPS[0]))
    (tap_full,) = call(
        assemble_body, (taps, taps_far), (VMEM,) * 2, (((LAYERS, B, B), BF16),), size=1200 * GIGA
    )
    two = jnp.concatenate([pay, got], axis=0)
    two, down_far, tap_full = lax.optimization_barrier((two, down_far, tap_full))
    got_two = hop_to(two, lambda core, place: (0, HOPS[1 + core]))
    stream, inverse, reduced, slope = call(
        forward_body,
        (features, counts, count_weight[None], down, down_far, tap_full, up_weight, up_far),
        (VMEM,) * 8,
        (
            ((LAYERS + 1, rows, width), F32),
            ((LAYERS, rows, 1), F32),
            ((LAYERS * rows, B), BF16),
            ((LAYERS, rows, B), F32),
        ), size=1800 * GIGA
    )
    four = jnp.concatenate([two, got_two], axis=0)
    four, stream, reduced = lax.optimization_barrier((four, stream, reduced))
    got_four = hop_to(four, lambda core, place: (0, HOPS[2 - core]))
    reduced_far = swap(reduced, "dp", 1)
    down_full, local, mark, reach, edge, rate = call(
        local_body,
        (decay_rate, scale, cotangent, keep_share, mode_weight, stream, down, down_far),
        (SMEM, SMEM) + (VMEM,) * 6,
        (((LAYERS, B, width), BF16), ((rows, width), F32), ((8, width), F32), ((8, width), F32), ((32, rows), BF16), ((2, 8, 128), F32)), size=1600 * GIGA
    )
    local, reduced_far = lax.optimization_barrier((local, reduced_far))
    gradient, mixed, partial = call(
        backward_body,
        (
            pay, got, got_two, got_four, mode_weight, local, mark, reach, edge, rate,
            stream, inverse, slope, down_full, tap_full, up_weight, up_far,
        ),
        (VMEM,) * 17,
        (((rows, width), F32), ((LAYERS * rows + 32, B), BF16), ((16, B), F32)), size=2100 * GIGA
    )
    mixed_far = swap(mixed, "dp", 1)
    (grad,) = call(
        output_body,
        (gradient, mixed, stream, inverse, down_full, tap_full),
        (VMEM,) * 6,
        (((1, rows, width), BF16),), size=1300 * GIGA
    )
    kept_rows = RING * BLOCK // 2
    (left,) = call(
        select_body,
        (reduced, reduced_far),
        (VMEM,) * 2,
        (((LAYERS, kept_rows, 2 * rows), BF16),),
        (pltpu.VMEM((LAYERS, B, 2 * rows), BF16),),
        size=500 * GIGA,
    )
    kept, send, partial = call(
        taps_body,
        (left, mixed, mixed_far, partial),
        (VMEM,) * 4,
        (((kept_rows, B), F32), ((kept_rows + 16, B), BF16), ((16, B), F32)),
        size=300 * GIGA,
    )
    got = hop_to(send, lambda core, place: (1, 1 + class_of(core, place)))
    for stage in (1, 2):
        kept_rows = kept.shape[0] // 2
        mode_rows = (16, 8)[stage - 1]
        kept, send, partial = call(
            functools.partial(join_body, stage),
            (kept, got, partial),
            (VMEM,) * 3,
            (((kept_rows, B), F32), ((kept_rows + mode_rows, B), BF16), ((mode_rows, B), F32)),
        )
        if stage == 1:
            send, grad = lax.optimization_barrier((send, grad))
        if stage == 1:
            got = hop_to(send, lambda core, place: (1, 2 - class_of(core, place)))
        else:
            got = hop_to(send, lambda core, place: (1, 4))
    total = features.shape[0] * lax.axis_size("dp") * rows * lax.axis_size("seq")
    report = 1.0 / math.sqrt(total)
    block, narrow = call(
        functools.partial(finish_body, report),
        (kept, got),
        (VMEM,) * 2,
        (((BLOCK, B), F32), ((BLOCK, B), BF16)),
    )
    parts = []
    for table in SOURCES:
        pairs = [(8 * layer + table[j], 8 * layer + j) for layer in range(LAYERS) for j in range(8)]
        parts.append(lax.ppermute(narrow, ("seq", "dp"), pairs))
    (mode_sum,) = call(
        functools.partial(modes_body, report), (got, partial), (VMEM,) * 2, (((8, BLOCK), F32),)
    )
    (taps_sum,) = call(place_body, (block, *parts), (VMEM,) * 3, (((3 * BLOCK, B), F32),))
    return grad, taps_sum, mode_sum


def solution(mesh):
    placed = (
        P(("parts", "dp"), "seq", None),
        P(("parts", "dp"), "seq", None),
        P(("parts", "dp"), "seq"),
        P(),
        P(None, None, "dp"),
        P(None, None, None, "dp"),
        P(None, None, "dp"),
        P(),
        P(("parts", "dp"), "seq"),
        P(),
    )

    def per_device(*operands):
        rows = operands[0].shape[1]
        ring = lax.axis_size("seq")
        loop = ring * rows
        wraps = all(dilation % loop == 0 for dilation in (DILATION_FIRST1, DILATION_SECOND2))
        fits = ring == RING and lax.axis_size("dp") == 2 and operands[0].shape[0] == 1
        return (wrapped_device if wraps and fits else general_device)(*operands)

    return jax.shard_map(
        per_device,
        mesh=mesh,
        in_specs=placed,
        out_specs=(
            P(("parts", "dp"), "seq", None),
            P(("parts", "seq", "dp"), None),
            P("parts", ("seq", "dp")),
        ),
        check_vma=False,
    )
```
